32 devices in a mesh: kv: 2 (over x), seq: 16 (over z, y, core).
Axes of the slice: x: 2, y: 2, z: 4, core: 2. Of those that a mesh axis runs over, the one named last changes fastest.
Arguments:
- hidden: bfloat16 [1024, 2048], P('seq', 'kv'), may hold values from -1.5 to 1.5
- in_gain: float32 [2048], replicated, may hold values from 0.5 to 1.5
- w_query: bfloat16 [2048, 2048], P(None, 'kv'), may hold values from -0.125 to 0.125
- key_projection_weight: bfloat16 [2048, 1024], P(None, 'kv'), may hold values from -0.125 to 0.125
- value_projection_weight: bfloat16 [2048, 1024], P(None, 'kv'), may hold values from -0.125 to 0.125
- w_gate: bfloat16 [2048, 16], P(None, 'kv'), may hold values from -0.125 to 0.125
- w_out: bfloat16 [2048, 2048], P('kv'), may hold values from -0.125 to 0.125
- q_gain: float32 [128], replicated, may hold values from 0.1 to 1.9
- k_gain: float32 [128], replicated, may hold values from 0.1 to 1.9
- cache_keys: bfloat16 [32768, 8, 128], P('seq', 'kv'), may hold values from -160 to 160
- pooled_cache_values: bfloat16 [32768, 8, 128], P('seq', 'kv'), may hold values from -6 to 6
- prefix_len: int32 [4], replicated, may hold values from 1024 to 8192, as said below
- own_len: int32 [32], replicated, may hold values from 256 to 2048, as said below
- request_group: int32 [32], replicated, may hold values from 0 to 3, as said below
- parents: int32 [32, 32], P('seq'), may hold values from 0 to 30, as said below
- accepted_leaf: int32 [32], P('seq'), may hold values from 0 to 31
Outputs:
- layer_out: bfloat16 [1024, 2048], P('seq', 'kv')
- accepted_keys: bfloat16 [32, 32, 1024], P('seq', None, 'kv')
- accepted_values: bfloat16 [32, 32, 1024], P('seq', None, 'kv')
The draws below stay inside these ranges and needn't reach their ends.
Inputs may be any that keep to these rules, and one draw needn't show every extreme that they name: parents[r, 0] is 0 and node 0 is the root; for i >= 1, parents[r, i] < i. `prefix_len`: the lengths sum to 32768 // 2; one is exactly 8192 and one exactly 1024. `own_len`: the lengths sum to 32768 // 2; one is exactly 2048 and one exactly 256. `request_group`: every group holds exactly 8 requests.
All inputs are finite; a program needn't handle non-finite values.
Results may differ from the reference program's by a relative error of at most 0.017.
The reference program's roundings to bfloat16 on the way count: a program that leaves them out, or rounds other values in their place, can miss the bound.
Values may be sent and summed in bfloat16 or wider, within the bound.
A program may use at most 128 MiB of HBM per device.

```python
import math
import jax
import jax.numpy as jnp
from jax import lax

MODEL_WIDTH = 2048
HQ = 16
KEY_VALUE_HEADS = 8
HEAD_SIZE = 128
TREE = 32
R = 32
TOKENS = 1024
CACHE_SLOTS = 32768
GROUPS = 4
PRE_MOST = 8192
PRE_LEAST = 1024
OWN_MOST = 2048
OWN_LEAST = 256


def draw_parents(key, part):
    nodes = jnp.arange(TREE, dtype=jnp.int32)
    upper = jnp.maximum(nodes, 1)
    picked = jax.random.randint(key, (R, TREE), 0, upper[None, :])
    picked = jnp.where(nodes[None, :] > 0, picked, 0).astype(jnp.int32)
    chosen = jax.random.randint(jax.random.fold_in(key, 3), (), 0, R)
    rows = jnp.arange(R, dtype=jnp.int32)
    deepest = (rows[:, None] == chosen) & (nodes[None, :] == TREE - 1)
    return jnp.where(deepest, TREE - 2, picked).astype(jnp.int32)


def draw_cache_keys(key, part):
    base_offset = jnp.clip(jax.random.normal(key, (CACHE_SLOTS, KEY_VALUE_HEADS, HEAD_SIZE), jnp.float32), -4.0, 4.0)
    return (base_offset * 2.5).astype(jnp.bfloat16)


def fill_lengths(key, count, total, most, floor_limit):
    order = jax.random.permutation(jax.random.fold_in(key, 11), count).astype(jnp.int32)
    places = jnp.arange(count, dtype=jnp.int32)
    sorted_index = jnp.zeros((count,), jnp.int32).at[order].set(places)
    weights = jax.random.randint(jax.random.fold_in(key, 12), (count,), 500, 1000).astype(jnp.int32)
    unfilled_entries = sorted_index >= 2
    weights = jnp.where(unfilled_entries, weights, 0)
    extra = total - most - floor_limit * (count - 1)
    common_prefix_part = weights * extra // jnp.sum(weights)
    leftover_number = extra - jnp.sum(common_prefix_part)
    extra_symbol = (unfilled_entries & (sorted_index < 2 + leftover_number)).astype(jnp.int32)
    query_spans = floor_limit + common_prefix_part + extra_symbol
    return jnp.where(sorted_index == 0, most, query_spans).astype(jnp.int32)


def draw_prefix_len(key, part):
    return fill_lengths(key, GROUPS, CACHE_SLOTS // 2, PRE_MOST, PRE_LEAST)


def draw_own_len(key, part):
    return fill_lengths(key, R, CACHE_SLOTS // 2, OWN_MOST, OWN_LEAST)


def draw_request_group(key, part):
    order = jax.random.permutation(jax.random.fold_in(key, 21), R).astype(jnp.int32)
    return (order // 8).astype(jnp.int32)


def plant(array, key, smallest, largest):
    spot = [jax.random.randint(jax.random.fold_in(key, axis), (), 0, length) for axis, length in enumerate(array.shape)]
    longest = array.shape.index(max(array.shape))
    next_to = spot[:longest] + [(spot[longest] + 1) % array.shape[longest]] + spot[longest + 1:]
    return array.at[tuple(spot)].set(smallest).at[tuple(next_to)].set(largest)


def block_levels(stream_key, shape, shards, smallest, largest):
    def one(dim, parts):
        steps = jax.random.uniform(jax.random.fold_in(jax.random.fold_in(stream_key, 6), dim), (parts,), jnp.float32, smallest / len(shards), largest / len(shards))
        return jnp.repeat(jnp.exp(steps), shape[dim] // parts).reshape((-1,) + (1,) * (len(shape) - dim - 1))

    factor_of = one(*shards[0])
    for cut in shards[1:]:
        factor_of = factor_of * one(*cut)
    return factor_of


def scatter_about(key, shape, spread, most, split=(), held_as=jnp.bfloat16):
    array = spread * jax.random.normal(key, shape, jnp.float32)
    if split:
        array = array * block_levels(key, shape, split, -0.22, 0.18)
    return jnp.clip(array, -most, most).astype(held_as)


def setup_inputs(seed: int = 0) -> dict:
    keys = jax.random.split(jax.random.key(seed), 17)
    return {
        "hidden": scatter_about(keys[0], (TOKENS, MODEL_WIDTH), 0.25, 1.5, ((0, 16), (1, 2))),
        "in_gain": jnp.clip(1.0 + 0.1 * jax.random.normal(keys[1], (MODEL_WIDTH,), jnp.float32), 0.5, 1.5),
        "w_query": scatter_about(keys[2], (MODEL_WIDTH, HQ * HEAD_SIZE), MODEL_WIDTH ** -0.5, 0.125, ((1, 2),)),
        "key_projection_weight": scatter_about(keys[3], (MODEL_WIDTH, KEY_VALUE_HEADS * HEAD_SIZE), MODEL_WIDTH ** -0.5, 0.125, ((1, 2),)),
        "value_projection_weight": scatter_about(keys[4], (MODEL_WIDTH, KEY_VALUE_HEADS * HEAD_SIZE), MODEL_WIDTH ** -0.5, 0.125, ((1, 2),)),
        "w_gate": scatter_about(keys[5], (MODEL_WIDTH, HQ), MODEL_WIDTH ** -0.5, 0.125, ((1, 2),)),
        "w_out": scatter_about(keys[6], (HQ * HEAD_SIZE, MODEL_WIDTH), (HQ * HEAD_SIZE) ** -0.5, 0.125, ((0, 2),)),
        "q_gain": jnp.clip(1.0 + 0.18 * jax.random.normal(keys[7], (HEAD_SIZE,), jnp.float32), 0.1, 1.9),
        "k_gain": jnp.clip(1.0 + 0.18 * jax.random.normal(keys[8], (HEAD_SIZE,), jnp.float32), 0.1, 1.9),
        "cache_keys": draw_cache_keys(jax.random.fold_in(keys[16], 71), 0),
        "pooled_cache_values": scatter_about(keys[10], (CACHE_SLOTS, KEY_VALUE_HEADS, HEAD_SIZE), 1.0, 6.0, ((0, 16), (1, 2))),
        "prefix_len": draw_prefix_len(jax.random.fold_in(keys[16], 71), 0),
        "own_len": draw_own_len(jax.random.fold_in(keys[16], 71), 0),
        "request_group": draw_request_group(jax.random.fold_in(keys[16], 71), 0),
        "parents": draw_parents(jax.random.fold_in(keys[16], 71), 0),
        "accepted_leaf": plant(jax.random.randint(keys[15], (R,), 0, TREE), jax.random.fold_in(keys[15], 1), 0, TREE - 1).astype(jnp.int32),
    }


EPSILON = 1e-06
ROPE_BASE = 1000000.0
NEGATIVE = -1e+30

def rms_scale(values, scales):
    mean_square = lax.optimization_barrier(jnp.mean(values * values, axis=-1, keepdims=True))
    return values * lax.rsqrt(mean_square + EPSILON) * scales

def rotate_pairs(values, positions):
    half_width = values.shape[-1] // 2
    freqs = jnp.exp(jnp.arange(half_width, dtype=jnp.float32) * (-2.0 * math.log(ROPE_BASE) / values.shape[-1]))
    angles = positions[:, None] * freqs[None, :]
    cosine = jnp.concatenate([jnp.cos(angles), jnp.cos(angles)], axis=-1)[:, None, :]
    sine = jnp.concatenate([jnp.sin(angles), jnp.sin(angles)], axis=-1)[:, None, :]
    turned = jnp.concatenate([-values[..., half_width:], values[..., :half_width]], axis=-1)
    return values * cosine + turned * sine

def tree_paths(parents):
    width = parents.shape[-1]
    nodes = jnp.arange(width, dtype=jnp.int32)
    linked = (parents[:, :, None] == nodes[None, None, :]).astype(jnp.float32)
    identity_mat = jnp.eye(width, dtype=jnp.float32)
    reach = jnp.minimum(identity_mat[None] + linked * (1.0 - identity_mat[None]), 1.0)
    for squaring in range(max(1, (width - 1).bit_length())):
        reach = jnp.minimum(jnp.einsum('mij,mjk->mik', reach, reach, precision=lax.Precision.HIGHEST), 1.0)
    depth_f = lax.optimization_barrier(jnp.sum(reach, axis=-1)) - 1.0
    return (reach, depth_f)

def accepted_rows(reach, depth_f, leaves, tree_rows):
    width = reach.shape[-1]
    nodes = jnp.arange(width, dtype=jnp.int32)
    leaf_pick = (leaves[:, None] == nodes[None, :]).astype(jnp.float32)
    on_path = jnp.einsum('mi,mij->mj', leaf_pick, reach, precision=lax.Precision.HIGHEST)
    levels = (depth_f[:, None, :] == nodes.astype(jnp.float32)[None, :, None]).astype(jnp.float32)
    select = levels * on_path[:, None, :]
    return jnp.einsum('mdj,mjc->mdc', select, tree_rows.astype(jnp.float32), precision=lax.Precision.HIGHEST).astype(jnp.bfloat16)

def reference(hidden, in_gain, w_query, key_projection_weight, value_projection_weight, w_gate, w_out, q_gain, k_gain, cache_keys, pooled_cache_values, prefix_len, own_len, request_group, parents, accepted_leaf):
    requests = own_len.shape[0]
    tree = parents.shape[1]
    heads = w_gate.shape[1]
    head_width = q_gain.shape[0]
    kv_heads = key_projection_weight.shape[1] // head_width
    per_kv = heads // kv_heads
    groups = prefix_len.shape[0]
    score_scale = 1.0 / math.sqrt(head_width)
    normed = rms_scale(hidden.astype(jnp.float32), in_gain).astype(jnp.bfloat16)
    reach, depth_f = tree_paths(parents)
    context = prefix_len[request_group] + own_len
    positions = (context[:, None].astype(jnp.float32) + depth_f).reshape(-1)
    query = jnp.dot(normed, w_query, preferred_element_type=jnp.float32).reshape(-1, heads, head_width)
    query = rotate_pairs(rms_scale(query, q_gain), positions).astype(jnp.bfloat16)
    key_new = jnp.dot(normed, key_projection_weight, preferred_element_type=jnp.float32).reshape(-1, kv_heads, head_width)
    key_new = rotate_pairs(rms_scale(key_new, k_gain), positions).astype(jnp.bfloat16)
    value_new = jnp.dot(normed, value_projection_weight, preferred_element_type=jnp.float32).astype(jnp.bfloat16).reshape(-1, kv_heads, head_width)
    gate_logit = jnp.dot(normed, w_gate, preferred_element_type=jnp.float32)
    lengths_all = jnp.concatenate([prefix_len, own_len]).astype(jnp.int32)
    starts = (jnp.cumsum(lengths_all) - lengths_all).astype(jnp.int32)
    span = max(PRE_MOST, OWN_MOST)
    padding = jnp.zeros((span, kv_heads, head_width), cache_keys.dtype)
    keys_pool = jnp.concatenate([cache_keys, padding], axis=0)
    values_pool = jnp.concatenate([pooled_cache_values, padding], axis=0)
    pre_start = starts[request_group].astype(jnp.int32)
    pre_count = prefix_len[request_group].astype(jnp.int32)
    own_start = starts[groups:].astype(jnp.int32)

    def one_request(inputs):
        q_rows, k_rows, v_rows, reach_rows, first_pre, count_pre, first_own, count_own = inputs
        zero_index = jnp.zeros((), jnp.int32)
        k_pre = lax.dynamic_slice(keys_pool, (first_pre, zero_index, zero_index), (PRE_MOST, kv_heads, head_width))
        v_pre = lax.dynamic_slice(values_pool, (first_pre, zero_index, zero_index), (PRE_MOST, kv_heads, head_width))
        k_own = lax.dynamic_slice(keys_pool, (first_own, zero_index, zero_index), (OWN_MOST, kv_heads, head_width))
        v_own = lax.dynamic_slice(values_pool, (first_own, zero_index, zero_index), (OWN_MOST, kv_heads, head_width))
        keys_all = jnp.concatenate([k_pre, k_own, k_rows], axis=0).astype(jnp.float32)
        values_all = jnp.concatenate([v_pre, v_own, v_rows], axis=0).astype(jnp.float32)
        pre_mask = jnp.arange(PRE_MOST, dtype=jnp.int32) < count_pre
        own_mask = jnp.arange(OWN_MOST, dtype=jnp.int32) < count_own
        visible = jnp.concatenate([jnp.broadcast_to(pre_mask[None, :], (tree, PRE_MOST)), jnp.broadcast_to(own_mask[None, :], (tree, OWN_MOST)), reach_rows > 0.5], axis=1)
        q_grouped = q_rows.reshape(tree, kv_heads, per_kv, head_width).astype(jnp.float32)
        scores = jnp.einsum('tkgd,lkd->kgtl', q_grouped, keys_all) * score_scale
        scores = jnp.where(visible[None, None], scores, NEGATIVE)
        row_max = lax.optimization_barrier(jnp.max(scores, axis=-1, keepdims=True))
        weights = jnp.where(visible[None, None], jnp.exp(scores - row_max), 0.0)
        weight_sum = lax.optimization_barrier(jnp.sum(weights, axis=-1))
        rounded = weights.astype(jnp.bfloat16).astype(jnp.float32)
        summed = jnp.einsum('kgtl,lkd->tkgd', rounded, values_all)
        return summed / jnp.transpose(weight_sum, (2, 0, 1))[..., None]
    mixed = lax.map(one_request, (query.reshape(requests, tree, heads, head_width), key_new.reshape(requests, tree, kv_heads, head_width), value_new.reshape(requests, tree, kv_heads, head_width), reach, pre_start, pre_count, own_start, own_len.astype(jnp.int32)))
    mixed = mixed.reshape(-1, heads, head_width) * jax.nn.sigmoid(gate_logit)[:, :, None]
    attended = mixed.astype(jnp.bfloat16).reshape(-1, heads * head_width)
    layer_out = (jnp.dot(attended, w_out, preferred_element_type=jnp.float32) + hidden.astype(jnp.float32)).astype(jnp.bfloat16)
    tree_rows = jnp.concatenate([key_new.reshape(requests, tree, kv_heads * head_width), value_new.reshape(requests, tree, kv_heads * head_width)], axis=-1)
    picked = accepted_rows(reach, depth_f, accepted_leaf, tree_rows)
    accepted_keys = picked[:, :, :kv_heads * head_width]
    accepted_values = picked[:, :, kv_heads * head_width:]
    return (layer_out, accepted_keys, accepted_values)
```

```python
import functools
import math

import jax
import jax.numpy as jnp
import numpy as np
from jax import lax
from jax.experimental import pallas as pl
from jax.experimental.pallas import tpu as pltpu
from jax.sharding import PartitionSpec as P

EPSILON = 1e-06
ROPE_BASE = 1000000.0
NEGATIVE = -1e30
FRONT_VMEM = 47 * 2**20


def rms_scale(values, scales):
    mean_square = jnp.mean(values * values, axis=-1, keepdims=True)
    return values * lax.rsqrt(mean_square + EPSILON) * scales


def rope_angles(positions, freqs):
    angles = positions * freqs
    turns = jnp.floor(angles * (2.0 / math.pi) + 0.5)
    rest = angles - turns * 1.5703125
    rest = rest - turns * 4.837512969970703125e-4
    rest = rest - turns * 7.549789954891882e-8
    square = rest * rest
    sine = rest + rest * square * (
        -1.6666654611e-1 + square * (8.3321608736e-3 - square * 1.9515295891e-4)
    )
    cosine = (
        1.0
        - 0.5 * square
        + square * square * (4.166664568298827e-2 + square * (-1.388731625493765e-3 + square * 2.443315711809948e-5))
    )
    quarter = turns.astype(jnp.int32) & 3
    swapped = (quarter & 1) == 1
    cos_out = jnp.where(swapped, sine, cosine)
    sin_out = jnp.where(swapped, cosine, sine)
    cos_out = jnp.where((quarter == 1) | (quarter == 2), -cos_out, cos_out)
    sin_out = jnp.where(quarter >= 2, -sin_out, sin_out)
    return cos_out, sin_out


def tree_tables(parents, leaves, contexts, freqs):
    local_req, width = parents.shape
    tokens = local_req * width
    rows = lax.broadcasted_iota(jnp.int32, (tokens, tokens), 0)
    cols = lax.broadcasted_iota(jnp.int32, (tokens, tokens), 1)
    above = jnp.concatenate(
        [parents[at : at + 1, :] + at * width for at in range(local_req)], axis=1
    )
    reached = jnp.where((above == rows) | (rows == cols), 1.0, 0.0)
    for squaring in range(max(1, (width - 1).bit_length())):
        half = reached.astype(jnp.bfloat16)
        reached = jnp.minimum(jnp.dot(half, half, preferred_element_type=jnp.float32), 1.0)
    reach = jnp.transpose(reached)
    depth_across = jnp.sum(reached, axis=0, keepdims=True) - 1.0
    depth_down = jnp.sum(reach, axis=1, keepdims=True) - 1.0
    which = lax.broadcasted_iota(jnp.int32, (tokens, 1), 0) // width
    context = jnp.zeros((tokens, 1), jnp.float32)
    is_leaf = rows < 0
    for at in range(local_req):
        context = jnp.where(which == at, contexts[at], context)
        is_leaf = is_leaf | (rows == leaves[:, at : at + 1] + at * width)
    on_path = jnp.sum(jnp.where(is_leaf, reach, 0.0), axis=0, keepdims=True)
    level = (rows % width).astype(jnp.float32)
    picked = (depth_across == level) & (rows // width == cols // width)
    select = jnp.where(picked, jnp.broadcast_to(on_path, (tokens, tokens)), 0.0)
    cosine, sine = rope_angles(context + depth_down, freqs)
    lanes = lax.broadcasted_iota(jnp.int32, cosine.shape, 1)
    sine = jnp.where(lanes < cosine.shape[1] // 2, -sine, sine)
    return reach, select, cosine, sine


def lowest(distance):
    return distance & -distance


def flip(index, distance):
    out = index
    bit = 1
    while bit <= distance:
        if distance & bit:
            out = out + bit * (1 - 2 * ((index // bit) % 2))
        bit *= 2
    return out


def one_bits(count):
    bits = []
    bit = 1
    while bit < count:
        bits.append(bit)
        bit *= 2
    return bits


def greet(me, count, kv, kv_count):
    barrier = pltpu.get_barrier_semaphore()
    bits = one_bits(count)
    for bit in bits:
        pl.semaphore_signal(barrier, inc=1, device_id={"seq": flip(me, bit)})
    for hop in range(1, kv_count):
        pl.semaphore_signal(barrier, inc=1, device_id={"kv": (kv + hop) % kv_count})
    pl.semaphore_wait(barrier, len(bits) + kv_count - 1)


def layer_kernel(
    count,
    kv_count,
    tree,
    score_scale,
    hidden_ref,
    small_ref,
    w_query_ref,
    w_key_ref,
    w_value_ref,
    w_gate_ref,
    cache_key_ref,
    cache_value_ref,
    all_ref,
    key_ref,
    value_ref,
    tree_ref,
    tree_lse_ref,
    gate_ref,
    select_ref,
    keys_ref,
    turned_ref,
    wide,
    w_query,
    w_key,
    w_value,
    w_gate,
    raw_keys,
    raw_values,
    stage,
    cos_ref,
    sin_ref,
    seen_ref,
    load_sem,
    wide_send,
    wide_recv,
    send_sem,
    recv_sem,
):
    me = lax.axis_index("seq")
    kv = lax.axis_index("kv")
    loads = [
        pltpu.make_async_copy(source, target, load_sem.at[which])
        for which, (source, target) in enumerate(
            [
                (hidden_ref, wide.at[kv]),
                (w_query_ref, w_query),
                (w_key_ref, w_key),
                (w_value_ref, w_value),
                (w_gate_ref, w_gate),
                (cache_key_ref, raw_keys),
                (cache_value_ref, raw_values),
            ]
        )
    ]
    for load in loads:
        load.start()
    loads[0].wait()
    greet(me, count, kv, kv_count)

    def wide_message(hop, owner):
        return pltpu.make_async_remote_copy(
            src_ref=wide.at[owner],
            dst_ref=wide.at[owner],
            send_sem=wide_send.at[hop],
            recv_sem=wide_recv.at[hop],
            device_id={"kv": (kv + hop) % kv_count},
        )

    wide_sent = [wide_message(hop, kv) for hop in range(1, kv_count)]
    for copy in wide_sent:
        copy.start()
    lane = lax.broadcasted_iota(jnp.int32, (1, 128), 1)
    tables = wide.shape[0] * wide.shape[2] // 128

    def row(at):
        return small_ref[tables + at : tables + at + 1, :]

    def taken(values, index):
        return jnp.sum(jnp.where(lane == index, values, 0.0), axis=1, keepdims=True)

    local_req = hidden_ref.shape[0] // tree
    contexts = [
        taken(row(3), taken(row(5), me * local_req + at).astype(jnp.int32))
        + taken(row(4), me * local_req + at)
        for at in range(local_req)
    ]
    parents = jnp.concatenate([row(7 + at)[:, :tree] for at in range(local_req)], axis=0).astype(jnp.int32)
    reach, select, cosine, sine = tree_tables(parents, row(6).astype(jnp.int32), contexts, row(2))
    seen_ref[...] = reach
    select_ref[...] = select.astype(jnp.bfloat16)
    cos_ref[...] = cosine
    sin_ref[...] = sine
    for hop in range(1, kv_count):
        wide_message(hop, (kv + kv_count - hop) % kv_count).wait_recv()
    rows = jnp.concatenate([wide[at] for at in range(kv_count)], axis=1).astype(jnp.float32)
    mean_square = jnp.mean(rows * rows, axis=-1, keepdims=True)
    inverse = lax.rsqrt(mean_square + EPSILON)
    normed = jnp.concatenate(
        [
            (rows[:, at * 128 : (at + 1) * 128] * inverse * small_ref[at : at + 1, :]).astype(jnp.bfloat16)
            for at in range(rows.shape[1] // 128)
        ],
        axis=1,
    )

    def rotated(values, gain):
        values = rms_scale(values, gain)
        return (values * cos_ref[...] + pltpu.roll(values, 64, 1) * sin_ref[...]).astype(jnp.bfloat16)

    loads[1].wait()
    query = jnp.dot(normed, w_query[...], preferred_element_type=jnp.float32)
    heads = query.shape[1] // 128
    queries = [rotated(query[:, h * 128 : (h + 1) * 128], row(0)) for h in range(heads)]
    for head in range(heads):
        all_ref[me, :, head * 128 : (head + 1) * 128] = queries[head]

    def message(distance, owner):
        return pltpu.make_async_remote_copy(
            src_ref=all_ref.at[owner],
            dst_ref=all_ref.at[owner],
            send_sem=send_sem.at[distance],
            recv_sem=recv_sem.at[distance],
            device_id={"seq": flip(me, lowest(distance))},
        )

    sent = []

    def hand_on(distance):
        owner = flip(me, distance)
        if distance:
            message(distance, owner).wait_recv()
        for bit in reversed(one_bits(lowest(distance) if distance else count)):
            copy = message(distance | bit, owner)
            copy.start()
            sent.append(copy)

    hand_on(0)
    local_kv = key_ref.shape[1] // 128
    per_kv = heads // local_kv
    tokens = hidden_ref.shape[0]

    def keys_work():
        loads[2].wait()
        key = jnp.dot(normed, w_key[...], preferred_element_type=jnp.float32)
        for at in range(local_kv):
            cols = slice(at * 128, (at + 1) * 128)
            key_ref[:, cols] = rotated(key[:, cols], row(1))

    def values_work():
        loads[3].wait()
        loads[4].wait()
        value_ref[...] = jnp.dot(
            normed, w_value[...], preferred_element_type=jnp.float32
        ).astype(jnp.bfloat16)
        gate_ref[...] = jax.nn.sigmoid(
            lax.dot_general(
                normed, w_gate[...], (((1,), (1,)), ((), ())), preferred_element_type=jnp.float32
            )
        )
        tree_lse_ref[...] = jnp.zeros(tree_lse_ref.shape, jnp.float32)

    def tree_work(at):
        cols = slice(at * 128, (at + 1) * 128)
        stacked = jnp.concatenate(queries[at * per_kv : (at + 1) * per_kv], axis=0)
        scores = (
            lax.dot_general(
                stacked,
                key_ref[:, cols],
                (((1,), (1,)), ((), ())),
                preferred_element_type=jnp.float32,
            )
            * score_scale
        )
        seen = jnp.concatenate([seen_ref[...]] * per_kv, axis=0) > 0.5
        scores = jnp.where(seen, scores, NEGATIVE)
        top = jnp.max(scores, axis=1, keepdims=True)
        weights = jnp.where(seen, jnp.exp(scores - top), 0.0)
        total = jnp.sum(weights, axis=1, keepdims=True)
        mixed = (
            jnp.dot(
                weights.astype(jnp.bfloat16), value_ref[:, cols], preferred_element_type=jnp.float32
            )
            / total
        )
        lse = top + jnp.log(total)
        for sub in range(per_kv):
            head = at * per_kv + sub
            part = slice(sub * tokens, (sub + 1) * tokens)
            tree_ref[:, head * 128 : (head + 1) * 128] = mixed[part]
            column = sub * local_kv + at
            tree_lse_ref[:, column : column + 1] = lse[part]

    pieces = 8
    slots = keys_ref.shape[0] // pieces

    def apart(source, which):
        stage[...] = source[which * slots * local_kv : (which + 1) * slots * local_kv, :].astype(jnp.float32)
        return [stage[pl.ds(at, slots, stride=local_kv), :] for at in range(local_kv)]

    def keys_apart(which):
        if which == 0:
            loads[5].wait()
        for at, part in enumerate(apart(raw_keys, which)):
            keys_ref[which * slots : (which + 1) * slots, at * 128 : (at + 1) * 128] = part.astype(jnp.bfloat16)

    def values_apart(which):
        if which == 0:
            loads[6].wait()
        for at, part in enumerate(apart(raw_values, which)):
            turned_ref[at * 128 : (at + 1) * 128, which * slots : (which + 1) * slots] = jnp.transpose(
                part
            ).astype(jnp.bfloat16)

    work = [keys_work, values_work] + [functools.partial(tree_work, at) for at in range(local_kv)]
    work += [functools.partial(keys_apart, which) for which in range(pieces)]
    work += [functools.partial(values_apart, which) for which in range(pieces)]
    order = sorted(range(2, count, 2), key=lambda d: (-lowest(d), d))
    for distance in order:
        for once in range(3):
            if work:
                work.pop(0)()
        hand_on(distance)
    for rest in work:
        rest()
    for distance in range(1, count, 2):
        hand_on(distance)
    for copy in wide_sent + sent:
        copy.wait_send()


def layer_front(
    hidden,
    small,
    w_query,
    w_key,
    w_value,
    w_gate,
    cache_keys,
    cache_values,
    count,
    kv_count,
    tree,
    score_scale,
):
    tokens = hidden.shape[0]
    width = w_query.shape[1]
    local_kv = w_key.shape[1] // 128
    slots = cache_keys.shape[0] // local_kv
    vmem = pl.BlockSpec(memory_space=pltpu.VMEM)
    hbm = pl.BlockSpec(memory_space=pltpu.HBM)
    return pl.pallas_call(
        functools.partial(layer_kernel, count, kv_count, tree, score_scale),
        out_shape=(
            jax.ShapeDtypeStruct((count, tokens, width), jnp.bfloat16),
            jax.ShapeDtypeStruct((tokens, w_key.shape[1]), jnp.bfloat16),
            jax.ShapeDtypeStruct((tokens, w_value.shape[1]), jnp.bfloat16),
            jax.ShapeDtypeStruct((tokens, width), jnp.float32),
            jax.ShapeDtypeStruct((tokens, 128), jnp.float32),
            jax.ShapeDtypeStruct((tokens, w_gate.shape[0]), jnp.float32),
            jax.ShapeDtypeStruct((tokens, tokens), jnp.bfloat16),
            jax.ShapeDtypeStruct((slots, local_kv * 128), jnp.bfloat16),
            jax.ShapeDtypeStruct((local_kv * 128, slots), jnp.bfloat16),
        ),
        in_specs=[hbm, vmem] + [hbm] * 6,
        out_specs=(vmem,) * 9,
        scratch_shapes=[
            pltpu.VMEM((kv_count,) + hidden.shape, hidden.dtype),
            pltpu.VMEM(w_query.shape, w_query.dtype),
            pltpu.VMEM(w_key.shape, w_key.dtype),
            pltpu.VMEM(w_value.shape, w_value.dtype),
            pltpu.VMEM(w_gate.shape, w_gate.dtype),
            pltpu.VMEM(cache_keys.shape, jnp.bfloat16),
            pltpu.VMEM(cache_values.shape, jnp.bfloat16),
            pltpu.VMEM((cache_keys.shape[0] // 8, 128), jnp.float32),
            pltpu.VMEM((tokens, 128), jnp.float32),
            pltpu.VMEM((tokens, 128), jnp.float32),
            pltpu.VMEM((tokens, tokens), jnp.float32),
            pltpu.SemaphoreType.DMA((7,)),
            pltpu.SemaphoreType.DMA((kv_count,)),
            pltpu.SemaphoreType.DMA((kv_count,)),
            pltpu.SemaphoreType.DMA((count,)),
            pltpu.SemaphoreType.DMA((count,)),
        ],
        compiler_params=pltpu.CompilerParams(
            collective_id=0, has_side_effects=True, vmem_limit_bytes=FRONT_VMEM
        ),
        name="layer_front",
    )(
        hidden,
        small,
        w_query,
        w_key,
        w_value,
        w_gate,
        cache_keys,
        cache_values,
    )


def merge_kernel(
    count,
    kv_count,
    per_kv,
    part_ref,
    lse_ref,
    tree_ref,
    tree_lse_ref,
    gate_ref,
    w_out_ref,
    hidden_ref,
    out_ref,
    got,
    got_lse,
    held,
    held_lse,
    w_out,
    attended,
    outgoing,
    arrived,
    send_sem,
    recv_sem,
    load_sem,
    out_send,
    out_recv,
):
    me = lax.axis_index("seq")
    kv = lax.axis_index("kv")
    heads = part_ref.shape[2] // 128
    load = pltpu.make_async_copy(w_out_ref, w_out, load_sem)
    load.start()
    rows = part_ref.shape[1]

    def across(level):
        turned = jnp.transpose(level)[:8]
        return jnp.concatenate([turned] * (128 // rows), axis=1)

    greet(me, count, kv, kv_count)

    def messages(distance):
        owner = flip(me, distance)
        if distance % 2:
            sources = (part_ref.at[owner], lse_ref.at[owner])
        else:
            sources = (held.at[distance // 2], held_lse.at[distance // 2])
        return [
            pltpu.make_async_remote_copy(
                src_ref=source,
                dst_ref=target.at[distance],
                send_sem=send_sem.at[which, distance],
                recv_sem=recv_sem.at[which, distance],
                device_id={"seq": flip(me, lowest(distance))},
            )
            for which, (source, target) in enumerate(zip(sources, (got, got_lse)))
        ]

    sent = []

    def send(distance):
        for copy in messages(distance):
            copy.start()
            sent.append(copy)

    for distance in sorted(range(1, count, 2), reverse=True):
        send(distance)
    evens = sorted(range(2, count, 2), key=lambda d: (lowest(d), -d))
    for distance in evens + [0]:
        owner = flip(me, distance)
        incoming = [distance | bit for bit in one_bits(lowest(distance) if distance else count)]
        for message in incoming:
            for copy in messages(message):
                copy.wait_recv()
        levels = [lse_ref[owner]] + [got_lse[message] for message in incoming]
        if not distance:
            levels.append(across(tree_lse_ref[...]))
        top = functools.reduce(jnp.maximum, levels)
        shares = [jnp.exp(level - top) for level in levels]
        total = functools.reduce(jnp.add, shares)
        inverse = 1.0 / total
        shares = [jnp.transpose(share * inverse)[:rows] for share in shares]
        if distance:
            held_lse[distance // 2] = top + jnp.log(total)
        for head in range(heads):
            cols = slice(head * 128, (head + 1) * 128)
            place = head % per_kv * (heads // per_kv) + head // per_kv
            pieces = [part_ref[owner, :, cols]] + [got[message, :, cols] for message in incoming]
            if not distance:
                pieces.append(tree_ref[:, cols])
            mixed = functools.reduce(
                jnp.add,
                [
                    piece.astype(jnp.float32) * share[:, place : place + 1]
                    for piece, share in zip(pieces, shares)
                ],
            )
            if distance:
                held[distance // 2, :, cols] = mixed.astype(held.dtype)
            else:
                attended[:, cols] = (mixed * gate_ref[:, head : head + 1]).astype(jnp.bfloat16)
        if distance:
            send(distance)
    load.wait()
    width = out_ref.shape[1]

    def projected(target):
        cols = pl.ds(pl.multiple_of(target * width, 128), width)
        return jnp.dot(attended[...], w_out[:, cols], preferred_element_type=jnp.float32)

    def out_message(hop):
        return pltpu.make_async_remote_copy(
            src_ref=outgoing.at[hop],
            dst_ref=arrived.at[hop],
            send_sem=out_send.at[hop],
            recv_sem=out_recv.at[hop],
            device_id={"kv": (kv + hop) % kv_count},
        )

    for hop in range(1, kv_count):
        outgoing[hop] = projected((kv + hop) % kv_count).astype(jnp.bfloat16)
        copy = out_message(hop)
        copy.start()
        sent.append(copy)
    total = projected(kv)
    for hop in range(1, kv_count):
        out_message(hop).wait_recv()
        total = total + arrived[hop].astype(jnp.float32)
    out_ref[...] = (total + hidden_ref[...].astype(jnp.float32)).astype(jnp.bfloat16)
    for copy in sent:
        copy.wait_send()


def merge_parts(parts, lse, tree_mix, tree_lse, gate, w_out, hidden, count, kv_count, per_kv):
    rows, width = parts.shape[1:]
    lanes = lse.shape[2]
    half = max(1, count // 2)
    vmem = pl.BlockSpec(memory_space=pltpu.VMEM)
    return pl.pallas_call(
        functools.partial(merge_kernel, count, kv_count, per_kv),
        out_shape=jax.ShapeDtypeStruct(hidden.shape, jnp.bfloat16),
        in_specs=[vmem] * 5 + [pl.BlockSpec(memory_space=pltpu.HBM), vmem],
        out_specs=vmem,
        scratch_shapes=[
            pltpu.VMEM((count, rows, width), parts.dtype),
            pltpu.VMEM((count, 8, lanes), jnp.float32),
            pltpu.VMEM((half, rows, width), parts.dtype),
            pltpu.VMEM((half, 8, lanes), jnp.float32),
            pltpu.VMEM(w_out.shape, w_out.dtype),
            pltpu.VMEM((rows, width), jnp.bfloat16),
            pltpu.VMEM((kv_count,) + hidden.shape, jnp.bfloat16),
            pltpu.VMEM((kv_count,) + hidden.shape, jnp.bfloat16),
            pltpu.SemaphoreType.DMA((2, count)),
            pltpu.SemaphoreType.DMA((2, count)),
            pltpu.SemaphoreType.DMA,
            pltpu.SemaphoreType.DMA((kv_count,)),
            pltpu.SemaphoreType.DMA((kv_count,)),
        ],
        compiler_params=pltpu.CompilerParams(
            collective_id=1, has_side_effects=True, vmem_limit_bytes=48 * 2**20
        ),
        name="merge_parts",
    )(parts, lse, tree_mix, tree_lse, gate, w_out, hidden)


def pool_kernel(
    local_req,
    per_kv,
    block,
    own_block,
    score_scale,
    prefix_ref,
    own_ref,
    group_ref,
    q_ref,
    k_ref,
    vt_ref,
    select_ref,
    key_new_ref,
    value_new_ref,
    o_ref,
    lse_ref,
    accepted_keys_ref,
    accepted_values_ref,
    member_ref,
    picked_keys,
    picked_values,
    shared_q,
    shared_top,
    shared_sum,
    shared_mix,
    own_q,
    own_top,
    own_sum,
    own_mix,
    picked_sem,
):
    requests, tree, width = q_ref.shape
    groups = prefix_ref.shape[0]
    pool, kv_width = k_ref.shape
    local_kv = kv_width // 128
    heads = local_kv * per_kv
    per_group = requests // groups
    rows = per_kv * per_group * tree
    base_two = score_scale / math.log(2.0)
    base = lax.axis_index("seq") * pool
    picked = select_ref[...]
    picked_keys[...] = jnp.dot(picked, key_new_ref[...], preferred_element_type=jnp.float32).astype(jnp.bfloat16)
    picked_values[...] = jnp.dot(picked, value_new_ref[...], preferred_element_type=jnp.float32).astype(
        jnp.bfloat16
    )
    copies = [
        pltpu.make_async_copy(picked_keys, accepted_keys_ref, picked_sem.at[0]),
        pltpu.make_async_copy(picked_values, accepted_values_ref, picked_sem.at[1]),
    ]
    for copy in copies:
        copy.start()
    o_ref[...] = jnp.zeros_like(o_ref)
    lse_ref[...] = jnp.full(lse_ref.shape, NEGATIVE, jnp.float32)

    def put_lse(owner, levels):
        wide = jnp.concatenate([levels] * (128 // tree), axis=1)
        if heads < 8:
            wide = jnp.concatenate([wide] * (8 // heads), axis=0)
        lanes = lax.broadcasted_iota(jnp.int32, wide.shape, 1) // tree % local_req
        device = owner // local_req
        lse_ref[device] = jnp.where(lanes == owner % local_req, wide, lse_ref[device])

    def bounds(start, length):
        return jnp.clip(start - base, 0, pool), jnp.clip(start + length - base, 0, pool)

    def shown_bias(start, size, lanes, first, last):
        slots = start + lax.broadcasted_iota(jnp.int32, (size, 128), 0)
        bias = jnp.where((slots >= first) & (slots < last), 0.0, NEGATIVE)
        return jnp.concatenate([bias] * (lanes // 128), axis=1)

    def shared_part(group, first, last):
        def find(request, found):
            member_ref[found] = request
            return found + (group_ref[request] == group).astype(jnp.int32)

        lax.fori_loop(0, requests, find, 0)
        members = [member_ref[at] for at in range(per_group)]
        for kv in range(local_kv):
            for sub in range(per_kv):
                head = kv * per_kv + sub
                for at, owner in enumerate(members):
                    place = sub * per_group + at
                    shared_q[kv, place * tree : (place + 1) * tree, :] = q_ref[
                        owner, :, head * 128 : (head + 1) * 128
                    ]
        shared_top[...] = jnp.full(shared_top.shape, NEGATIVE, jnp.float32)
        shared_sum[...] = jnp.zeros_like(shared_sum)
        shared_mix[...] = jnp.zeros_like(shared_mix)

        def visit(step, unused):
            start = pl.multiple_of(step * block, block)
            bias = shown_bias(start, block, rows, first, last)
            for kv in range(local_kv):
                cols = slice(kv * 128, (kv + 1) * 128)
                scores = (
                    lax.dot_general(
                        k_ref[pl.ds(start, block), cols],
                        shared_q[kv],
                        (((1,), (1,)), ((), ())),
                        preferred_element_type=jnp.float32,
                    )
                    + bias
                )
                old_top = shared_top[kv : kv + 1, :]
                top = jnp.maximum(old_top, jnp.max(scores, axis=0, keepdims=True))
                weights = jnp.exp2((scores - top) * base_two)
                factor = jnp.exp2((old_top - top) * base_two)
                shared_top[kv : kv + 1, :] = top
                shared_sum[kv : kv + 1, :] = shared_sum[kv : kv + 1, :] * factor + jnp.sum(
                    weights, axis=0, keepdims=True
                )
                shared_mix[kv] = shared_mix[kv] * factor + jnp.dot(
                    vt_ref[cols, pl.ds(start, block)],
                    weights.astype(jnp.bfloat16),
                    preferred_element_type=jnp.float32,
                )
            return unused

        lax.fori_loop(first // block, (last + block - 1) // block, visit, 0)
        levels = shared_top[...] * score_scale + jnp.log(shared_sum[...])
        for kv in range(local_kv):
            mixed = jnp.transpose(shared_mix[kv] / shared_sum[kv : kv + 1, :]).astype(o_ref.dtype)
            for sub in range(per_kv):
                head = kv * per_kv + sub
                for at, owner in enumerate(members):
                    place = sub * per_group + at
                    o_ref[owner, :, head * 128 : (head + 1) * 128] = mixed[place * tree : (place + 1) * tree]
        for at, owner in enumerate(members):
            put_lse(
                owner,
                jnp.concatenate(
                    [
                        levels[:, (sub * per_group + at) * tree : (sub * per_group + at + 1) * tree]
                        for sub in range(per_kv)
                    ],
                    axis=0,
                ),
            )

    def own_part(owner, first, last):
        lanes = heads * tree
        span = per_kv * tree
        for head in range(heads):
            cols = slice(head // per_kv * 128, (head // per_kv + 1) * 128)
            own_q[head * tree : (head + 1) * tree, cols] = q_ref[owner, :, head * 128 : (head + 1) * 128]
        own_top[...] = jnp.full(own_top.shape, NEGATIVE, jnp.float32)
        own_sum[...] = jnp.zeros_like(own_sum)
        own_mix[...] = jnp.zeros_like(own_mix)

        def visit(step, unused):
            start = pl.multiple_of(step * own_block, own_block)
            scores = lax.dot_general(
                k_ref[pl.ds(start, own_block), :],
                own_q[...],
                (((1,), (1,)), ((), ())),
                preferred_element_type=jnp.float32,
            ) + shown_bias(start, own_block, lanes, first, last)
            old_top = own_top[...]
            top = jnp.maximum(old_top, jnp.max(scores, axis=0, keepdims=True))
            weights = jnp.exp2((scores - top) * base_two)
            factor = jnp.exp2((old_top - top) * base_two)
            own_top[...] = top
            own_sum[...] = own_sum[...] * factor + jnp.sum(weights, axis=0, keepdims=True)
            whole = jnp.dot(
                vt_ref[:, pl.ds(start, own_block)],
                weights.astype(jnp.bfloat16),
                preferred_element_type=jnp.float32,
            )
            which = lax.broadcasted_iota(jnp.int32, (128, lanes), 1) // span
            mixed = whole[:128]
            for kv in range(1, local_kv):
                mixed = jnp.where(which == kv, whole[kv * 128 : (kv + 1) * 128], mixed)
            own_mix[...] = own_mix[...] * factor + mixed
            return unused

        lax.fori_loop(first // own_block, (last + own_block - 1) // own_block, visit, 0)
        levels = own_top[...] * score_scale + jnp.log(own_sum[...])
        mixed = jnp.transpose(own_mix[...] / own_sum[...]).astype(o_ref.dtype)
        for head in range(heads):
            o_ref[owner, :, head * 128 : (head + 1) * 128] = mixed[head * tree : (head + 1) * tree]
        put_lse(
            owner,
            jnp.concatenate(
                [
                    levels[:, (kv * per_kv + sub) * tree : (kv * per_kv + sub + 1) * tree]
                    for sub in range(per_kv)
                    for kv in range(local_kv)
                ],
                axis=0,
            ),
        )

    def group_step(group, start):
        first, last = bounds(start, prefix_ref[group])

        @pl.when(last > first)
        def _():
            shared_part(group, first, last)

        return start + prefix_ref[group]

    def own_step(owner, start):
        first, last = bounds(start, own_ref[owner])

        @pl.when(last > first)
        def _():
            own_part(owner, first, last)

        return start + own_ref[owner]

    own_start = lax.fori_loop(0, groups, group_step, 0)

    @pl.when(base + pool > own_start)
    def _():
        own_q[...] = jnp.zeros_like(own_q)
        lax.fori_loop(0, requests, own_step, own_start)

    for copy in copies:
        copy.wait()


def pool_attention(
    prefix_len, own_len, request_group, query, keys, turned, select, key_new, value_new, local_req, per_kv, score_scale
):
    requests, tree, width = query.shape
    pool, kv_width = keys.shape
    local_kv = kv_width // 128
    heads = local_kv * per_kv
    rows = per_kv * (requests // prefix_len.shape[0]) * tree
    lanes = heads * tree
    vmem = pl.BlockSpec(memory_space=pltpu.VMEM)
    smem = pl.BlockSpec(memory_space=pltpu.SMEM)
    hbm = pl.BlockSpec(memory_space=pltpu.HBM)
    return pl.pallas_call(
        functools.partial(pool_kernel, local_req, per_kv, min(512, pool), min(256, pool), score_scale),
        out_shape=(
            jax.ShapeDtypeStruct(query.shape, jnp.bfloat16),
            jax.ShapeDtypeStruct((requests // local_req, 8, 128), jnp.float32),
            jax.ShapeDtypeStruct(key_new.shape, jnp.bfloat16),
            jax.ShapeDtypeStruct(value_new.shape, jnp.bfloat16),
        ),
        in_specs=[smem] * 3 + [vmem] * 6,
        out_specs=(vmem, vmem, hbm, hbm),
        scratch_shapes=[
            pltpu.SMEM((requests + 1,), jnp.int32),
            pltpu.VMEM(key_new.shape, jnp.bfloat16),
            pltpu.VMEM(value_new.shape, jnp.bfloat16),
            pltpu.VMEM((local_kv, rows, 128), jnp.bfloat16),
            pltpu.VMEM((local_kv, rows), jnp.float32),
            pltpu.VMEM((local_kv, rows), jnp.float32),
            pltpu.VMEM((local_kv, 128, rows), jnp.float32),
            pltpu.VMEM((lanes, kv_width), jnp.bfloat16),
            pltpu.VMEM((1, lanes), jnp.float32),
            pltpu.VMEM((1, lanes), jnp.float32),
            pltpu.VMEM((128, lanes), jnp.float32),
            pltpu.SemaphoreType.DMA((2,)),
        ],
        compiler_params=pltpu.CompilerParams(vmem_limit_bytes=40 * 2**20),
        name="pool_attention",
    )(prefix_len, own_len, request_group, query, keys, turned, select, key_new, value_new)


def body(
    hidden,
    in_gain,
    w_query,
    key_projection_weight,
    value_projection_weight,
    w_gate,
    w_out,
    q_gain,
    k_gain,
    cache_keys,
    pooled_cache_values,
    prefix_len,
    own_len,
    request_group,
    parents,
    accepted_leaf,
):
    local_req, tree = parents.shape
    requests = own_len.shape[0]
    head_width = q_gain.shape[0]
    local_heads = w_gate.shape[1]
    local_kv = key_projection_weight.shape[1] // head_width
    per_kv = local_heads // local_kv
    local_tok = hidden.shape[0]
    pool_dev = cache_keys.shape[0]
    score_scale = 1.0 / math.sqrt(head_width)
    seq_count = requests // local_req
    kv_count = in_gain.shape[0] // hidden.shape[1]
    half = np.exp(np.arange(head_width // 2) * (-2.0 * math.log(ROPE_BASE) / head_width))
    freqs = np.concatenate([half, half]).astype(np.float32)

    lines = [in_gain.reshape(-1, head_width), q_gain[None], k_gain[None], jnp.asarray(freqs)[None]]
    lines += [prefix_len[None], own_len[None], request_group[None], accepted_leaf[None], parents]
    depth = sum(values.shape[0] for values in lines)
    depth += -depth % 8
    sums = {}
    top = 0
    for values in lines:
        rows, lanes = values.shape
        edges = ((top, depth - top - rows, 0), (0, head_width - lanes, 0))
        padded = lax.pad(values, jnp.zeros((), values.dtype), edges)
        sums[values.dtype] = sums[values.dtype] + padded if values.dtype in sums else padded
        top += rows
    small = functools.reduce(jnp.add, [total.astype(jnp.float32) for total in sums.values()])
    gathered, key_new, value_new, tree_mix, tree_lse, gate, select, keys, turned = layer_front(
        hidden,
        small,
        w_query,
        key_projection_weight,
        value_projection_weight,
        w_gate.T,
        cache_keys.reshape(pool_dev * local_kv, head_width),
        pooled_cache_values.reshape(pool_dev * local_kv, head_width),
        seq_count,
        kv_count,
        tree,
        score_scale,
    )
    parts, part_lse, accepted_keys, accepted_values = pool_attention(
        prefix_len,
        own_len,
        request_group,
        gathered.reshape(requests, tree, local_heads * head_width),
        keys,
        turned,
        select,
        key_new,
        value_new,
        local_req,
        per_kv,
        score_scale,
    )
    layer_out = merge_parts(
        parts.reshape(seq_count, local_tok, local_heads * head_width),
        part_lse,
        tree_mix,
        tree_lse,
        gate,
        w_out,
        hidden,
        seq_count,
        kv_count,
        per_kv,
    )
    return (
        layer_out,
        accepted_keys.reshape(local_req, tree, local_kv * head_width),
        accepted_values.reshape(local_req, tree, local_kv * head_width),
    )


def solution(mesh):
    in_specs = (
        P("seq", "kv"),
        P(),
        P(None, "kv"),
        P(None, "kv"),
        P(None, "kv"),
        P(None, "kv"),
        P("kv", None),
        P(),
        P(),
        P("seq", "kv", None),
        P("seq", "kv", None),
        P(),
        P(),
        P(),
        P("seq", None),
        P("seq"),
    )
    out_specs = (P("seq", "kv"), P("seq", None, "kv"), P("seq", None, "kv"))
    return jax.shard_map(body, mesh=mesh, in_specs=in_specs, out_specs=out_specs, check_vma=False)
```

```python
import functools
import math

import jax
import jax.numpy as jnp
import numpy as np
from jax import lax
from jax.experimental import pallas as pl
from jax.experimental.pallas import tpu as pltpu
from jax.sharding import PartitionSpec as P

EPSILON = 1e-06
ROPE_BASE = 1000000.0
NEGATIVE = -1e30
FRONT_VMEM = 47 * 2**20


def rms_scale(values, scales):
    mean_square = jnp.mean(values * values, axis=-1, keepdims=True)
    return values * lax.rsqrt(mean_square + EPSILON) * scales


def rope_angles(positions, freqs):
    angles = positions * freqs
    turns = jnp.floor(angles * (2.0 / math.pi) + 0.5)
    rest = angles - turns * 1.5703125
    rest = rest - turns * 4.837512969970703125e-4
    rest = rest - turns * 7.549789954891882e-8
    square = rest * rest
    sine = rest + rest * square * (
        -1.6666654611e-1 + square * (8.3321608736e-3 - square * 1.9515295891e-4)
    )
    cosine = (
        1.0
        - 0.5 * square
        + square * square * (4.166664568298827e-2 + square * (-1.388731625493765e-3 + square * 2.443315711809948e-5))
    )
    quarter = turns.astype(jnp.int32) & 3
    swapped = (quarter & 1) == 1
    cos_out = jnp.where(swapped, sine, cosine)
    sin_out = jnp.where(swapped, cosine, sine)
    cos_out = jnp.where((quarter == 1) | (quarter == 2), -cos_out, cos_out)
    sin_out = jnp.where(quarter >= 2, -sin_out, sin_out)
    return cos_out, sin_out


def tree_tables(parents, leaves, contexts, freqs):
    local_req, width = parents.shape
    tokens = local_req * width
    rows = lax.broadcasted_iota(jnp.int32, (tokens, tokens), 0)
    cols = lax.broadcasted_iota(jnp.int32, (tokens, tokens), 1)
    above = jnp.concatenate(
        [parents[at : at + 1, :] + at * width for at in range(local_req)], axis=1
    )
    reached = jnp.where((above == rows) | (rows == cols), 1.0, 0.0)
    for squaring in range(max(1, (width - 1).bit_length())):
        half = reached.astype(jnp.bfloat16)
        reached = jnp.minimum(jnp.dot(half, half, preferred_element_type=jnp.float32), 1.0)
    reach = jnp.transpose(reached)
    depth_across = jnp.sum(reached, axis=0, keepdims=True) - 1.0
    depth_down = jnp.sum(reach, axis=1, keepdims=True) - 1.0
    which = lax.broadcasted_iota(jnp.int32, (tokens, 1), 0) // width
    context = jnp.zeros((tokens, 1), jnp.float32)
    is_leaf = rows < 0
    for at in range(local_req):
        context = jnp.where(which == at, contexts[at], context)
        is_leaf = is_leaf | (rows == leaves[:, at : at + 1] + at * width)
    on_path = jnp.sum(jnp.where(is_leaf, reach, 0.0), axis=0, keepdims=True)
    level = (rows % width).astype(jnp.float32)
    picked = (depth_across == level) & (rows // width == cols // width)
    select = jnp.where(picked, jnp.broadcast_to(on_path, (tokens, tokens)), 0.0)
    cosine, sine = rope_angles(context + depth_down, freqs)
    lanes = lax.broadcasted_iota(jnp.int32, cosine.shape, 1)
    sine = jnp.where(lanes < cosine.shape[1] // 2, -sine, sine)
    return reach, select, cosine, sine


def lowest(distance):
    return distance & -distance


def flip(index, distance):
    out = index
    bit = 1
    while bit <= distance:
        if distance & bit:
            out = out + bit * (1 - 2 * ((index // bit) % 2))
        bit *= 2
    return out


def one_bits(count):
    bits = []
    bit = 1
    while bit < count:
        bits.append(bit)
        bit *= 2
    return bits


def greet(me, count, kv, kv_count):
    barrier = pltpu.get_barrier_semaphore()
    bits = one_bits(count)
    for bit in bits:
        pl.semaphore_signal(barrier, inc=1, device_id={"seq": flip(me, bit)})
    for hop in range(1, kv_count):
        pl.semaphore_signal(barrier, inc=1, device_id={"kv": (kv + hop) % kv_count})
    pl.semaphore_wait(barrier, len(bits) + kv_count - 1)


def layer_kernel(
    count,
    kv_count,
    tree,
    score_scale,
    hidden_ref,
    small_ref,
    w_query_ref,
    w_key_ref,
    w_value_ref,
    w_gate_ref,
    cache_key_ref,
    cache_value_ref,
    all_ref,
    key_ref,
    value_ref,
    tree_ref,
    tree_lse_ref,
    gate_ref,
    select_ref,
    keys_ref,
    turned_ref,
    wide,
    w_query,
    w_key,
    w_value,
    w_gate,
    raw_keys,
    raw_values,
    stage,
    cos_ref,
    sin_ref,
    seen_ref,
    load_sem,
    wide_send,
    wide_recv,
    send_sem,
    recv_sem,
):
    me = lax.axis_index("seq")
    kv = lax.axis_index("kv")
    loads = [
        pltpu.make_async_copy(source, target, load_sem.at[which])
        for which, (source, target) in enumerate(
            [
                (hidden_ref, wide.at[kv]),
                (w_query_ref, w_query),
                (w_key_ref, w_key),
                (w_value_ref, w_value),
                (w_gate_ref, w_gate),
                (cache_key_ref, raw_keys),
                (cache_value_ref, raw_values),
            ]
        )
    ]
    for load in loads:
        load.start()
    loads[0].wait()
    greet(me, count, kv, kv_count)

    def wide_message(hop, owner):
        return pltpu.make_async_remote_copy(
            src_ref=wide.at[owner],
            dst_ref=wide.at[owner],
            send_sem=wide_send.at[hop],
            recv_sem=wide_recv.at[hop],
            device_id={"kv": (kv + hop) % kv_count},
        )

    wide_sent = [wide_message(hop, kv) for hop in range(1, kv_count)]
    for copy in wide_sent:
        copy.start()
    lane = lax.broadcasted_iota(jnp.int32, (1, 128), 1)
    tables = wide.shape[0] * wide.shape[2] // 128

    def row(at):
        return small_ref[tables + at : tables + at + 1, :]

    def taken(values, index):
        return jnp.sum(jnp.where(lane == index, values, 0.0), axis=1, keepdims=True)

    local_req = hidden_ref.shape[0] // tree
    contexts = [
        taken(row(3), taken(row(5), me * local_req + at).astype(jnp.int32))
        + taken(row(4), me * local_req + at)
        for at in range(local_req)
    ]
    parents = jnp.concatenate([row(7 + at)[:, :tree] for at in range(local_req)], axis=0).astype(jnp.int32)
    reach, select, cosine, sine = tree_tables(parents, row(6).astype(jnp.int32), contexts, row(2))
    seen_ref[...] = reach
    select_ref[...] = select.astype(jnp.bfloat16)
    cos_ref[...] = cosine
    sin_ref[...] = sine
    for hop in range(1, kv_count):
        wide_message(hop, (kv + kv_count - hop) % kv_count).wait_recv()
    rows = jnp.concatenate([wide[at] for at in range(kv_count)], axis=1).astype(jnp.float32)
    mean_square = jnp.mean(rows * rows, axis=-1, keepdims=True)
    inverse = lax.rsqrt(mean_square + EPSILON)
    normed = jnp.concatenate(
        [
            (rows[:, at * 128 : (at + 1) * 128] * inverse * small_ref[at : at + 1, :]).astype(jnp.bfloat16)
            for at in range(rows.shape[1] // 128)
        ],
        axis=1,
    )

    def rotated(values, gain):
        values = rms_scale(values, gain)
        return (values * cos_ref[...] + pltpu.roll(values, 64, 1) * sin_ref[...]).astype(jnp.bfloat16)

    loads[1].wait()
    query = jnp.dot(normed, w_query[...], preferred_element_type=jnp.float32)
    heads = query.shape[1] // 128
    queries = [rotated(query[:, h * 128 : (h + 1) * 128], row(0)) for h in range(heads)]
    for head in range(heads):
        for at in range(local_req):
            all_ref[me * local_req + at, :, head * 128 : (head + 1) * 128] = queries[head][
                at * tree : (at + 1) * tree
            ]

    def message(distance, place, at):
        return pltpu.make_async_remote_copy(
            src_ref=all_ref.at[place],
            dst_ref=all_ref.at[place],
            send_sem=send_sem.at[distance, at],
            recv_sem=recv_sem.at[distance, at],
            device_id={"seq": flip(me, lowest(distance))},
        )

    sent = []

    def hand_on(distance, at):
        owner = flip(me, distance) * local_req + at
        if distance:
            message(distance, owner, at).wait_recv()
        for bit in reversed(one_bits(lowest(distance) if distance else count)):
            copy = message(distance | bit, owner, at)
            copy.start()
            sent.append(copy)

    for at in range(local_req):
        hand_on(0, at)
    local_kv = key_ref.shape[1] // 128
    per_kv = heads // local_kv
    tokens = hidden_ref.shape[0]

    def keys_work():
        loads[2].wait()
        key = jnp.dot(normed, w_key[...], preferred_element_type=jnp.float32)
        for at in range(local_kv):
            cols = slice(at * 128, (at + 1) * 128)
            key_ref[:, cols] = rotated(key[:, cols], row(1))

    def values_work():
        loads[3].wait()
        loads[4].wait()
        value_ref[...] = jnp.dot(
            normed, w_value[...], preferred_element_type=jnp.float32
        ).astype(jnp.bfloat16)
        gate_ref[...] = jax.nn.sigmoid(
            lax.dot_general(
                normed, w_gate[...], (((1,), (1,)), ((), ())), preferred_element_type=jnp.float32
            )
        )
        tree_lse_ref[...] = jnp.zeros(tree_lse_ref.shape, jnp.float32)

    def tree_work(at):
        cols = slice(at * 128, (at + 1) * 128)
        stacked = jnp.concatenate(queries[at * per_kv : (at + 1) * per_kv], axis=0)
        scores = (
            lax.dot_general(
                stacked,
                key_ref[:, cols],
                (((1,), (1,)), ((), ())),
                preferred_element_type=jnp.float32,
            )
            * score_scale
        )
        seen = jnp.concatenate([seen_ref[...]] * per_kv, axis=0) > 0.5
        scores = jnp.where(seen, scores, NEGATIVE)
        top = jnp.max(scores, axis=1, keepdims=True)
        weights = jnp.where(seen, jnp.exp(scores - top), 0.0)
        total = jnp.sum(weights, axis=1, keepdims=True)
        mixed = (
            jnp.dot(
                weights.astype(jnp.bfloat16), value_ref[:, cols], preferred_element_type=jnp.float32
            )
            / total
        )
        lse = top + jnp.log(total)
        for sub in range(per_kv):
            head = at * per_kv + sub
            part = slice(sub * tokens, (sub + 1) * tokens)
            tree_ref[:, head * 128 : (head + 1) * 128] = mixed[part]
            column = sub * local_kv + at
            tree_lse_ref[:, column : column + 1] = lse[part]

    pieces = 8
    slots = keys_ref.shape[0] // pieces

    def apart(source, which):
        stage[...] = source[which * slots * local_kv : (which + 1) * slots * local_kv, :].astype(jnp.float32)
        return [stage[pl.ds(at, slots, stride=local_kv), :] for at in range(local_kv)]

    def keys_apart(which):
        if which == 0:
            loads[5].wait()
        for at, part in enumerate(apart(raw_keys, which)):
            keys_ref[which * slots : (which + 1) * slots, at * 128 : (at + 1) * 128] = part.astype(jnp.bfloat16)

    def values_apart(which):
        if which == 0:
            loads[6].wait()
        for at, part in enumerate(apart(raw_values, which)):
            turned_ref[at * 128 : (at + 1) * 128, which * slots : (which + 1) * slots] = jnp.transpose(
                part
            ).astype(jnp.bfloat16)

    work = [keys_work, values_work] + [functools.partial(tree_work, at) for at in range(local_kv)]
    work += [functools.partial(keys_apart, which) for which in range(pieces)]
    work += [functools.partial(values_apart, which) for which in range(pieces)]
    order = sorted(range(2, count, 2), key=lambda d: (-lowest(d), d))
    for distance in order:
        for at in range(local_req):
            for once in range(2):
                if work:
                    work.pop(0)()
            hand_on(distance, at)
    for rest in work:
        rest()
    for distance in range(1, count, 2):
        for at in range(local_req):
            hand_on(distance, at)
    for copy in wide_sent + sent:
        copy.wait_send()


def layer_front(
    hidden,
    small,
    w_query,
    w_key,
    w_value,
    w_gate,
    cache_keys,
    cache_values,
    count,
    kv_count,
    tree,
    score_scale,
):
    tokens = hidden.shape[0]
    width = w_query.shape[1]
    local_kv = w_key.shape[1] // 128
    slots = cache_keys.shape[0] // local_kv
    vmem = pl.BlockSpec(memory_space=pltpu.VMEM)
    hbm = pl.BlockSpec(memory_space=pltpu.HBM)
    return pl.pallas_call(
        functools.partial(layer_kernel, count, kv_count, tree, score_scale),
        out_shape=(
            jax.ShapeDtypeStruct((count * tokens // tree, tree, width), jnp.bfloat16),
            jax.ShapeDtypeStruct((tokens, w_key.shape[1]), jnp.bfloat16),
            jax.ShapeDtypeStruct((tokens, w_value.shape[1]), jnp.bfloat16),
            jax.ShapeDtypeStruct((tokens, width), jnp.float32),
            jax.ShapeDtypeStruct((tokens, 128), jnp.float32),
            jax.ShapeDtypeStruct((tokens, w_gate.shape[0]), jnp.float32),
            jax.ShapeDtypeStruct((tokens, tokens), jnp.bfloat16),
            jax.ShapeDtypeStruct((slots, local_kv * 128), jnp.bfloat16),
            jax.ShapeDtypeStruct((local_kv * 128, slots), jnp.bfloat16),
        ),
        in_specs=[hbm, vmem] + [hbm] * 6,
        out_specs=(vmem,) * 9,
        scratch_shapes=[
            pltpu.VMEM((kv_count,) + hidden.shape, hidden.dtype),
            pltpu.VMEM(w_query.shape, w_query.dtype),
            pltpu.VMEM(w_key.shape, w_key.dtype),
            pltpu.VMEM(w_value.shape, w_value.dtype),
            pltpu.VMEM(w_gate.shape, w_gate.dtype),
            pltpu.VMEM(cache_keys.shape, jnp.bfloat16),
            pltpu.VMEM(cache_values.shape, jnp.bfloat16),
            pltpu.VMEM((cache_keys.shape[0] // 8, 128), jnp.float32),
            pltpu.VMEM((tokens, 128), jnp.float32),
            pltpu.VMEM((tokens, 128), jnp.float32),
            pltpu.VMEM((tokens, tokens), jnp.float32),
            pltpu.SemaphoreType.DMA((7,)),
            pltpu.SemaphoreType.DMA((kv_count,)),
            pltpu.SemaphoreType.DMA((kv_count,)),
            pltpu.SemaphoreType.DMA((count, tokens // tree)),
            pltpu.SemaphoreType.DMA((count, tokens // tree)),
        ],
        compiler_params=pltpu.CompilerParams(
            collective_id=0, has_side_effects=True, vmem_limit_bytes=FRONT_VMEM
        ),
        name="layer_front",
    )(
        hidden,
        small,
        w_query,
        w_key,
        w_value,
        w_gate,
        cache_keys,
        cache_values,
    )


def merge_kernel(
    count,
    kv_count,
    per_kv,
    part_ref,
    lse_ref,
    tree_ref,
    tree_lse_ref,
    gate_ref,
    w_out_ref,
    hidden_ref,
    out_ref,
    got,
    got_lse,
    held,
    held_lse,
    w_out,
    attended,
    outgoing,
    arrived,
    send_sem,
    recv_sem,
    load_sem,
    out_send,
    out_recv,
):
    me = lax.axis_index("seq")
    kv = lax.axis_index("kv")
    requests, rows, _ = part_ref.shape
    local_req = requests // count
    heads = part_ref.shape[2] // 128
    load = pltpu.make_async_copy(w_out_ref, w_out, load_sem)
    load.start()
    greet(me, count, kv, kv_count)

    def messages(distance, at):
        owner = flip(me, distance) * local_req + at
        if distance % 2:
            sources = (part_ref.at[owner], lse_ref.at[owner])
        else:
            sources = (held.at[distance // 2, at], held_lse.at[distance // 2, at])
        return [
            pltpu.make_async_remote_copy(
                src_ref=source,
                dst_ref=target.at[distance, at],
                send_sem=send_sem.at[which, distance, at],
                recv_sem=recv_sem.at[which, distance, at],
                device_id={"seq": flip(me, lowest(distance))},
            )
            for which, (source, target) in enumerate(zip(sources, (got, got_lse)))
        ]

    sent = []

    def send(distance, at):
        for copy in messages(distance, at):
            copy.start()
            sent.append(copy)

    def combined(distance, at):
        owner = flip(me, distance) * local_req + at
        incoming = [distance | bit for bit in one_bits(lowest(distance) if distance else count)]
        for message in incoming:
            for copy in messages(message, at):
                copy.wait_recv()
        levels = [lse_ref[owner]] + [got_lse[message, at] for message in incoming]
        own = slice(at * rows, (at + 1) * rows)
        if not distance:
            turned = jnp.transpose(tree_lse_ref[own, :])[:8]
            levels.append(jnp.concatenate([turned] * (128 // rows), axis=1))
        top = functools.reduce(jnp.maximum, levels)
        shares = [jnp.exp(level - top) for level in levels]
        total = functools.reduce(jnp.add, shares)
        inverse = 1.0 / total
        shares = [jnp.transpose(share * inverse)[:rows] for share in shares]
        if distance:
            held_lse[distance // 2, at] = top + jnp.log(total)
        for head in range(heads):
            cols = slice(head * 128, (head + 1) * 128)
            place = head % per_kv * (heads // per_kv) + head // per_kv
            pieces = [part_ref[owner, :, cols]] + [got[message, at, :, cols] for message in incoming]
            if not distance:
                pieces.append(tree_ref[own, cols])
            mixed = functools.reduce(
                jnp.add,
                [
                    piece.astype(jnp.float32) * share[:, place : place + 1]
                    for piece, share in zip(pieces, shares)
                ],
            )
            if distance:
                held[distance // 2, at, :, cols] = mixed.astype(held.dtype)
            else:
                attended[own, cols] = (mixed * gate_ref[own, head : head + 1]).astype(jnp.bfloat16)

    for distance in sorted(range(1, count, 2), reverse=True):
        for at in range(local_req):
            send(distance, at)
    for distance in sorted(range(2, count, 2), key=lambda d: (lowest(d), -d)):
        for at in range(local_req):
            combined(distance, at)
            send(distance, at)
    width = out_ref.shape[1]

    def projected(target, at):
        cols = pl.ds(pl.multiple_of(target * width, 128), width)
        return jnp.dot(
            attended[at * rows : (at + 1) * rows, :], w_out[:, cols], preferred_element_type=jnp.float32
        )

    def out_message(hop, at):
        return pltpu.make_async_remote_copy(
            src_ref=outgoing.at[hop, at],
            dst_ref=arrived.at[hop, at],
            send_sem=out_send.at[hop, at],
            recv_sem=out_recv.at[hop, at],
            device_id={"kv": (kv + hop) % kv_count},
        )

    totals = []
    for at in range(local_req):
        combined(0, at)
        if not at:
            load.wait()
        for hop in range(1, kv_count):
            outgoing[hop, at] = projected((kv + hop) % kv_count, at).astype(jnp.bfloat16)
            copy = out_message(hop, at)
            copy.start()
            sent.append(copy)
        totals.append(projected(kv, at))
    for at in range(local_req):
        total = totals[at]
        own = slice(at * rows, (at + 1) * rows)
        for hop in range(1, kv_count):
            out_message(hop, at).wait_recv()
            total = total + arrived[hop, at].astype(jnp.float32)
        out_ref[own, :] = (total + hidden_ref[own, :].astype(jnp.float32)).astype(jnp.bfloat16)
    for copy in sent:
        copy.wait_send()


def merge_parts(parts, lse, tree_mix, tree_lse, gate, w_out, hidden, count, kv_count, per_kv):
    requests, rows, width = parts.shape
    local_req = requests // count
    half = max(1, count // 2)
    vmem = pl.BlockSpec(memory_space=pltpu.VMEM)
    crossing = (kv_count, local_req, rows, hidden.shape[1])
    return pl.pallas_call(
        functools.partial(merge_kernel, count, kv_count, per_kv),
        out_shape=jax.ShapeDtypeStruct(hidden.shape, jnp.bfloat16),
        in_specs=[vmem] * 5 + [pl.BlockSpec(memory_space=pltpu.HBM), vmem],
        out_specs=vmem,
        scratch_shapes=[
            pltpu.VMEM((count, local_req, rows, width), parts.dtype),
            pltpu.VMEM((count, local_req) + lse.shape[1:], jnp.float32),
            pltpu.VMEM((half, local_req, rows, width), parts.dtype),
            pltpu.VMEM((half, local_req) + lse.shape[1:], jnp.float32),
            pltpu.VMEM(w_out.shape, w_out.dtype),
            pltpu.VMEM((local_req * rows, width), jnp.bfloat16),
            pltpu.VMEM(crossing, jnp.bfloat16),
            pltpu.VMEM(crossing, jnp.bfloat16),
            pltpu.SemaphoreType.DMA((2, count, local_req)),
            pltpu.SemaphoreType.DMA((2, count, local_req)),
            pltpu.SemaphoreType.DMA,
            pltpu.SemaphoreType.DMA((kv_count, local_req)),
            pltpu.SemaphoreType.DMA((kv_count, local_req)),
        ],
        compiler_params=pltpu.CompilerParams(
            collective_id=1, has_side_effects=True, vmem_limit_bytes=48 * 2**20
        ),
        name="merge_parts",
    )(parts, lse, tree_mix, tree_lse, gate, w_out, hidden)


def pool_kernel(
    per_kv,
    block,
    own_block,
    score_scale,
    prefix_ref,
    own_ref,
    group_ref,
    q_ref,
    k_ref,
    vt_ref,
    select_ref,
    key_new_ref,
    value_new_ref,
    o_ref,
    lse_ref,
    accepted_keys_ref,
    accepted_values_ref,
    member_ref,
    picked_keys,
    picked_values,
    shared_q,
    shared_top,
    shared_sum,
    shared_mix,
    own_q,
    own_top,
    own_sum,
    own_mix,
    picked_sem,
):
    requests, tree, width = q_ref.shape
    groups = prefix_ref.shape[0]
    pool, kv_width = k_ref.shape
    local_kv = kv_width // 128
    heads = local_kv * per_kv
    per_group = requests // groups
    rows = per_kv * per_group * tree
    base_two = score_scale / math.log(2.0)
    base = lax.axis_index("seq") * pool
    picked = select_ref[...]
    picked_keys[...] = jnp.dot(picked, key_new_ref[...], preferred_element_type=jnp.float32).astype(jnp.bfloat16)
    picked_values[...] = jnp.dot(picked, value_new_ref[...], preferred_element_type=jnp.float32).astype(
        jnp.bfloat16
    )
    copies = [
        pltpu.make_async_copy(picked_keys, accepted_keys_ref, picked_sem.at[0]),
        pltpu.make_async_copy(picked_values, accepted_values_ref, picked_sem.at[1]),
    ]
    for copy in copies:
        copy.start()
    o_ref[...] = jnp.zeros_like(o_ref)
    lse_ref[...] = jnp.full(lse_ref.shape, NEGATIVE, jnp.float32)

    def put_lse(owner, levels):
        wide = jnp.concatenate([levels] * (128 // tree), axis=1)
        if heads < 8:
            wide = jnp.concatenate([wide] * (8 // heads), axis=0)
        lse_ref[owner] = wide

    def bounds(start, length):
        return jnp.clip(start - base, 0, pool), jnp.clip(start + length - base, 0, pool)

    def shown_bias(start, size, lanes, first, last):
        slots = start + lax.broadcasted_iota(jnp.int32, (size, 128), 0)
        bias = jnp.where((slots >= first) & (slots < last), 0.0, NEGATIVE)
        return jnp.concatenate([bias] * (lanes // 128), axis=1)

    def shared_part(group, first, last):
        def find(request, found):
            member_ref[found] = request
            return found + (group_ref[request] == group).astype(jnp.int32)

        lax.fori_loop(0, requests, find, 0)
        members = [member_ref[at] for at in range(per_group)]
        for kv in range(local_kv):
            for sub in range(per_kv):
                head = kv * per_kv + sub
                for at, owner in enumerate(members):
                    place = sub * per_group + at
                    shared_q[kv, place * tree : (place + 1) * tree, :] = q_ref[
                        owner, :, head * 128 : (head + 1) * 128
                    ]
        shared_top[...] = jnp.full(shared_top.shape, NEGATIVE, jnp.float32)
        shared_sum[...] = jnp.zeros_like(shared_sum)
        shared_mix[...] = jnp.zeros_like(shared_mix)

        def visit(step, unused):
            start = pl.multiple_of(step * block, block)
            bias = shown_bias(start, block, rows, first, last)
            for kv in range(local_kv):
                cols = slice(kv * 128, (kv + 1) * 128)
                scores = (
                    lax.dot_general(
                        k_ref[pl.ds(start, block), cols],
                        shared_q[kv],
                        (((1,), (1,)), ((), ())),
                        preferred_element_type=jnp.float32,
                    )
                    + bias
                )
                old_top = shared_top[kv : kv + 1, :]
                top = jnp.maximum(old_top, jnp.max(scores, axis=0, keepdims=True))
                weights = jnp.exp2((scores - top) * base_two)
                factor = jnp.exp2((old_top - top) * base_two)
                shared_top[kv : kv + 1, :] = top
                shared_sum[kv : kv + 1, :] = shared_sum[kv : kv + 1, :] * factor + jnp.sum(
                    weights, axis=0, keepdims=True
                )
                shared_mix[kv] = shared_mix[kv] * factor + jnp.dot(
                    vt_ref[cols, pl.ds(start, block)],
                    weights.astype(jnp.bfloat16),
                    preferred_element_type=jnp.float32,
                )
            return unused

        lax.fori_loop(first // block, (last + block - 1) // block, visit, 0)
        levels = shared_top[...] * score_scale + jnp.log(shared_sum[...])
        for kv in range(local_kv):
            mixed = jnp.transpose(shared_mix[kv] / shared_sum[kv : kv + 1, :]).astype(o_ref.dtype)
            for sub in range(per_kv):
                head = kv * per_kv + sub
                for at, owner in enumerate(members):
                    place = sub * per_group + at
                    o_ref[owner, :, head * 128 : (head + 1) * 128] = mixed[place * tree : (place + 1) * tree]
        for at, owner in enumerate(members):
            put_lse(
                owner,
                jnp.concatenate(
                    [
                        levels[:, (sub * per_group + at) * tree : (sub * per_group + at + 1) * tree]
                        for sub in range(per_kv)
                    ],
                    axis=0,
                ),
            )

    def own_part(owner, first, last):
        lanes = heads * tree
        span = per_kv * tree
        for head in range(heads):
            cols = slice(head // per_kv * 128, (head // per_kv + 1) * 128)
            own_q[head * tree : (head + 1) * tree, cols] = q_ref[owner, :, head * 128 : (head + 1) * 128]
        own_top[...] = jnp.full(own_top.shape, NEGATIVE, jnp.float32)
        own_sum[...] = jnp.zeros_like(own_sum)
        own_mix[...] = jnp.zeros_like(own_mix)

        def visit(step, unused):
            start = pl.multiple_of(step * own_block, own_block)
            scores = lax.dot_general(
                k_ref[pl.ds(start, own_block), :],
                own_q[...],
                (((1,), (1,)), ((), ())),
                preferred_element_type=jnp.float32,
            ) + shown_bias(start, own_block, lanes, first, last)
            old_top = own_top[...]
            top = jnp.maximum(old_top, jnp.max(scores, axis=0, keepdims=True))
            weights = jnp.exp2((scores - top) * base_two)
            factor = jnp.exp2((old_top - top) * base_two)
            own_top[...] = top
            own_sum[...] = own_sum[...] * factor + jnp.sum(weights, axis=0, keepdims=True)
            whole = jnp.dot(
                vt_ref[:, pl.ds(start, own_block)],
                weights.astype(jnp.bfloat16),
                preferred_element_type=jnp.float32,
            )
            which = lax.broadcasted_iota(jnp.int32, (128, lanes), 1) // span
            mixed = whole[:128]
            for kv in range(1, local_kv):
                mixed = jnp.where(which == kv, whole[kv * 128 : (kv + 1) * 128], mixed)
            own_mix[...] = own_mix[...] * factor + mixed
            return unused

        lax.fori_loop(first // own_block, (last + own_block - 1) // own_block, visit, 0)
        levels = own_top[...] * score_scale + jnp.log(own_sum[...])
        mixed = jnp.transpose(own_mix[...] / own_sum[...]).astype(o_ref.dtype)
        for head in range(heads):
            o_ref[owner, :, head * 128 : (head + 1) * 128] = mixed[head * tree : (head + 1) * tree]
        put_lse(
            owner,
            jnp.concatenate(
                [
                    levels[:, (kv * per_kv + sub) * tree : (kv * per_kv + sub + 1) * tree]
                    for sub in range(per_kv)
                    for kv in range(local_kv)
                ],
                axis=0,
            ),
        )

    def group_step(group, start):
        first, last = bounds(start, prefix_ref[group])

        @pl.when(last > first)
        def _():
            shared_part(group, first, last)

        return start + prefix_ref[group]

    def own_step(owner, start):
        first, last = bounds(start, own_ref[owner])

        @pl.when(last > first)
        def _():
            own_part(owner, first, last)

        return start + own_ref[owner]

    own_start = lax.fori_loop(0, groups, group_step, 0)

    @pl.when(base + pool > own_start)
    def _():
        own_q[...] = jnp.zeros_like(own_q)
        lax.fori_loop(0, requests, own_step, own_start)

    for copy in copies:
        copy.wait()


def pool_attention(
    prefix_len, own_len, request_group, query, keys, turned, select, key_new, value_new, per_kv, score_scale
):
    requests, tree, width = query.shape
    pool, kv_width = keys.shape
    local_kv = kv_width // 128
    heads = local_kv * per_kv
    rows = per_kv * (requests // prefix_len.shape[0]) * tree
    lanes = heads * tree
    vmem = pl.BlockSpec(memory_space=pltpu.VMEM)
    smem = pl.BlockSpec(memory_space=pltpu.SMEM)
    hbm = pl.BlockSpec(memory_space=pltpu.HBM)
    return pl.pallas_call(
        functools.partial(pool_kernel, per_kv, min(512, pool), min(256, pool), score_scale),
        out_shape=(
            jax.ShapeDtypeStruct(query.shape, jnp.bfloat16),
            jax.ShapeDtypeStruct((requests, 8, 128), jnp.float32),
            jax.ShapeDtypeStruct(key_new.shape, jnp.bfloat16),
            jax.ShapeDtypeStruct(value_new.shape, jnp.bfloat16),
        ),
        in_specs=[smem] * 3 + [vmem] * 6,
        out_specs=(vmem, vmem, hbm, hbm),
        scratch_shapes=[
            pltpu.SMEM((requests + 1,), jnp.int32),
            pltpu.VMEM(key_new.shape, jnp.bfloat16),
            pltpu.VMEM(value_new.shape, jnp.bfloat16),
            pltpu.VMEM((local_kv, rows, 128), jnp.bfloat16),
            pltpu.VMEM((local_kv, rows), jnp.float32),
            pltpu.VMEM((local_kv, rows), jnp.float32),
            pltpu.VMEM((local_kv, 128, rows), jnp.float32),
            pltpu.VMEM((lanes, kv_width), jnp.bfloat16),
            pltpu.VMEM((1, lanes), jnp.float32),
            pltpu.VMEM((1, lanes), jnp.float32),
            pltpu.VMEM((128, lanes), jnp.float32),
            pltpu.SemaphoreType.DMA((2,)),
        ],
        compiler_params=pltpu.CompilerParams(vmem_limit_bytes=40 * 2**20),
        name="pool_attention",
    )(prefix_len, own_len, request_group, query, keys, turned, select, key_new, value_new)


def body(
    hidden,
    in_gain,
    w_query,
    key_projection_weight,
    value_projection_weight,
    w_gate,
    w_out,
    q_gain,
    k_gain,
    cache_keys,
    pooled_cache_values,
    prefix_len,
    own_len,
    request_group,
    parents,
    accepted_leaf,
):
    local_req, tree = parents.shape
    requests = own_len.shape[0]
    head_width = q_gain.shape[0]
    local_heads = w_gate.shape[1]
    local_kv = key_projection_weight.shape[1] // head_width
    per_kv = local_heads // local_kv
    local_tok = hidden.shape[0]
    pool_dev = cache_keys.shape[0]
    score_scale = 1.0 / math.sqrt(head_width)
    seq_count = requests // local_req
    kv_count = in_gain.shape[0] // hidden.shape[1]
    half = np.exp(np.arange(head_width // 2) * (-2.0 * math.log(ROPE_BASE) / head_width))
    freqs = np.concatenate([half, half]).astype(np.float32)

    lines = [in_gain.reshape(-1, head_width), q_gain[None], k_gain[None], jnp.asarray(freqs)[None]]
    lines += [prefix_len[None], own_len[None], request_group[None], accepted_leaf[None], parents]
    depth = sum(values.shape[0] for values in lines)
    depth += -depth % 8
    sums = {}
    top = 0
    for values in lines:
        rows, lanes = values.shape
        edges = ((top, depth - top - rows, 0), (0, head_width - lanes, 0))
        padded = lax.pad(values, jnp.zeros((), values.dtype), edges)
        sums[values.dtype] = sums[values.dtype] + padded if values.dtype in sums else padded
        top += rows
    small = functools.reduce(jnp.add, [total.astype(jnp.float32) for total in sums.values()])
    gathered, key_new, value_new, tree_mix, tree_lse, gate, select, keys, turned = layer_front(
        hidden,
        small,
        w_query,
        key_projection_weight,
        value_projection_weight,
        w_gate.T,
        cache_keys.reshape(pool_dev * local_kv, head_width),
        pooled_cache_values.reshape(pool_dev * local_kv, head_width),
        seq_count,
        kv_count,
        tree,
        score_scale,
    )
    parts, part_lse, accepted_keys, accepted_values = pool_attention(
        prefix_len,
        own_len,
        request_group,
        gathered,
        keys,
        turned,
        select,
        key_new,
        value_new,
        per_kv,
        score_scale,
    )
    layer_out = merge_parts(
        parts, part_lse, tree_mix, tree_lse, gate, w_out, hidden, seq_count, kv_count, per_kv
    )
    return (
        layer_out,
        accepted_keys.reshape(local_req, tree, local_kv * head_width),
        accepted_values.reshape(local_req, tree, local_kv * head_width),
    )


def solution(mesh):
    in_specs = (
        P("seq", "kv"),
        P(),
        P(None, "kv"),
        P(None, "kv"),
        P(None, "kv"),
        P(None, "kv"),
        P("kv", None),
        P(),
        P(),
        P("seq", "kv", None),
        P("seq", "kv", None),
        P(),
        P(),
        P(),
        P("seq", None),
        P("seq"),
    )
    out_specs = (P("seq", "kv"), P("seq", None, "kv"), P("seq", None, "kv"))
    return jax.shard_map(body, mesh=mesh, in_specs=in_specs, out_specs=out_specs, check_vma=False)
```

```python
import functools
import math

import jax
import jax.numpy as jnp
import numpy as np
from jax import lax
from jax.experimental import pallas as pl
from jax.experimental.pallas import tpu as pltpu
from jax.sharding import PartitionSpec as P

EPSILON = 1e-06
ROPE_BASE = 1000000.0
NEGATIVE = -1e30
FRONT_VMEM = 47 * 2**20


def rms_scale(values, scales):
    mean_square = jnp.mean(values * values, axis=-1, keepdims=True)
    return values * lax.rsqrt(mean_square + EPSILON) * scales


def rope_angles(positions, freqs):
    angles = positions * freqs
    turns = jnp.floor(angles * (2.0 / math.pi) + 0.5)
    rest = angles - turns * 1.5703125
    rest = rest - turns * 4.837512969970703125e-4
    rest = rest - turns * 7.549789954891882e-8
    square = rest * rest
    sine = rest + rest * square * (
        -1.6666654611e-1 + square * (8.3321608736e-3 - square * 1.9515295891e-4)
    )
    cosine = (
        1.0
        - 0.5 * square
        + square * square * (4.166664568298827e-2 + square * (-1.388731625493765e-3 + square * 2.443315711809948e-5))
    )
    quarter = turns.astype(jnp.int32) & 3
    swapped = (quarter & 1) == 1
    cos_out = jnp.where(swapped, sine, cosine)
    sin_out = jnp.where(swapped, cosine, sine)
    cos_out = jnp.where((quarter == 1) | (quarter == 2), -cos_out, cos_out)
    sin_out = jnp.where(quarter >= 2, -sin_out, sin_out)
    return cos_out, sin_out


def tree_tables(parents, leaves, contexts, freqs):
    local_req, width = parents.shape
    tokens = local_req * width
    rows = lax.broadcasted_iota(jnp.int32, (tokens, tokens), 0)
    cols = lax.broadcasted_iota(jnp.int32, (tokens, tokens), 1)
    above = jnp.concatenate(
        [parents[at : at + 1, :] + at * width for at in range(local_req)], axis=1
    )
    reached = jnp.where((above == rows) | (rows == cols), 1.0, 0.0)
    for squaring in range(max(1, (width - 1).bit_length())):
        half = reached.astype(jnp.bfloat16)
        reached = jnp.minimum(jnp.dot(half, half, preferred_element_type=jnp.float32), 1.0)
    reach = jnp.transpose(reached)
    depth_across = jnp.sum(reached, axis=0, keepdims=True) - 1.0
    depth_down = jnp.sum(reach, axis=1, keepdims=True) - 1.0
    which = lax.broadcasted_iota(jnp.int32, (tokens, 1), 0) // width
    context = jnp.zeros((tokens, 1), jnp.float32)
    is_leaf = rows < 0
    for at in range(local_req):
        context = jnp.where(which == at, contexts[at], context)
        is_leaf = is_leaf | (rows == leaves[:, at : at + 1] + at * width)
    on_path = jnp.sum(jnp.where(is_leaf, reach, 0.0), axis=0, keepdims=True)
    level = (rows % width).astype(jnp.float32)
    picked = (depth_across == level) & (rows // width == cols // width)
    select = jnp.where(picked, jnp.broadcast_to(on_path, (tokens, tokens)), 0.0)
    cosine, sine = rope_angles(context + depth_down, freqs)
    lanes = lax.broadcasted_iota(jnp.int32, cosine.shape, 1)
    sine = jnp.where(lanes < cosine.shape[1] // 2, -sine, sine)
    return reach, select, cosine, sine


def lowest(distance):
    return distance & -distance


def flip(index, distance):
    out = index
    bit = 1
    while bit <= distance:
        if distance & bit:
            out = out + bit * (1 - 2 * ((index // bit) % 2))
        bit *= 2
    return out


def one_bits(count):
    bits = []
    bit = 1
    while bit < count:
        bits.append(bit)
        bit *= 2
    return bits


def greet(me, count, kv, kv_count):
    barrier = pltpu.get_barrier_semaphore()
    bits = one_bits(count)
    for bit in bits:
        pl.semaphore_signal(barrier, inc=1, device_id={"seq": flip(me, bit)})
    for hop in range(1, kv_count):
        pl.semaphore_signal(barrier, inc=1, device_id={"kv": (kv + hop) % kv_count})
    pl.semaphore_wait(barrier, len(bits) + kv_count - 1)


def layer_kernel(
    count,
    kv_count,
    tree,
    score_scale,
    hidden_ref,
    small_ref,
    w_query_ref,
    w_key_ref,
    w_value_ref,
    w_gate_ref,
    cache_key_ref,
    cache_value_ref,
    all_ref,
    key_ref,
    value_ref,
    tree_ref,
    tree_lse_ref,
    gate_ref,
    select_ref,
    keys_ref,
    turned_ref,
    wide,
    w_query,
    w_key,
    w_value,
    w_gate,
    raw_keys,
    raw_values,
    stage,
    cos_ref,
    sin_ref,
    seen_ref,
    load_sem,
    wide_send,
    wide_recv,
    send_sem,
    recv_sem,
):
    me = lax.axis_index("seq")
    kv = lax.axis_index("kv")
    loads = [
        pltpu.make_async_copy(source, target, load_sem.at[which])
        for which, (source, target) in enumerate(
            [
                (hidden_ref, wide.at[kv]),
                (w_query_ref, w_query),
                (w_key_ref, w_key),
                (w_value_ref, w_value),
                (w_gate_ref, w_gate),
                (cache_key_ref, raw_keys),
                (cache_value_ref, raw_values),
            ]
        )
    ]
    for load in loads:
        load.start()
    loads[0].wait()
    greet(me, count, kv, kv_count)

    def wide_message(hop, owner):
        return pltpu.make_async_remote_copy(
            src_ref=wide.at[owner],
            dst_ref=wide.at[owner],
            send_sem=wide_send.at[hop],
            recv_sem=wide_recv.at[hop],
            device_id={"kv": (kv + hop) % kv_count},
        )

    wide_sent = [wide_message(hop, kv) for hop in range(1, kv_count)]
    for copy in wide_sent:
        copy.start()
    lane = lax.broadcasted_iota(jnp.int32, (1, 128), 1)
    tables = wide.shape[0] * wide.shape[2] // 128

    def row(at):
        return small_ref[tables + at : tables + at + 1, :]

    def taken(values, index):
        return jnp.sum(jnp.where(lane == index, values, 0.0), axis=1, keepdims=True)

    local_req = hidden_ref.shape[0] // tree
    contexts = [
        taken(row(3), taken(row(5), me * local_req + at).astype(jnp.int32))
        + taken(row(4), me * local_req + at)
        for at in range(local_req)
    ]
    parents = jnp.concatenate([row(7 + at)[:, :tree] for at in range(local_req)], axis=0).astype(jnp.int32)
    reach, select, cosine, sine = tree_tables(parents, row(6).astype(jnp.int32), contexts, row(2))
    seen_ref[...] = reach
    select_ref[...] = select.astype(jnp.bfloat16)
    cos_ref[...] = cosine
    sin_ref[...] = sine
    for hop in range(1, kv_count):
        wide_message(hop, (kv + kv_count - hop) % kv_count).wait_recv()
    rows = jnp.concatenate([wide[at] for at in range(kv_count)], axis=1).astype(jnp.float32)
    mean_square = jnp.mean(rows * rows, axis=-1, keepdims=True)
    inverse = lax.rsqrt(mean_square + EPSILON)
    normed = jnp.concatenate(
        [
            (rows[:, at * 128 : (at + 1) * 128] * inverse * small_ref[at : at + 1, :]).astype(jnp.bfloat16)
            for at in range(rows.shape[1] // 128)
        ],
        axis=1,
    )

    def rotated(values, gain):
        values = rms_scale(values, gain)
        return (values * cos_ref[...] + pltpu.roll(values, 64, 1) * sin_ref[...]).astype(jnp.bfloat16)

    loads[1].wait()
    query = jnp.dot(normed, w_query[...], preferred_element_type=jnp.float32)
    heads = query.shape[1] // 128
    queries = [rotated(query[:, h * 128 : (h + 1) * 128], row(0)) for h in range(heads)]
    for head in range(heads):
        for at in range(local_req):
            all_ref[me * local_req + at, :, head * 128 : (head + 1) * 128] = queries[head][
                at * tree : (at + 1) * tree
            ]

    def message(distance, place, at):
        return pltpu.make_async_remote_copy(
            src_ref=all_ref.at[place],
            dst_ref=all_ref.at[place],
            send_sem=send_sem.at[distance, at],
            recv_sem=recv_sem.at[distance, at],
            device_id={"seq": flip(me, lowest(distance))},
        )

    sent = []

    def hand_on(distance, at):
        owner = flip(me, distance) * local_req + at
        if distance:
            message(distance, owner, at).wait_recv()
        for bit in reversed(one_bits(lowest(distance) if distance else count)):
            copy = message(distance | bit, owner, at)
            copy.start()
            sent.append(copy)

    for at in range(local_req):
        hand_on(0, at)
    local_kv = key_ref.shape[1] // 128
    per_kv = heads // local_kv
    tokens = hidden_ref.shape[0]

    def keys_work():
        loads[2].wait()
        key = jnp.dot(normed, w_key[...], preferred_element_type=jnp.float32)
        for at in range(local_kv):
            cols = slice(at * 128, (at + 1) * 128)
            key_ref[:, cols] = rotated(key[:, cols], row(1))

    def values_work():
        loads[3].wait()
        loads[4].wait()
        value_ref[...] = jnp.dot(
            normed, w_value[...], preferred_element_type=jnp.float32
        ).astype(jnp.bfloat16)
        gate_ref[...] = jax.nn.sigmoid(
            lax.dot_general(
                normed, w_gate[...], (((1,), (1,)), ((), ())), preferred_element_type=jnp.float32
            )
        )
        tree_lse_ref[...] = jnp.zeros(tree_lse_ref.shape, jnp.float32)

    def tree_work(at):
        cols = slice(at * 128, (at + 1) * 128)
        stacked = jnp.concatenate(queries[at * per_kv : (at + 1) * per_kv], axis=0)
        scores = (
            lax.dot_general(
                stacked,
                key_ref[:, cols],
                (((1,), (1,)), ((), ())),
                preferred_element_type=jnp.float32,
            )
            * score_scale
        )
        seen = jnp.concatenate([seen_ref[...]] * per_kv, axis=0) > 0.5
        scores = jnp.where(seen, scores, NEGATIVE)
        top = jnp.max(scores, axis=1, keepdims=True)
        weights = jnp.where(seen, jnp.exp(scores - top), 0.0)
        total = jnp.sum(weights, axis=1, keepdims=True)
        mixed = (
            jnp.dot(
                weights.astype(jnp.bfloat16), value_ref[:, cols], preferred_element_type=jnp.float32
            )
            / total
        )
        lse = top + jnp.log(total)
        for sub in range(per_kv):
            head = at * per_kv + sub
            part = slice(sub * tokens, (sub + 1) * tokens)
            tree_ref[:, head * 128 : (head + 1) * 128] = mixed[part]
            column = sub * local_kv + at
            tree_lse_ref[:, column : column + 1] = lse[part]

    pieces = 8
    slots = keys_ref.shape[0] // pieces

    def apart(source, which):
        stage[...] = source[which * slots * local_kv : (which + 1) * slots * local_kv, :].astype(jnp.float32)
        return [stage[pl.ds(at, slots, stride=local_kv), :] for at in range(local_kv)]

    def keys_apart(which):
        if which == 0:
            loads[5].wait()
        for at, part in enumerate(apart(raw_keys, which)):
            keys_ref[which * slots : (which + 1) * slots, at * 128 : (at + 1) * 128] = part.astype(jnp.bfloat16)

    def values_apart(which):
        if which == 0:
            loads[6].wait()
        for at, part in enumerate(apart(raw_values, which)):
            turned_ref[at * 128 : (at + 1) * 128, which * slots : (which + 1) * slots] = jnp.transpose(
                part
            ).astype(jnp.bfloat16)

    work = [keys_work, values_work] + [functools.partial(tree_work, at) for at in range(local_kv)]
    work += [functools.partial(keys_apart, which) for which in range(pieces)]
    work += [functools.partial(values_apart, which) for which in range(pieces)]
    order = sorted(range(2, count, 2), key=lambda d: (-lowest(d), d))
    for distance in order:
        for at in range(local_req):
            for once in range(2):
                if work:
                    work.pop(0)()
            hand_on(distance, at)
    for rest in work:
        rest()
    for distance in range(1, count, 2):
        for at in range(local_req):
            hand_on(distance, at)
    for copy in wide_sent + sent:
        copy.wait_send()


def layer_front(
    hidden,
    small,
    w_query,
    w_key,
    w_value,
    w_gate,
    cache_keys,
    cache_values,
    count,
    kv_count,
    tree,
    score_scale,
):
    tokens = hidden.shape[0]
    width = w_query.shape[1]
    local_kv = w_key.shape[1] // 128
    slots = cache_keys.shape[0] // local_kv
    vmem = pl.BlockSpec(memory_space=pltpu.VMEM)
    hbm = pl.BlockSpec(memory_space=pltpu.HBM)
    return pl.pallas_call(
        functools.partial(layer_kernel, count, kv_count, tree, score_scale),
        out_shape=(
            jax.ShapeDtypeStruct((count * tokens // tree, tree, width), jnp.bfloat16),
            jax.ShapeDtypeStruct((tokens, w_key.shape[1]), jnp.bfloat16),
            jax.ShapeDtypeStruct((tokens, w_value.shape[1]), jnp.bfloat16),
            jax.ShapeDtypeStruct((tokens, width), jnp.float32),
            jax.ShapeDtypeStruct((tokens, 128), jnp.float32),
            jax.ShapeDtypeStruct((tokens, w_gate.shape[0]), jnp.float32),
            jax.ShapeDtypeStruct((tokens, tokens), jnp.bfloat16),
            jax.ShapeDtypeStruct((slots, local_kv * 128), jnp.bfloat16),
            jax.ShapeDtypeStruct((local_kv * 128, slots), jnp.bfloat16),
        ),
        in_specs=[hbm, vmem] + [hbm] * 6,
        out_specs=(vmem,) * 9,
        scratch_shapes=[
            pltpu.VMEM((kv_count,) + hidden.shape, hidden.dtype),
            pltpu.VMEM(w_query.shape, w_query.dtype),
            pltpu.VMEM(w_key.shape, w_key.dtype),
            pltpu.VMEM(w_value.shape, w_value.dtype),
            pltpu.VMEM(w_gate.shape, w_gate.dtype),
            pltpu.VMEM(cache_keys.shape, jnp.bfloat16),
            pltpu.VMEM(cache_values.shape, jnp.bfloat16),
            pltpu.VMEM((cache_keys.shape[0] // 8, 128), jnp.float32),
            pltpu.VMEM((tokens, 128), jnp.float32),
            pltpu.VMEM((tokens, 128), jnp.float32),
            pltpu.VMEM((tokens, tokens), jnp.float32),
            pltpu.SemaphoreType.DMA((7,)),
            pltpu.SemaphoreType.DMA((kv_count,)),
            pltpu.SemaphoreType.DMA((kv_count,)),
            pltpu.SemaphoreType.DMA((count, tokens // tree)),
            pltpu.SemaphoreType.DMA((count, tokens // tree)),
        ],
        compiler_params=pltpu.CompilerParams(
            collective_id=0, has_side_effects=True, vmem_limit_bytes=FRONT_VMEM
        ),
        name="layer_front",
    )(
        hidden,
        small,
        w_query,
        w_key,
        w_value,
        w_gate,
        cache_keys,
        cache_values,
    )


def merge_kernel(
    count,
    kv_count,
    per_kv,
    part_ref,
    lse_ref,
    tree_ref,
    tree_lse_ref,
    gate_ref,
    w_out_ref,
    hidden_ref,
    out_ref,
    got,
    got_lse,
    held,
    held_lse,
    w_out,
    attended,
    outgoing,
    arrived,
    send_sem,
    recv_sem,
    load_sem,
    out_send,
    out_recv,
):
    me = lax.axis_index("seq")
    kv = lax.axis_index("kv")
    requests, rows, _ = part_ref.shape
    local_req = requests // count
    heads = part_ref.shape[2] // 128
    load = pltpu.make_async_copy(w_out_ref, w_out, load_sem)
    load.start()
    greet(me, count, kv, kv_count)

    def messages(distance, at):
        owner = flip(me, distance) * local_req + at
        if distance % 2:
            sources = (part_ref.at[owner], lse_ref.at[owner])
        else:
            sources = (held.at[distance // 2, at], held_lse.at[distance // 2, at])
        return [
            pltpu.make_async_remote_copy(
                src_ref=source,
                dst_ref=target.at[distance, at],
                send_sem=send_sem.at[which, distance, at],
                recv_sem=recv_sem.at[which, distance, at],
                device_id={"seq": flip(me, lowest(distance))},
            )
            for which, (source, target) in enumerate(zip(sources, (got, got_lse)))
        ]

    sent = []

    def send(distance, at):
        for copy in messages(distance, at):
            copy.start()
            sent.append(copy)

    def combined(distance, at):
        owner = flip(me, distance) * local_req + at
        incoming = [distance | bit for bit in one_bits(lowest(distance) if distance else count)]
        for message in incoming:
            for copy in messages(message, at):
                copy.wait_recv()
        levels = [lse_ref[owner]] + [got_lse[message, at] for message in incoming]
        own = slice(at * rows, (at + 1) * rows)
        if not distance:
            turned = jnp.transpose(tree_lse_ref[own, :])[:8]
            levels.append(jnp.concatenate([turned] * (128 // rows), axis=1))
        top = functools.reduce(jnp.maximum, levels)
        shares = [jnp.exp(level - top) for level in levels]
        total = functools.reduce(jnp.add, shares)
        inverse = 1.0 / total
        shares = [jnp.transpose(share * inverse)[:rows] for share in shares]
        if distance:
            held_lse[distance // 2, at] = top + jnp.log(total)
        for head in range(heads):
            cols = slice(head * 128, (head + 1) * 128)
            place = head % per_kv * (heads // per_kv) + head // per_kv
            pieces = [part_ref[owner, :, cols]] + [got[message, at, :, cols] for message in incoming]
            if not distance:
                pieces.append(tree_ref[own, cols])
            mixed = functools.reduce(
                jnp.add,
                [
                    piece.astype(jnp.float32) * share[:, place : place + 1]
                    for piece, share in zip(pieces, shares)
                ],
            )
            if distance:
                held[distance // 2, at, :, cols] = mixed.astype(held.dtype)
            else:
                attended[own, cols] = (mixed * gate_ref[own, head : head + 1]).astype(jnp.bfloat16)

    for distance in sorted(range(1, count, 2), reverse=True):
        for at in range(local_req):
            send(distance, at)
    for distance in sorted(range(2, count, 2), key=lambda d: (lowest(d), -d)):
        for at in range(local_req):
            combined(distance, at)
            send(distance, at)
    width = out_ref.shape[1]

    def projected(target, at):
        cols = pl.ds(pl.multiple_of(target * width, 128), width)
        return jnp.dot(
            attended[at * rows : (at + 1) * rows, :], w_out[:, cols], preferred_element_type=jnp.float32
        )

    def out_message(hop, at):
        return pltpu.make_async_remote_copy(
            src_ref=outgoing.at[hop, at],
            dst_ref=arrived.at[hop, at],
            send_sem=out_send.at[hop, at],
            recv_sem=out_recv.at[hop, at],
            device_id={"kv": (kv + hop) % kv_count},
        )

    totals = []
    for at in range(local_req):
        combined(0, at)
        if not at:
            load.wait()
        for hop in range(1, kv_count):
            outgoing[hop, at] = projected((kv + hop) % kv_count, at).astype(jnp.bfloat16)
            copy = out_message(hop, at)
            copy.start()
            sent.append(copy)
        totals.append(projected(kv, at))
    for at in range(local_req):
        total = totals[at]
        own = slice(at * rows, (at + 1) * rows)
        for hop in range(1, kv_count):
            out_message(hop, at).wait_recv()
            total = total + arrived[hop, at].astype(jnp.float32)
        out_ref[own, :] = (total + hidden_ref[own, :].astype(jnp.float32)).astype(jnp.bfloat16)
    for copy in sent:
        copy.wait_send()


def merge_parts(parts, lse, tree_mix, tree_lse, gate, w_out, hidden, count, kv_count, per_kv):
    requests, rows, width = parts.shape
    local_req = requests // count
    half = max(1, count // 2)
    vmem = pl.BlockSpec(memory_space=pltpu.VMEM)
    crossing = (kv_count, local_req, rows, hidden.shape[1])
    return pl.pallas_call(
        functools.partial(merge_kernel, count, kv_count, per_kv),
        out_shape=jax.ShapeDtypeStruct(hidden.shape, jnp.bfloat16),
        in_specs=[vmem] * 5 + [pl.BlockSpec(memory_space=pltpu.HBM), vmem],
        out_specs=vmem,
        scratch_shapes=[
            pltpu.VMEM((count, local_req, rows, width), parts.dtype),
            pltpu.VMEM((count, local_req) + lse.shape[1:], jnp.float32),
            pltpu.VMEM((half, local_req, rows, width), parts.dtype),
            pltpu.VMEM((half, local_req) + lse.shape[1:], jnp.float32),
            pltpu.VMEM(w_out.shape, w_out.dtype),
            pltpu.VMEM((local_req * rows, width), jnp.bfloat16),
            pltpu.VMEM(crossing, jnp.bfloat16),
            pltpu.VMEM(crossing, jnp.bfloat16),
            pltpu.SemaphoreType.DMA((2, count, local_req)),
            pltpu.SemaphoreType.DMA((2, count, local_req)),
            pltpu.SemaphoreType.DMA,
            pltpu.SemaphoreType.DMA((kv_count, local_req)),
            pltpu.SemaphoreType.DMA((kv_count, local_req)),
        ],
        compiler_params=pltpu.CompilerParams(
            collective_id=1, has_side_effects=True, vmem_limit_bytes=48 * 2**20
        ),
        name="merge_parts",
    )(parts, lse, tree_mix, tree_lse, gate, w_out, hidden)


def pool_kernel(
    per_kv,
    block,
    own_block,
    score_scale,
    prefix_ref,
    own_ref,
    group_ref,
    q_ref,
    k_ref,
    vt_ref,
    select_ref,
    key_new_ref,
    value_new_ref,
    o_ref,
    lse_ref,
    accepted_keys_ref,
    accepted_values_ref,
    member_ref,
    picked_keys,
    picked_values,
    shared_q,
    shared_top,
    shared_sum,
    shared_mix,
    own_q,
    own_top,
    own_sum,
    own_mix,
    score_ref,
    peak_ref,
    picked_sem,
):
    requests, tree, width = q_ref.shape
    groups = prefix_ref.shape[0]
    pool, kv_width = k_ref.shape
    local_kv = kv_width // 128
    heads = local_kv * per_kv
    per_group = requests // groups
    rows = per_kv * per_group * tree
    part = min(256, block)
    base_two = score_scale / math.log(2.0)
    base = lax.axis_index("seq") * pool
    picked = select_ref[...]
    picked_keys[...] = jnp.dot(picked, key_new_ref[...], preferred_element_type=jnp.float32).astype(jnp.bfloat16)
    picked_values[...] = jnp.dot(picked, value_new_ref[...], preferred_element_type=jnp.float32).astype(
        jnp.bfloat16
    )
    copies = [
        pltpu.make_async_copy(picked_keys, accepted_keys_ref, picked_sem.at[0]),
        pltpu.make_async_copy(picked_values, accepted_values_ref, picked_sem.at[1]),
    ]
    for copy in copies:
        copy.start()
    o_ref[...] = jnp.zeros_like(o_ref)
    lse_ref[...] = jnp.full(lse_ref.shape, NEGATIVE, jnp.float32)

    def put_lse(owner, levels):
        wide = jnp.concatenate([levels] * (128 // tree), axis=1)
        if heads < 8:
            wide = jnp.concatenate([wide] * (8 // heads), axis=0)
        lse_ref[owner] = wide

    def bounds(start, length):
        return jnp.clip(start - base, 0, pool), jnp.clip(start + length - base, 0, pool)

    def find_members(group):
        def find(request, found):
            member_ref[found] = request
            return found + (group_ref[request] == group).astype(jnp.int32)

        lax.fori_loop(0, requests, find, 0)
        return [member_ref[at] for at in range(per_group)]

    def shared_part(group, first, last):
        members = find_members(group)
        for kv in range(local_kv):
            for sub in range(per_kv):
                head = kv * per_kv + sub
                for at, owner in enumerate(members):
                    place = sub * per_group + at
                    shared_q[kv, place * tree : (place + 1) * tree, :] = q_ref[
                        owner, :, head * 128 : (head + 1) * 128
                    ]
        shared_top[...] = jnp.full(shared_top.shape, NEGATIVE, jnp.float32)
        shared_sum[...] = jnp.zeros_like(shared_sum)
        shared_mix[...] = jnp.zeros_like(shared_mix)
        first_step = first // block
        final_step = (last + block - 1) // block - 1

        def scored(start, kv, piece):
            low = pl.multiple_of(start + piece * part, part)
            slots = low + lax.broadcasted_iota(jnp.int32, (part, 128), 0)
            bias = jnp.where((slots >= first) & (slots < last), 0.0, NEGATIVE)
            bias = jnp.concatenate([bias] * (rows // 128), axis=1)
            raw = (
                lax.dot_general(
                    k_ref[pl.ds(low, part), kv * 128 : (kv + 1) * 128],
                    shared_q[kv],
                    (((1,), (1,)), ((), ())),
                    preferred_element_type=jnp.float32,
                )
                + bias
            )
            score_ref[kv % 2, piece * part : (piece + 1) * part, :rows] = raw
            return jnp.max(raw, axis=0, keepdims=True)

        peaks = [scored(first_step * block, 0, piece) for piece in range(block // part)]
        peak_ref[0:1, :rows] = functools.reduce(jnp.maximum, peaks)

        def visit(step, unused):
            start = step * block
            later = jnp.minimum(step + 1, final_step) * block
            for kv in range(local_kv):
                next_kv = (kv + 1) % local_kv
                next_start = later if next_kv == 0 else start
                slot = kv % 2
                old_top = shared_top[kv : kv + 1, :]
                top = jnp.maximum(old_top, peak_ref[slot : slot + 1, :rows])
                factor = jnp.exp2((old_top - top) * base_two)
                shared_top[kv : kv + 1, :] = top
                total = shared_sum[kv : kv + 1, :] * factor
                mixed = shared_mix[kv] * factor
                peaks = []
                for piece in range(block // part):
                    peaks.append(scored(next_start, next_kv, piece))
                    weights = jnp.exp2(
                        (score_ref[slot, piece * part : (piece + 1) * part, :rows] - top) * base_two
                    )
                    total = total + jnp.sum(weights, axis=0, keepdims=True)
                    low = pl.multiple_of(start + piece * part, part)
                    mixed = mixed + jnp.dot(
                        vt_ref[kv * 128 : (kv + 1) * 128, pl.ds(low, part)],
                        weights.astype(jnp.bfloat16),
                        preferred_element_type=jnp.float32,
                    )
                peak_ref[1 - slot : 2 - slot, :rows] = functools.reduce(jnp.maximum, peaks)
                shared_sum[kv : kv + 1, :] = total
                shared_mix[kv] = mixed
            return unused

        lax.fori_loop(first_step, final_step + 1, visit, 0)
        levels = shared_top[...] * score_scale + jnp.log(shared_sum[...])
        for kv in range(local_kv):
            mixed = jnp.transpose(shared_mix[kv] / shared_sum[kv : kv + 1, :]).astype(o_ref.dtype)
            for sub in range(per_kv):
                head = kv * per_kv + sub
                for at, owner in enumerate(members):
                    place = sub * per_group + at
                    o_ref[owner, :, head * 128 : (head + 1) * 128] = mixed[place * tree : (place + 1) * tree]
        for at, owner in enumerate(members):
            put_lse(
                owner,
                jnp.concatenate(
                    [
                        levels[:, (sub * per_group + at) * tree : (sub * per_group + at + 1) * tree]
                        for sub in range(per_kv)
                    ],
                    axis=0,
                ),
            )

    lanes = heads * tree
    blocks = pool // own_block

    def own_parts(start):
        own_q[...] = jnp.zeros_like(own_q)

        def seek(request, found):
            owner, begin = found
            passed = (owner == request) & (begin + own_ref[request] <= base)
            return (
                owner + passed.astype(jnp.int32),
                begin + jnp.where(passed, own_ref[request], 0),
            )

        owner, begin = lax.fori_loop(0, requests - 1, seek, (0, start))

        def stop_of(owner, begin):
            return begin + own_ref[owner] - base

        def scored(step, slot, owner, stop):
            other = jnp.minimum(owner + 1, requests - 1)
            for which, request in enumerate((owner, other)):
                for head in range(heads):
                    cols = slice(head // per_kv * 128, (head // per_kv + 1) * 128)
                    low = which * lanes + head * tree
                    own_q[slot, low : low + tree, cols] = q_ref[request, :, head * 128 : (head + 1) * 128]
            low = pl.multiple_of(step * own_block, own_block)
            slots = low + lax.broadcasted_iota(jnp.int32, (own_block, 128), 0)
            before = jnp.where(slots < stop, 0.0, NEGATIVE)
            after = jnp.where(slots < stop, NEGATIVE, 0.0)
            bias = jnp.concatenate([before] * (lanes // 128) + [after] * (lanes // 128), axis=1)
            raw = (
                lax.dot_general(
                    k_ref[pl.ds(low, own_block), :],
                    own_q[slot],
                    (((1,), (1,)), ((), ())),
                    preferred_element_type=jnp.float32,
                )
                + bias
            )
            score_ref[slot, :own_block, : 2 * lanes] = raw
            peak_ref[pl.ds(slot, 1), : 2 * lanes] = jnp.max(raw, axis=0, keepdims=True)

        def finish(owner):
            levels = own_top[...] * score_scale + jnp.log(own_sum[...])
            mixed = jnp.transpose(own_mix[...] / own_sum[...]).astype(o_ref.dtype)
            for head in range(heads):
                o_ref[owner, :, head * 128 : (head + 1) * 128] = mixed[head * tree : (head + 1) * tree]
            put_lse(
                owner,
                jnp.concatenate(
                    [
                        levels[:, (kv * per_kv + sub) * tree : (kv * per_kv + sub + 1) * tree]
                        for sub in range(per_kv)
                        for kv in range(local_kv)
                    ],
                    axis=0,
                ),
            )

        scored(0, 0, owner, stop_of(owner, begin))
        own_top[...] = jnp.full(own_top.shape, NEGATIVE, jnp.float32)
        own_sum[...] = jnp.zeros_like(own_sum)
        own_mix[...] = jnp.zeros_like(own_mix)

        def visit(step, at):
            owner, begin = at
            slot = step % 2
            ended = stop_of(owner, begin) <= (step + 1) * own_block
            next_owner = jnp.where(ended, jnp.minimum(owner + 1, requests - 1), owner)
            next_begin = jnp.where(ended, begin + own_ref[owner], begin)
            scored(jnp.minimum(step + 1, blocks - 1), 1 - slot, next_owner, stop_of(next_owner, next_begin))
            peak = peak_ref[pl.ds(slot, 1), : 2 * lanes]
            old_top = own_top[...]
            mine = jnp.maximum(old_top, peak[:, :lanes])
            top = jnp.concatenate([mine, peak[:, lanes:]], axis=1)
            factor = jnp.exp2((old_top - mine) * base_two)
            weights = jnp.exp2((score_ref[slot, :own_block, : 2 * lanes] - top) * base_two)
            total = jnp.sum(weights, axis=0, keepdims=True)
            low = pl.multiple_of(step * own_block, own_block)
            whole = jnp.dot(
                vt_ref[:, pl.ds(low, own_block)],
                weights.astype(jnp.bfloat16),
                preferred_element_type=jnp.float32,
            )
            which = lax.broadcasted_iota(jnp.int32, (128, 2 * lanes), 1) // (per_kv * tree) % local_kv
            mixed = whole[:128]
            for kv in range(1, local_kv):
                mixed = jnp.where(which == kv, whole[kv * 128 : (kv + 1) * 128], mixed)
            own_top[...] = mine
            own_sum[...] = own_sum[...] * factor + total[:, :lanes]
            own_mix[...] = own_mix[...] * factor + mixed[:, :lanes]

            @pl.when(ended)
            def _():
                finish(owner)
                own_top[...] = peak[:, lanes:]
                own_sum[...] = total[:, lanes:]
                own_mix[...] = mixed[:, lanes:]

            return next_owner, next_begin

        owner, begin = lax.fori_loop(0, blocks, visit, (owner, begin))

        @pl.when(begin < base + pool)
        def _():
            finish(owner)

    def group_step(group, start):
        first, last = bounds(start, prefix_ref[group])

        @pl.when(last > first)
        def _():
            shared_part(group, first, last)

        return start + prefix_ref[group]

    own_start = lax.fori_loop(0, groups, group_step, 0)

    @pl.when(base + pool > own_start)
    def _():
        own_parts(own_start)

    for copy in copies:
        copy.wait()


def pool_attention(
    prefix_len, own_len, request_group, query, keys, turned, select, key_new, value_new, per_kv, score_scale
):
    requests, tree, width = query.shape
    pool, kv_width = keys.shape
    local_kv = kv_width // 128
    heads = local_kv * per_kv
    rows = per_kv * (requests // prefix_len.shape[0]) * tree
    lanes = heads * tree
    vmem = pl.BlockSpec(memory_space=pltpu.VMEM)
    smem = pl.BlockSpec(memory_space=pltpu.SMEM)
    hbm = pl.BlockSpec(memory_space=pltpu.HBM)
    return pl.pallas_call(
        functools.partial(pool_kernel, per_kv, min(512, pool), min(256, pool), score_scale),
        out_shape=(
            jax.ShapeDtypeStruct(query.shape, jnp.bfloat16),
            jax.ShapeDtypeStruct((requests, 8, 128), jnp.float32),
            jax.ShapeDtypeStruct(key_new.shape, jnp.bfloat16),
            jax.ShapeDtypeStruct(value_new.shape, jnp.bfloat16),
        ),
        in_specs=[smem] * 3 + [vmem] * 6,
        out_specs=(vmem, vmem, hbm, hbm),
        scratch_shapes=[
            pltpu.SMEM((requests + 1,), jnp.int32),
            pltpu.VMEM(key_new.shape, jnp.bfloat16),
            pltpu.VMEM(value_new.shape, jnp.bfloat16),
            pltpu.VMEM((local_kv, rows, 128), jnp.bfloat16),
            pltpu.VMEM((local_kv, rows), jnp.float32),
            pltpu.VMEM((local_kv, rows), jnp.float32),
            pltpu.VMEM((local_kv, 128, rows), jnp.float32),
            pltpu.VMEM((2, 2 * lanes, kv_width), jnp.bfloat16),
            pltpu.VMEM((1, lanes), jnp.float32),
            pltpu.VMEM((1, lanes), jnp.float32),
            pltpu.VMEM((128, lanes), jnp.float32),
            pltpu.VMEM((2, 512, max(rows, 2 * lanes)), jnp.float32),
            pltpu.VMEM((2, max(rows, 2 * lanes)), jnp.float32),
            pltpu.SemaphoreType.DMA((2,)),
        ],
        compiler_params=pltpu.CompilerParams(vmem_limit_bytes=40 * 2**20),
        name="pool_attention",
    )(prefix_len, own_len, request_group, query, keys, turned, select, key_new, value_new)


def body(
    hidden,
    in_gain,
    w_query,
    key_projection_weight,
    value_projection_weight,
    w_gate,
    w_out,
    q_gain,
    k_gain,
    cache_keys,
    pooled_cache_values,
    prefix_len,
    own_len,
    request_group,
    parents,
    accepted_leaf,
):
    local_req, tree = parents.shape
    requests = own_len.shape[0]
    head_width = q_gain.shape[0]
    local_heads = w_gate.shape[1]
    local_kv = key_projection_weight.shape[1] // head_width
    per_kv = local_heads // local_kv
    local_tok = hidden.shape[0]
    pool_dev = cache_keys.shape[0]
    score_scale = 1.0 / math.sqrt(head_width)
    seq_count = requests // local_req
    kv_count = in_gain.shape[0] // hidden.shape[1]
    half = np.exp(np.arange(head_width // 2) * (-2.0 * math.log(ROPE_BASE) / head_width))
    freqs = np.concatenate([half, half]).astype(np.float32)

    lines = [in_gain.reshape(-1, head_width), q_gain[None], k_gain[None], jnp.asarray(freqs)[None]]
    lines += [prefix_len[None], own_len[None], request_group[None], accepted_leaf[None], parents]
    depth = sum(values.shape[0] for values in lines)
    depth += -depth % 8
    sums = {}
    top = 0
    for values in lines:
        rows, lanes = values.shape
        edges = ((top, depth - top - rows, 0), (0, head_width - lanes, 0))
        padded = lax.pad(values, jnp.zeros((), values.dtype), edges)
        sums[values.dtype] = sums[values.dtype] + padded if values.dtype in sums else padded
        top += rows
    small = functools.reduce(jnp.add, [total.astype(jnp.float32) for total in sums.values()])
    gathered, key_new, value_new, tree_mix, tree_lse, gate, select, keys, turned = layer_front(
        hidden,
        small,
        w_query,
        key_projection_weight,
        value_projection_weight,
        w_gate.T,
        cache_keys.reshape(pool_dev * local_kv, head_width),
        pooled_cache_values.reshape(pool_dev * local_kv, head_width),
        seq_count,
        kv_count,
        tree,
        score_scale,
    )
    parts, part_lse, accepted_keys, accepted_values = pool_attention(
        prefix_len,
        own_len,
        request_group,
        gathered,
        keys,
        turned,
        select,
        key_new,
        value_new,
        per_kv,
        score_scale,
    )
    layer_out = merge_parts(
        parts, part_lse, tree_mix, tree_lse, gate, w_out, hidden, seq_count, kv_count, per_kv
    )
    return (
        layer_out,
        accepted_keys.reshape(local_req, tree, local_kv * head_width),
        accepted_values.reshape(local_req, tree, local_kv * head_width),
    )


def solution(mesh):
    in_specs = (
        P("seq", "kv"),
        P(),
        P(None, "kv"),
        P(None, "kv"),
        P(None, "kv"),
        P(None, "kv"),
        P("kv", None),
        P(),
        P(),
        P("seq", "kv", None),
        P("seq", "kv", None),
        P(),
        P(),
        P(),
        P("seq", None),
        P("seq"),
    )
    out_specs = (P("seq", "kv"), P("seq", None, "kv"), P("seq", None, "kv"))
    return jax.shard_map(body, mesh=mesh, in_specs=in_specs, out_specs=out_specs, check_vma=False)
```

```python
import functools
import math

import jax
import jax.numpy as jnp
import numpy as np
from jax import lax
from jax.experimental import pallas as pl
from jax.experimental.pallas import tpu as pltpu
from jax.sharding import PartitionSpec as P

EPSILON = 1e-06
ROPE_BASE = 1000000.0
NEGATIVE = -1e30
FRONT_VMEM = 47 * 2**20


def rms_scale(values, scales):
    mean_square = jnp.mean(values * values, axis=-1, keepdims=True)
    return values * lax.rsqrt(mean_square + EPSILON) * scales


def rope_angles(positions, freqs):
    angles = positions * freqs
    turns = jnp.floor(angles * (2.0 / math.pi) + 0.5)
    rest = angles - turns * 1.5703125
    rest = rest - turns * 4.837512969970703125e-4
    rest = rest - turns * 7.549789954891882e-8
    square = rest * rest
    sine = rest + rest * square * (
        -1.6666654611e-1 + square * (8.3321608736e-3 - square * 1.9515295891e-4)
    )
    cosine = (
        1.0
        - 0.5 * square
        + square * square * (4.166664568298827e-2 + square * (-1.388731625493765e-3 + square * 2.443315711809948e-5))
    )
    quarter = turns.astype(jnp.int32) & 3
    swapped = (quarter & 1) == 1
    cos_out = jnp.where(swapped, sine, cosine)
    sin_out = jnp.where(swapped, cosine, sine)
    cos_out = jnp.where((quarter == 1) | (quarter == 2), -cos_out, cos_out)
    sin_out = jnp.where(quarter >= 2, -sin_out, sin_out)
    return cos_out, sin_out


def tree_tables(parents, leaves, contexts, freqs):
    local_req, width = parents.shape
    tokens = local_req * width
    rows = lax.broadcasted_iota(jnp.int32, (tokens, tokens), 0)
    cols = lax.broadcasted_iota(jnp.int32, (tokens, tokens), 1)
    above = jnp.concatenate(
        [parents[at : at + 1, :] + at * width for at in range(local_req)], axis=1
    )
    reached = jnp.where((above == rows) | (rows == cols), 1.0, 0.0)
    for squaring in range(max(1, (width - 1).bit_length())):
        half = reached.astype(jnp.bfloat16)
        reached = jnp.minimum(jnp.dot(half, half, preferred_element_type=jnp.float32), 1.0)
    reach = jnp.transpose(reached)
    depth_across = jnp.sum(reached, axis=0, keepdims=True) - 1.0
    depth_down = jnp.sum(reach, axis=1, keepdims=True) - 1.0
    which = lax.broadcasted_iota(jnp.int32, (tokens, 1), 0) // width
    context = jnp.zeros((tokens, 1), jnp.float32)
    is_leaf = rows < 0
    for at in range(local_req):
        context = jnp.where(which == at, contexts[at], context)
        is_leaf = is_leaf | (rows == leaves[:, at : at + 1] + at * width)
    on_path = jnp.sum(jnp.where(is_leaf, reach, 0.0), axis=0, keepdims=True)
    level = (rows % width).astype(jnp.float32)
    picked = (depth_across == level) & (rows // width == cols // width)
    select = jnp.where(picked, jnp.broadcast_to(on_path, (tokens, tokens)), 0.0)
    cosine, sine = rope_angles(context + depth_down, freqs)
    lanes = lax.broadcasted_iota(jnp.int32, cosine.shape, 1)
    sine = jnp.where(lanes < cosine.shape[1] // 2, -sine, sine)
    return reach, select, cosine, sine


def lowest(distance):
    return distance & -distance


def flip(index, distance):
    out = index
    bit = 1
    while bit <= distance:
        if distance & bit:
            out = out + bit * (1 - 2 * ((index // bit) % 2))
        bit *= 2
    return out


def one_bits(count):
    bits = []
    bit = 1
    while bit < count:
        bits.append(bit)
        bit *= 2
    return bits


def greet(me, count, kv, kv_count):
    barrier = pltpu.get_barrier_semaphore()
    bits = one_bits(count)
    for bit in bits:
        pl.semaphore_signal(barrier, inc=1, device_id={"seq": flip(me, bit)})
    for hop in range(1, kv_count):
        pl.semaphore_signal(barrier, inc=1, device_id={"kv": (kv + hop) % kv_count})
    pl.semaphore_wait(barrier, len(bits) + kv_count - 1)


def layer_kernel(
    count,
    kv_count,
    tree,
    score_scale,
    hidden_ref,
    small_ref,
    w_query_ref,
    w_key_ref,
    w_value_ref,
    cache_key_ref,
    cache_value_ref,
    all_ref,
    key_ref,
    value_ref,
    tree_ref,
    tree_lse_ref,
    gate_ref,
    select_ref,
    keys_ref,
    turned_ref,
    wide,
    w_query,
    w_key,
    w_value,
    raw_keys,
    raw_values,
    stage,
    cos_ref,
    sin_ref,
    seen_ref,
    load_sem,
    wide_send,
    wide_recv,
    send_sem,
    recv_sem,
):
    me = lax.axis_index("seq")
    kv = lax.axis_index("kv")
    loads = [
        pltpu.make_async_copy(source, target, load_sem.at[which])
        for which, (source, target) in enumerate(
            [
                (hidden_ref, wide.at[kv]),
                (w_query_ref, w_query),
                (w_key_ref, w_key),
                (w_value_ref, w_value),
                (cache_key_ref, raw_keys),
                (cache_value_ref, raw_values),
            ]
        )
    ]
    for load in loads:
        load.start()
    loads[0].wait()
    greet(me, count, kv, kv_count)

    def wide_message(hop, owner):
        return pltpu.make_async_remote_copy(
            src_ref=wide.at[owner],
            dst_ref=wide.at[owner],
            send_sem=wide_send.at[hop],
            recv_sem=wide_recv.at[hop],
            device_id={"kv": (kv + hop) % kv_count},
        )

    wide_sent = [wide_message(hop, kv) for hop in range(1, kv_count)]
    for copy in wide_sent:
        copy.start()
    lane = lax.broadcasted_iota(jnp.int32, (1, 128), 1)

    def row(at):
        return small_ref[1 + at : 2 + at, :128]

    def taken(values, index):
        return jnp.sum(jnp.where(lane == index, values, 0.0), axis=1, keepdims=True)

    local_req = hidden_ref.shape[0] // tree
    contexts = [
        taken(row(3), taken(row(5), me * local_req + at).astype(jnp.int32))
        + taken(row(4), me * local_req + at)
        for at in range(local_req)
    ]
    parents = jnp.concatenate([row(7 + at)[:, :tree] for at in range(local_req)], axis=0).astype(jnp.int32)
    reach, select, cosine, sine = tree_tables(parents, row(6).astype(jnp.int32), contexts, row(2))
    seen_ref[...] = reach
    select_ref[...] = select.astype(jnp.bfloat16)
    cos_ref[...] = cosine
    sin_ref[...] = sine
    for hop in range(1, kv_count):
        wide_message(hop, (kv + kv_count - hop) % kv_count).wait_recv()
    rows = jnp.concatenate([wide[at] for at in range(kv_count)], axis=1).astype(jnp.float32)
    mean_square = jnp.mean(rows * rows, axis=-1, keepdims=True)
    inverse = lax.rsqrt(mean_square + EPSILON)
    normed = (rows * inverse * small_ref[0:1, :]).astype(jnp.bfloat16)

    def rotated(values, gain):
        values = rms_scale(values, gain)
        return (values * cos_ref[...] + pltpu.roll(values, 64, 1) * sin_ref[...]).astype(jnp.bfloat16)

    loads[1].wait()
    query = jnp.dot(normed, w_query[...], preferred_element_type=jnp.float32)
    heads = query.shape[1] // 128
    queries = [rotated(query[:, h * 128 : (h + 1) * 128], row(0)) for h in range(heads)]
    for head in range(heads):
        for at in range(local_req):
            all_ref[me * local_req + at, :, head * 128 : (head + 1) * 128] = queries[head][
                at * tree : (at + 1) * tree
            ]

    def message(distance, place, at):
        return pltpu.make_async_remote_copy(
            src_ref=all_ref.at[place],
            dst_ref=all_ref.at[place],
            send_sem=send_sem.at[distance, at],
            recv_sem=recv_sem.at[distance, at],
            device_id={"seq": flip(me, lowest(distance))},
        )

    sent = []

    def hand_on(distance, at):
        owner = flip(me, distance) * local_req + at
        if distance:
            message(distance, owner, at).wait_recv()
        bits = one_bits(lowest(distance) if distance else count)
        for bit in bits[1:] + bits[:1]:
            copy = message(distance | bit, owner, at)
            copy.start()
            sent.append(copy)

    for at in range(local_req):
        hand_on(0, at)
    local_kv = key_ref.shape[1] // 128
    per_kv = heads // local_kv
    tokens = hidden_ref.shape[0]

    def keys_work():
        loads[2].wait()
        key = jnp.dot(normed, w_key[...], preferred_element_type=jnp.float32)
        for at in range(local_kv):
            cols = slice(at * 128, (at + 1) * 128)
            key_ref[:, cols] = rotated(key[:, cols], row(1))

    def values_work():
        loads[3].wait()
        value_ref[...] = jnp.dot(
            normed, w_value[...], preferred_element_type=jnp.float32
        ).astype(jnp.bfloat16)
        gate_ref[...] = jax.nn.sigmoid(
            lax.dot_general(
                normed,
                small_ref[16 : 16 + heads, :].astype(jnp.bfloat16),
                (((1,), (1,)), ((), ())),
                preferred_element_type=jnp.float32,
            )
        )
        tree_lse_ref[...] = jnp.zeros(tree_lse_ref.shape, jnp.float32)

    def tree_work(at):
        cols = slice(at * 128, (at + 1) * 128)
        stacked = jnp.concatenate(queries[at * per_kv : (at + 1) * per_kv], axis=0)
        scores = (
            lax.dot_general(
                stacked,
                key_ref[:, cols],
                (((1,), (1,)), ((), ())),
                preferred_element_type=jnp.float32,
            )
            * score_scale
        )
        seen = jnp.concatenate([seen_ref[...]] * per_kv, axis=0) > 0.5
        scores = jnp.where(seen, scores, NEGATIVE)
        top = jnp.max(scores, axis=1, keepdims=True)
        weights = jnp.where(seen, jnp.exp(scores - top), 0.0)
        total = jnp.sum(weights, axis=1, keepdims=True)
        mixed = (
            jnp.dot(
                weights.astype(jnp.bfloat16), value_ref[:, cols], preferred_element_type=jnp.float32
            )
            / total
        )
        lse = top + jnp.log(total)
        for sub in range(per_kv):
            head = at * per_kv + sub
            part = slice(sub * tokens, (sub + 1) * tokens)
            tree_ref[:, head * 128 : (head + 1) * 128] = mixed[part]
            column = sub * local_kv + at
            tree_lse_ref[:, column : column + 1] = lse[part]

    pieces = 8
    slots = keys_ref.shape[0] // pieces

    def apart(source, which):
        stage[...] = source[which * slots * local_kv : (which + 1) * slots * local_kv, :].astype(jnp.float32)
        return [stage[pl.ds(at, slots, stride=local_kv), :] for at in range(local_kv)]

    def keys_apart(which):
        if which == 0:
            loads[4].wait()
        for at, part in enumerate(apart(raw_keys, which)):
            keys_ref[which * slots : (which + 1) * slots, at * 128 : (at + 1) * 128] = part.astype(jnp.bfloat16)

    def values_apart(which):
        if which == 0:
            loads[5].wait()
        for at, part in enumerate(apart(raw_values, which)):
            turned_ref[at * 128 : (at + 1) * 128, which * slots : (which + 1) * slots] = jnp.transpose(
                part
            ).astype(jnp.bfloat16)

    keys_work()
    values_work()
    work = [functools.partial(keys_apart, which) for which in range(pieces)]
    work += [functools.partial(values_apart, which) for which in range(pieces)]
    work += [functools.partial(tree_work, at) for at in range(local_kv)]
    order = sorted(range(2, count, 2), key=lambda d: (-lowest(d), d))
    for distance in order:
        for at in range(local_req):
            hand_on(distance, at)
            if work:
                work.pop(0)()
    for rest in work:
        rest()
    for distance in range(1, count, 2):
        for at in range(local_req):
            hand_on(distance, at)
    for copy in wide_sent + sent:
        copy.wait_send()


def layer_front(
    hidden,
    small,
    w_query,
    w_key,
    w_value,
    cache_keys,
    cache_values,
    count,
    kv_count,
    tree,
    score_scale,
):
    tokens = hidden.shape[0]
    width = w_query.shape[1]
    local_kv = w_key.shape[1] // 128
    slots = cache_keys.shape[0] // local_kv
    vmem = pl.BlockSpec(memory_space=pltpu.VMEM)
    hbm = pl.BlockSpec(memory_space=pltpu.HBM)
    return pl.pallas_call(
        functools.partial(layer_kernel, count, kv_count, tree, score_scale),
        out_shape=(
            jax.ShapeDtypeStruct((count * tokens // tree, tree, width), jnp.bfloat16),
            jax.ShapeDtypeStruct((tokens, w_key.shape[1]), jnp.bfloat16),
            jax.ShapeDtypeStruct((tokens, w_value.shape[1]), jnp.bfloat16),
            jax.ShapeDtypeStruct((tokens, width), jnp.float32),
            jax.ShapeDtypeStruct((tokens, 128), jnp.float32),
            jax.ShapeDtypeStruct((tokens, width // 128), jnp.float32),
            jax.ShapeDtypeStruct((tokens, tokens), jnp.bfloat16),
            jax.ShapeDtypeStruct((slots, local_kv * 128), jnp.bfloat16),
            jax.ShapeDtypeStruct((local_kv * 128, slots), jnp.bfloat16),
        ),
        in_specs=[hbm, vmem] + [hbm] * 5,
        out_specs=(vmem,) * 9,
        scratch_shapes=[
            pltpu.VMEM((kv_count,) + hidden.shape, hidden.dtype),
            pltpu.VMEM(w_query.shape, w_query.dtype),
            pltpu.VMEM(w_key.shape, w_key.dtype),
            pltpu.VMEM(w_value.shape, w_value.dtype),
            pltpu.VMEM(cache_keys.shape, jnp.bfloat16),
            pltpu.VMEM(cache_values.shape, jnp.bfloat16),
            pltpu.VMEM((cache_keys.shape[0] // 8, 128), jnp.float32),
            pltpu.VMEM((tokens, 128), jnp.float32),
            pltpu.VMEM((tokens, 128), jnp.float32),
            pltpu.VMEM((tokens, tokens), jnp.float32),
            pltpu.SemaphoreType.DMA((6,)),
            pltpu.SemaphoreType.DMA((kv_count,)),
            pltpu.SemaphoreType.DMA((kv_count,)),
            pltpu.SemaphoreType.DMA((count, tokens // tree)),
            pltpu.SemaphoreType.DMA((count, tokens // tree)),
        ],
        compiler_params=pltpu.CompilerParams(
            collective_id=0, has_side_effects=True, vmem_limit_bytes=FRONT_VMEM
        ),
        name="layer_front",
    )(
        hidden,
        small,
        w_query,
        w_key,
        w_value,
        cache_keys,
        cache_values,
    )


def merge_order(count):
    begin, free = {}, {}
    for distance in range(count - 2, 0, -2):
        bit = lowest(distance)
        ready = max([begin[distance | low] + 2 for low in one_bits(bit)[1:]], default=0)
        begin[distance] = max(ready, free.get(bit, 0))
        free[bit] = begin[distance] + 1
    return sorted(begin, key=lambda distance: (begin[distance], -distance))


def merge_kernel(
    count,
    kv_count,
    per_kv,
    part_ref,
    lse_ref,
    tree_ref,
    tree_lse_ref,
    gate_ref,
    w_out_ref,
    hidden_ref,
    out_ref,
    got,
    got_lse,
    held,
    held_lse,
    w_out,
    attended,
    outgoing,
    arrived,
    send_sem,
    recv_sem,
    load_sem,
    out_send,
    out_recv,
    pair_lse,
    pair_sem,
):
    me = lax.axis_index("seq")
    kv = lax.axis_index("kv")
    requests, rows, _ = part_ref.shape
    local_req = requests // count
    heads = part_ref.shape[2] // 128
    load = pltpu.make_async_copy(w_out_ref, w_out, load_sem)
    load.start()
    greet(me, count, kv, kv_count)

    def messages(distance, at):
        owner = flip(me, distance) * local_req + at
        if distance % 2:
            sources = (part_ref.at[owner],)
        else:
            sources = (held.at[distance // 2, at], held_lse.at[distance // 2, at])
        return [
            pltpu.make_async_remote_copy(
                src_ref=source,
                dst_ref=target.at[distance, at],
                send_sem=send_sem.at[which, distance, at],
                recv_sem=recv_sem.at[which, distance, at],
                device_id={"seq": flip(me, lowest(distance))},
            )
            for which, (source, target) in enumerate(zip(sources, (got, got_lse)))
        ]

    sent = []

    def send(distance, at):
        for copy in messages(distance, at):
            copy.start()
            sent.append(copy)

    def combined(distance, at):
        owner = flip(me, distance) * local_req + at
        incoming = [distance | bit for bit in one_bits(lowest(distance) if distance else count)]
        for message in incoming:
            for copy in messages(message, at):
                copy.wait_recv()
        levels = [lse_ref[owner]] + [
            pair_lse[owner] if message % 2 else got_lse[message, at] for message in incoming
        ]
        own = slice(at * rows, (at + 1) * rows)
        if not distance:
            turned = jnp.transpose(tree_lse_ref[own, :])[:8]
            levels.append(jnp.concatenate([turned] * (128 // rows), axis=1))
        top = functools.reduce(jnp.maximum, levels)
        shares = [jnp.exp(level - top) for level in levels]
        total = functools.reduce(jnp.add, shares)
        inverse = 1.0 / total
        shares = [jnp.transpose(share * inverse)[:rows] for share in shares]
        if distance:
            held_lse[distance // 2, at] = top + jnp.log(total)
        for head in range(heads):
            cols = slice(head * 128, (head + 1) * 128)
            place = head % per_kv * (heads // per_kv) + head // per_kv
            pieces = [part_ref[owner, :, cols]] + [got[message, at, :, cols] for message in incoming]
            if not distance:
                pieces.append(tree_ref[own, cols])
            mixed = functools.reduce(
                jnp.add,
                [
                    piece.astype(jnp.float32) * share[:, place : place + 1]
                    for piece, share in zip(pieces, shares)
                ],
            )
            if distance:
                held[distance // 2, at, :, cols] = mixed.astype(held.dtype)
            else:
                attended[own, cols] = (mixed * gate_ref[own, head : head + 1]).astype(jnp.bfloat16)

    all_lse = pltpu.make_async_remote_copy(
        src_ref=lse_ref,
        dst_ref=pair_lse,
        send_sem=pair_sem.at[0],
        recv_sem=pair_sem.at[1],
        device_id={"seq": flip(me, 1)},
    )
    all_lse.start()
    for distance in sorted(range(1, count, 2), reverse=True):
        for at in range(local_req):
            send(distance, at)
    all_lse.wait()
    for distance in merge_order(count):
        for at in range(local_req):
            combined(distance, at)
            send(distance, at)
    width = out_ref.shape[1]

    def projected(target, at):
        cols = pl.ds(pl.multiple_of(target * width, 128), width)
        return jnp.dot(
            attended[at * rows : (at + 1) * rows, :], w_out[:, cols], preferred_element_type=jnp.float32
        )

    def out_message(hop, at):
        return pltpu.make_async_remote_copy(
            src_ref=outgoing.at[hop, at],
            dst_ref=arrived.at[hop, at],
            send_sem=out_send.at[hop, at],
            recv_sem=out_recv.at[hop, at],
            device_id={"kv": (kv + hop) % kv_count},
        )

    totals = []
    for at in range(local_req):
        combined(0, at)
        if not at:
            load.wait()
        for hop in range(1, kv_count):
            outgoing[hop, at] = projected((kv + hop) % kv_count, at).astype(jnp.bfloat16)
            copy = out_message(hop, at)
            copy.start()
            sent.append(copy)
        totals.append(projected(kv, at))
    for at in range(local_req):
        total = totals[at]
        own = slice(at * rows, (at + 1) * rows)
        for hop in range(1, kv_count):
            out_message(hop, at).wait_recv()
            total = total + arrived[hop, at].astype(jnp.float32)
        out_ref[own, :] = (total + hidden_ref[own, :].astype(jnp.float32)).astype(jnp.bfloat16)
    for copy in sent:
        copy.wait_send()


def merge_parts(parts, lse, tree_mix, tree_lse, gate, w_out, hidden, count, kv_count, per_kv):
    requests, rows, width = parts.shape
    local_req = requests // count
    half = max(1, count // 2)
    vmem = pl.BlockSpec(memory_space=pltpu.VMEM)
    crossing = (kv_count, local_req, rows, hidden.shape[1])
    return pl.pallas_call(
        functools.partial(merge_kernel, count, kv_count, per_kv),
        out_shape=jax.ShapeDtypeStruct(hidden.shape, jnp.bfloat16),
        in_specs=[vmem] * 5 + [pl.BlockSpec(memory_space=pltpu.HBM), vmem],
        out_specs=vmem,
        scratch_shapes=[
            pltpu.VMEM((count, local_req, rows, width), parts.dtype),
            pltpu.VMEM((count, local_req) + lse.shape[1:], jnp.float32),
            pltpu.VMEM((half, local_req, rows, width), parts.dtype),
            pltpu.VMEM((half, local_req) + lse.shape[1:], jnp.float32),
            pltpu.VMEM(w_out.shape, w_out.dtype),
            pltpu.VMEM((local_req * rows, width), jnp.bfloat16),
            pltpu.VMEM(crossing, jnp.bfloat16),
            pltpu.VMEM(crossing, jnp.bfloat16),
            pltpu.SemaphoreType.DMA((2, count, local_req)),
            pltpu.SemaphoreType.DMA((2, count, local_req)),
            pltpu.SemaphoreType.DMA,
            pltpu.SemaphoreType.DMA((kv_count, local_req)),
            pltpu.SemaphoreType.DMA((kv_count, local_req)),
            pltpu.VMEM(lse.shape, jnp.float32),
            pltpu.SemaphoreType.DMA((2,)),
        ],
        compiler_params=pltpu.CompilerParams(
            collective_id=1, has_side_effects=True, vmem_limit_bytes=48 * 2**20
        ),
        name="merge_parts",
    )(parts, lse, tree_mix, tree_lse, gate, w_out, hidden)


def pool_kernel(
    per_kv,
    block,
    own_block,
    score_scale,
    prefix_ref,
    own_ref,
    group_ref,
    q_ref,
    k_ref,
    vt_ref,
    select_ref,
    key_new_ref,
    value_new_ref,
    o_ref,
    lse_ref,
    accepted_keys_ref,
    accepted_values_ref,
    member_ref,
    picked_keys,
    picked_values,
    shared_q,
    shared_top,
    shared_sum,
    shared_mix,
    own_q,
    own_top,
    own_sum,
    own_mix,
    score_ref,
    peak_ref,
    picked_sem,
):
    requests, tree, width = q_ref.shape
    groups = prefix_ref.shape[0]
    pool, kv_width = k_ref.shape
    local_kv = kv_width // 128
    heads = local_kv * per_kv
    per_group = requests // groups
    rows = per_kv * per_group * tree
    part = min(256, block)
    base_two = score_scale / math.log(2.0)
    base = lax.axis_index("seq") * pool
    picked = select_ref[...]
    picked_keys[...] = jnp.dot(picked, key_new_ref[...], preferred_element_type=jnp.float32).astype(jnp.bfloat16)
    picked_values[...] = jnp.dot(picked, value_new_ref[...], preferred_element_type=jnp.float32).astype(
        jnp.bfloat16
    )
    copies = [
        pltpu.make_async_copy(picked_keys, accepted_keys_ref, picked_sem.at[0]),
        pltpu.make_async_copy(picked_values, accepted_values_ref, picked_sem.at[1]),
    ]
    for copy in copies:
        copy.start()
    o_ref[...] = jnp.zeros_like(o_ref)
    lse_ref[...] = jnp.full(lse_ref.shape, NEGATIVE, jnp.float32)

    def put_lse(owner, levels):
        wide = jnp.concatenate([levels] * (128 // tree), axis=1)
        if heads < 8:
            wide = jnp.concatenate([wide] * (8 // heads), axis=0)
        lse_ref[owner] = wide

    def bounds(start, length):
        return jnp.clip(start - base, 0, pool), jnp.clip(start + length - base, 0, pool)

    def find_members(group):
        def find(request, found):
            member_ref[found] = request
            return found + (group_ref[request] == group).astype(jnp.int32)

        lax.fori_loop(0, requests, find, 0)
        return [member_ref[at] for at in range(per_group)]

    def shared_part(group, first, last):
        members = find_members(group)
        for kv in range(local_kv):
            for sub in range(per_kv):
                head = kv * per_kv + sub
                for at, owner in enumerate(members):
                    place = sub * per_group + at
                    shared_q[kv, place * tree : (place + 1) * tree, :] = q_ref[
                        owner, :, head * 128 : (head + 1) * 128
                    ]
        shared_top[...] = jnp.full(shared_top.shape, NEGATIVE, jnp.float32)
        shared_sum[...] = jnp.zeros_like(shared_sum)
        shared_mix[...] = jnp.zeros_like(shared_mix)
        first_step = first // block
        final_step = (last + block - 1) // block - 1

        def scored(start, kv, piece):
            low = pl.multiple_of(start + piece * part, part)
            slots = low + lax.broadcasted_iota(jnp.int32, (part, 128), 0)
            bias = jnp.where((slots >= first) & (slots < last), 0.0, NEGATIVE)
            bias = jnp.concatenate([bias] * (rows // 128), axis=1)
            raw = (
                lax.dot_general(
                    k_ref[pl.ds(low, part), kv * 128 : (kv + 1) * 128],
                    shared_q[kv],
                    (((1,), (1,)), ((), ())),
                    preferred_element_type=jnp.float32,
                )
                + bias
            )
            score_ref[kv % 2, piece * part : (piece + 1) * part, :rows] = raw
            return jnp.max(raw, axis=0, keepdims=True)

        peaks = [scored(first_step * block, 0, piece) for piece in range(block // part)]
        peak_ref[0:1, :rows] = functools.reduce(jnp.maximum, peaks)

        def visit(step, unused):
            start = step * block
            later = jnp.minimum(step + 1, final_step) * block
            for kv in range(local_kv):
                next_kv = (kv + 1) % local_kv
                next_start = later if next_kv == 0 else start
                slot = kv % 2
                old_top = shared_top[kv : kv + 1, :]
                top = jnp.maximum(old_top, peak_ref[slot : slot + 1, :rows])
                factor = jnp.exp2((old_top - top) * base_two)
                shared_top[kv : kv + 1, :] = top
                total = shared_sum[kv : kv + 1, :] * factor
                mixed = shared_mix[kv] * factor
                peaks = []
                for piece in range(block // part):
                    peaks.append(scored(next_start, next_kv, piece))
                    weights = jnp.exp2(
                        (score_ref[slot, piece * part : (piece + 1) * part, :rows] - top) * base_two
                    )
                    total = total + jnp.sum(weights, axis=0, keepdims=True)
                    low = pl.multiple_of(start + piece * part, part)
                    mixed = mixed + jnp.dot(
                        vt_ref[kv * 128 : (kv + 1) * 128, pl.ds(low, part)],
                        weights.astype(jnp.bfloat16),
                        preferred_element_type=jnp.float32,
                    )
                peak_ref[1 - slot : 2 - slot, :rows] = functools.reduce(jnp.maximum, peaks)
                shared_sum[kv : kv + 1, :] = total
                shared_mix[kv] = mixed
            return unused

        lax.fori_loop(first_step, final_step + 1, visit, 0)
        levels = shared_top[...] * score_scale + jnp.log(shared_sum[...])
        for kv in range(local_kv):
            mixed = jnp.transpose(shared_mix[kv] / shared_sum[kv : kv + 1, :]).astype(o_ref.dtype)
            for sub in range(per_kv):
                head = kv * per_kv + sub
                for at, owner in enumerate(members):
                    place = sub * per_group + at
                    o_ref[owner, :, head * 128 : (head + 1) * 128] = mixed[place * tree : (place + 1) * tree]
        for at, owner in enumerate(members):
            put_lse(
                owner,
                jnp.concatenate(
                    [
                        levels[:, (sub * per_group + at) * tree : (sub * per_group + at + 1) * tree]
                        for sub in range(per_kv)
                    ],
                    axis=0,
                ),
            )

    lanes = heads * tree
    blocks = pool // own_block

    def own_parts(start):
        own_q[...] = jnp.zeros_like(own_q)

        def seek(request, found):
            owner, begin = found
            passed = (owner == request) & (begin + own_ref[request] <= base)
            return (
                owner + passed.astype(jnp.int32),
                begin + jnp.where(passed, own_ref[request], 0),
            )

        owner, begin = lax.fori_loop(0, requests - 1, seek, (0, start))

        def stop_of(owner, begin):
            return begin + own_ref[owner] - base

        def scored(step, slot, owner, stop):
            other = jnp.minimum(owner + 1, requests - 1)
            for which, request in enumerate((owner, other)):
                for head in range(heads):
                    cols = slice(head // per_kv * 128, (head // per_kv + 1) * 128)
                    low = which * lanes + head * tree
                    own_q[slot, low : low + tree, cols] = q_ref[request, :, head * 128 : (head + 1) * 128]
            low = pl.multiple_of(step * own_block, own_block)
            slots = low + lax.broadcasted_iota(jnp.int32, (own_block, 128), 0)
            before = jnp.where(slots < stop, 0.0, NEGATIVE)
            after = jnp.where(slots < stop, NEGATIVE, 0.0)
            bias = jnp.concatenate([before] * (lanes // 128) + [after] * (lanes // 128), axis=1)
            raw = (
                lax.dot_general(
                    k_ref[pl.ds(low, own_block), :],
                    own_q[slot],
                    (((1,), (1,)), ((), ())),
                    preferred_element_type=jnp.float32,
                )
                + bias
            )
            score_ref[slot, :own_block, : 2 * lanes] = raw
            peak_ref[pl.ds(slot, 1), : 2 * lanes] = jnp.max(raw, axis=0, keepdims=True)

        def finish(owner):
            levels = own_top[...] * score_scale + jnp.log(own_sum[...])
            mixed = jnp.transpose(own_mix[...] / own_sum[...]).astype(o_ref.dtype)
            for head in range(heads):
                o_ref[owner, :, head * 128 : (head + 1) * 128] = mixed[head * tree : (head + 1) * tree]
            put_lse(
                owner,
                jnp.concatenate(
                    [
                        levels[:, (kv * per_kv + sub) * tree : (kv * per_kv + sub + 1) * tree]
                        for sub in range(per_kv)
                        for kv in range(local_kv)
                    ],
                    axis=0,
                ),
            )

        scored(0, 0, owner, stop_of(owner, begin))
        own_top[...] = jnp.full(own_top.shape, NEGATIVE, jnp.float32)
        own_sum[...] = jnp.zeros_like(own_sum)
        own_mix[...] = jnp.zeros_like(own_mix)

        def visit(step, at):
            owner, begin = at
            slot = step % 2
            ended = stop_of(owner, begin) <= (step + 1) * own_block
            next_owner = jnp.where(ended, jnp.minimum(owner + 1, requests - 1), owner)
            next_begin = jnp.where(ended, begin + own_ref[owner], begin)
            scored(jnp.minimum(step + 1, blocks - 1), 1 - slot, next_owner, stop_of(next_owner, next_begin))
            peak = peak_ref[pl.ds(slot, 1), : 2 * lanes]
            old_top = own_top[...]
            mine = jnp.maximum(old_top, peak[:, :lanes])
            top = jnp.concatenate([mine, peak[:, lanes:]], axis=1)
            factor = jnp.exp2((old_top - mine) * base_two)
            weights = jnp.exp2((score_ref[slot, :own_block, : 2 * lanes] - top) * base_two)
            total = jnp.sum(weights, axis=0, keepdims=True)
            low = pl.multiple_of(step * own_block, own_block)
            whole = jnp.dot(
                vt_ref[:, pl.ds(low, own_block)],
                weights.astype(jnp.bfloat16),
                preferred_element_type=jnp.float32,
            )
            which = lax.broadcasted_iota(jnp.int32, (128, 2 * lanes), 1) // (per_kv * tree) % local_kv
            mixed = whole[:128]
            for kv in range(1, local_kv):
                mixed = jnp.where(which == kv, whole[kv * 128 : (kv + 1) * 128], mixed)
            own_top[...] = mine
            own_sum[...] = own_sum[...] * factor + total[:, :lanes]
            own_mix[...] = own_mix[...] * factor + mixed[:, :lanes]

            @pl.when(ended)
            def _():
                finish(owner)
                own_top[...] = peak[:, lanes:]
                own_sum[...] = total[:, lanes:]
                own_mix[...] = mixed[:, lanes:]

            return next_owner, next_begin

        owner, begin = lax.fori_loop(0, blocks, visit, (owner, begin))

        @pl.when(begin < base + pool)
        def _():
            finish(owner)

    def group_step(group, start):
        first, last = bounds(start, prefix_ref[group])

        @pl.when(last > first)
        def _():
            shared_part(group, first, last)

        return start + prefix_ref[group]

    own_start = lax.fori_loop(0, groups, group_step, 0)

    @pl.when(base + pool > own_start)
    def _():
        own_parts(own_start)

    for copy in copies:
        copy.wait()


def pool_attention(
    prefix_len, own_len, request_group, query, keys, turned, select, key_new, value_new, per_kv, score_scale
):
    requests, tree, width = query.shape
    pool, kv_width = keys.shape
    local_kv = kv_width // 128
    heads = local_kv * per_kv
    rows = per_kv * (requests // prefix_len.shape[0]) * tree
    lanes = heads * tree
    vmem = pl.BlockSpec(memory_space=pltpu.VMEM)
    smem = pl.BlockSpec(memory_space=pltpu.SMEM)
    hbm = pl.BlockSpec(memory_space=pltpu.HBM)
    return pl.pallas_call(
        functools.partial(pool_kernel, per_kv, min(512, pool), min(256, pool), score_scale),
        out_shape=(
            jax.ShapeDtypeStruct(query.shape, jnp.bfloat16),
            jax.ShapeDtypeStruct((requests, 8, 128), jnp.float32),
            jax.ShapeDtypeStruct(key_new.shape, jnp.bfloat16),
            jax.ShapeDtypeStruct(value_new.shape, jnp.bfloat16),
        ),
        in_specs=[smem] * 3 + [vmem] * 6,
        out_specs=(vmem, vmem, hbm, hbm),
        scratch_shapes=[
            pltpu.SMEM((requests + 1,), jnp.int32),
            pltpu.VMEM(key_new.shape, jnp.bfloat16),
            pltpu.VMEM(value_new.shape, jnp.bfloat16),
            pltpu.VMEM((local_kv, rows, 128), jnp.bfloat16),
            pltpu.VMEM((local_kv, rows), jnp.float32),
            pltpu.VMEM((local_kv, rows), jnp.float32),
            pltpu.VMEM((local_kv, 128, rows), jnp.float32),
            pltpu.VMEM((2, 2 * lanes, kv_width), jnp.bfloat16),
            pltpu.VMEM((1, lanes), jnp.float32),
            pltpu.VMEM((1, lanes), jnp.float32),
            pltpu.VMEM((128, lanes), jnp.float32),
            pltpu.VMEM((2, 512, max(rows, 2 * lanes)), jnp.float32),
            pltpu.VMEM((2, max(rows, 2 * lanes)), jnp.float32),
            pltpu.SemaphoreType.DMA((2,)),
        ],
        compiler_params=pltpu.CompilerParams(vmem_limit_bytes=40 * 2**20),
        name="pool_attention",
    )(prefix_len, own_len, request_group, query, keys, turned, select, key_new, value_new)


def body(
    hidden,
    in_gain,
    w_query,
    key_projection_weight,
    value_projection_weight,
    w_gate,
    w_out,
    q_gain,
    k_gain,
    cache_keys,
    pooled_cache_values,
    prefix_len,
    own_len,
    request_group,
    parents,
    accepted_leaf,
):
    local_req, tree = parents.shape
    requests = own_len.shape[0]
    head_width = q_gain.shape[0]
    local_heads = w_gate.shape[1]
    local_kv = key_projection_weight.shape[1] // head_width
    per_kv = local_heads // local_kv
    local_tok = hidden.shape[0]
    pool_dev = cache_keys.shape[0]
    score_scale = 1.0 / math.sqrt(head_width)
    seq_count = requests // local_req
    kv_count = in_gain.shape[0] // hidden.shape[1]
    half = np.exp(np.arange(head_width // 2) * (-2.0 * math.log(ROPE_BASE) / head_width))
    freqs = np.concatenate([half, half]).astype(np.float32)

    lines = [in_gain[None], q_gain[None], k_gain[None], jnp.asarray(freqs)[None]]
    lines += [prefix_len[None], own_len[None], request_group[None], accepted_leaf[None], parents]
    gate_top = 16
    depth = gate_top + local_heads + -local_heads % 8
    sums = {}
    top = 0
    for values in lines + [w_gate.T]:
        rows, lanes = values.shape
        low = gate_top if values.dtype == jnp.bfloat16 else top
        edges = ((low, depth - low - rows, 0), (0, in_gain.shape[0] - lanes, 0))
        padded = lax.pad(values, jnp.zeros((), values.dtype), edges)
        sums[values.dtype] = sums[values.dtype] + padded if values.dtype in sums else padded
        top += rows
    small = functools.reduce(jnp.add, [total.astype(jnp.float32) for total in sums.values()])
    gathered, key_new, value_new, tree_mix, tree_lse, gate, select, keys, turned = layer_front(
        hidden,
        small,
        w_query,
        key_projection_weight,
        value_projection_weight,
        cache_keys.reshape(pool_dev * local_kv, head_width),
        pooled_cache_values.reshape(pool_dev * local_kv, head_width),
        seq_count,
        kv_count,
        tree,
        score_scale,
    )
    parts, part_lse, accepted_keys, accepted_values = pool_attention(
        prefix_len,
        own_len,
        request_group,
        gathered,
        keys,
        turned,
        select,
        key_new,
        value_new,
        per_kv,
        score_scale,
    )
    layer_out = merge_parts(
        parts, part_lse, tree_mix, tree_lse, gate, w_out, hidden, seq_count, kv_count, per_kv
    )
    return (
        layer_out,
        accepted_keys.reshape(local_req, tree, local_kv * head_width),
        accepted_values.reshape(local_req, tree, local_kv * head_width),
    )


def solution(mesh):
    in_specs = (
        P("seq", "kv"),
        P(),
        P(None, "kv"),
        P(None, "kv"),
        P(None, "kv"),
        P(None, "kv"),
        P("kv", None),
        P(),
        P(),
        P("seq", "kv", None),
        P("seq", "kv", None),
        P(),
        P(),
        P(),
        P("seq", None),
        P("seq"),
    )
    out_specs = (P("seq", "kv"), P("seq", None, "kv"), P("seq", None, "kv"))
    return jax.shard_map(body, mesh=mesh, in_specs=in_specs, out_specs=out_specs, check_vma=False)
```

```python
import functools
import math

import jax
import jax.numpy as jnp
import numpy as np
from jax import lax
from jax.experimental import pallas as pl
from jax.experimental.pallas import tpu as pltpu
from jax.sharding import PartitionSpec as P

EPSILON = 1e-06
ROPE_BASE = 1000000.0
NEGATIVE = -1e30
EARLY = 2
HALVES = 2
FRONT_VMEM = 47 * 2**20


def rms_scale(values, scales):
    mean_square = jnp.mean(values * values, axis=-1, keepdims=True)
    return values * lax.rsqrt(mean_square + EPSILON) * scales


def rope_angles(positions, freqs):
    angles = positions * freqs
    turns = jnp.floor(angles * (2.0 / math.pi) + 0.5)
    rest = angles - turns * 1.5703125
    rest = rest - turns * 4.837512969970703125e-4
    rest = rest - turns * 7.549789954891882e-8
    square = rest * rest
    sine = rest + rest * square * (
        -1.6666654611e-1 + square * (8.3321608736e-3 - square * 1.9515295891e-4)
    )
    cosine = (
        1.0
        - 0.5 * square
        + square * square * (4.166664568298827e-2 + square * (-1.388731625493765e-3 + square * 2.443315711809948e-5))
    )
    quarter = turns.astype(jnp.int32) & 3
    swapped = (quarter & 1) == 1
    cos_out = jnp.where(swapped, sine, cosine)
    sin_out = jnp.where(swapped, cosine, sine)
    cos_out = jnp.where((quarter == 1) | (quarter == 2), -cos_out, cos_out)
    sin_out = jnp.where(quarter >= 2, -sin_out, sin_out)
    return cos_out, sin_out


def tree_tables(parents, leaves, contexts, freqs):
    local_req, width = parents.shape
    tokens = local_req * width
    rows = lax.broadcasted_iota(jnp.int32, (tokens, tokens), 0)
    cols = lax.broadcasted_iota(jnp.int32, (tokens, tokens), 1)
    above = jnp.concatenate(
        [parents[at : at + 1, :] + at * width for at in range(local_req)], axis=1
    )
    reached = jnp.where((above == rows) | (rows == cols), 1.0, 0.0)
    for squaring in range(max(1, (width - 1).bit_length())):
        half = reached.astype(jnp.bfloat16)
        reached = jnp.minimum(jnp.dot(half, half, preferred_element_type=jnp.float32), 1.0)
    reach = jnp.transpose(reached)
    depth_across = jnp.sum(reached, axis=0, keepdims=True) - 1.0
    depth_down = jnp.sum(reach, axis=1, keepdims=True) - 1.0
    which = lax.broadcasted_iota(jnp.int32, (tokens, 1), 0) // width
    context = jnp.zeros((tokens, 1), jnp.float32)
    is_leaf = rows < 0
    for at in range(local_req):
        context = jnp.where(which == at, contexts[at], context)
        is_leaf = is_leaf | (rows == leaves[:, at : at + 1] + at * width)
    on_path = jnp.sum(jnp.where(is_leaf, reach, 0.0), axis=0, keepdims=True)
    level = (rows % width).astype(jnp.float32)
    picked = (depth_across == level) & (rows // width == cols // width)
    select = jnp.where(picked, jnp.broadcast_to(on_path, (tokens, tokens)), 0.0)
    cosine, sine = rope_angles(context + depth_down, freqs)
    lanes = lax.broadcasted_iota(jnp.int32, cosine.shape, 1)
    sine = jnp.where(lanes < cosine.shape[1] // 2, -sine, sine)
    return reach, select, cosine, sine


def lowest(distance):
    return distance & -distance


def flip(index, distance):
    out = index
    bit = 1
    while bit <= distance:
        if distance & bit:
            out = out + bit * (1 - 2 * ((index // bit) % 2))
        bit *= 2
    return out


def one_bits(count):
    bits = []
    bit = 1
    while bit < count:
        bits.append(bit)
        bit *= 2
    return bits


def greet(me, count, kv, kv_count):
    barrier = pltpu.get_barrier_semaphore()
    bits = one_bits(count)
    for bit in bits:
        pl.semaphore_signal(barrier, inc=1, device_id={"seq": flip(me, bit)})
    for hop in range(1, kv_count):
        pl.semaphore_signal(barrier, inc=1, device_id={"kv": (kv + hop) % kv_count})
    pl.semaphore_wait(barrier, len(bits) + kv_count - 1)


def layer_kernel(
    count,
    kv_count,
    tree,
    score_scale,
    hidden_ref,
    small_ref,
    w_query_ref,
    w_key_ref,
    w_value_ref,
    cache_key_ref,
    cache_value_ref,
    all_ref,
    key_ref,
    value_ref,
    tree_ref,
    tree_lse_ref,
    gate_ref,
    select_ref,
    keys_ref,
    turned_ref,
    wide,
    w_query,
    w_key,
    w_value,
    raw_keys,
    raw_values,
    stage,
    cos_ref,
    sin_ref,
    seen_ref,
    load_sem,
    wide_send,
    wide_recv,
    send_sem,
    recv_sem,
):
    me = lax.axis_index("seq")
    kv = lax.axis_index("kv")
    loads = [
        pltpu.make_async_copy(source, target, load_sem.at[which])
        for which, (source, target) in enumerate(
            [
                (hidden_ref, wide.at[kv]),
                (w_query_ref, w_query),
                (w_key_ref, w_key),
                (w_value_ref, w_value),
                (cache_key_ref, raw_keys),
                (cache_value_ref, raw_values),
            ]
        )
    ]
    for load in loads:
        load.start()
    loads[0].wait()
    greet(me, count, kv, kv_count)

    local_req = hidden_ref.shape[0] // tree

    def wide_message(hop, owner, at):
        own = slice(at * tree, (at + 1) * tree)
        return pltpu.make_async_remote_copy(
            src_ref=wide.at[owner, own],
            dst_ref=wide.at[owner, own],
            send_sem=wide_send.at[hop, at],
            recv_sem=wide_recv.at[hop, at],
            device_id={"kv": (kv + hop) % kv_count},
        )

    wide_sent = [wide_message(hop, kv, at) for at in range(local_req) for hop in range(1, kv_count)]
    for copy in wide_sent:
        copy.start()
    lane = lax.broadcasted_iota(jnp.int32, (1, 128), 1)

    def row(at):
        return small_ref[1 + at : 2 + at, :128]

    def taken(values, index):
        return jnp.sum(jnp.where(lane == index, values, 0.0), axis=1, keepdims=True)

    contexts = [
        taken(row(3), taken(row(5), me * local_req + at).astype(jnp.int32))
        + taken(row(4), me * local_req + at)
        for at in range(local_req)
    ]
    parents = jnp.concatenate([row(7 + at)[:, :tree] for at in range(local_req)], axis=0).astype(jnp.int32)
    reach, select, cosine, sine = tree_tables(parents, row(6).astype(jnp.int32), contexts, row(2))
    seen_ref[...] = reach
    select_ref[...] = select.astype(jnp.bfloat16)
    cos_ref[...] = cosine
    sin_ref[...] = sine
    heads = w_query.shape[1] // 128

    def rotated(values, gain, part):
        values = rms_scale(values, gain)
        return (values * cos_ref[part, :] + pltpu.roll(values, 64, 1) * sin_ref[part, :]).astype(jnp.bfloat16)

    def message(distance, place, at):
        return pltpu.make_async_remote_copy(
            src_ref=all_ref.at[place],
            dst_ref=all_ref.at[place],
            send_sem=send_sem.at[distance, at],
            recv_sem=recv_sem.at[distance, at],
            device_id={"seq": flip(me, lowest(distance))},
        )

    sent = []

    def hand_on(distance, at):
        owner = flip(me, distance) * local_req + at
        if distance:
            message(distance, owner, at).wait_recv()
        bits = one_bits(lowest(distance) if distance else count)
        for bit in bits[1:] + bits[:1]:
            copy = message(distance | bit, owner, at)
            copy.start()
            sent.append(copy)

    normed_parts = []
    query_parts = []
    for at in range(local_req):
        own = slice(at * tree, (at + 1) * tree)
        for hop in range(1, kv_count):
            wide_message(hop, (kv + kv_count - hop) % kv_count, at).wait_recv()
        rows = jnp.concatenate([wide[owner, own] for owner in range(kv_count)], axis=1).astype(jnp.float32)
        mean_square = jnp.mean(rows * rows, axis=-1, keepdims=True)
        inverse = lax.rsqrt(mean_square + EPSILON)
        normed_parts.append((rows * inverse * small_ref[0:1, :]).astype(jnp.bfloat16))
        if not at:
            loads[1].wait()
        query = jnp.dot(normed_parts[at], w_query[...], preferred_element_type=jnp.float32)
        query_parts.append([rotated(query[:, h * 128 : (h + 1) * 128], row(0), own) for h in range(heads)])
        for head in range(heads):
            all_ref[me * local_req + at, :, head * 128 : (head + 1) * 128] = query_parts[at][head]
        hand_on(0, at)
    normed = jnp.concatenate(normed_parts, axis=0)
    queries = [jnp.concatenate([part[head] for part in query_parts], axis=0) for head in range(heads)]
    local_kv = key_ref.shape[1] // 128
    per_kv = heads // local_kv
    tokens = hidden_ref.shape[0]

    def keys_work():
        loads[2].wait()
        key = jnp.dot(normed, w_key[...], preferred_element_type=jnp.float32)
        for at in range(local_kv):
            cols = slice(at * 128, (at + 1) * 128)
            key_ref[:, cols] = rotated(key[:, cols], row(1), slice(0, tokens))

    def values_work():
        loads[3].wait()
        value_ref[...] = jnp.dot(
            normed, w_value[...], preferred_element_type=jnp.float32
        ).astype(jnp.bfloat16)
        gate_ref[...] = jax.nn.sigmoid(
            lax.dot_general(
                normed,
                small_ref[16 : 16 + heads, :].astype(jnp.bfloat16),
                (((1,), (1,)), ((), ())),
                preferred_element_type=jnp.float32,
            )
        )
        tree_lse_ref[...] = jnp.zeros(tree_lse_ref.shape, jnp.float32)

    def tree_work(at):
        cols = slice(at * 128, (at + 1) * 128)
        stacked = jnp.concatenate(queries[at * per_kv : (at + 1) * per_kv], axis=0)
        scores = (
            lax.dot_general(
                stacked,
                key_ref[:, cols],
                (((1,), (1,)), ((), ())),
                preferred_element_type=jnp.float32,
            )
            * score_scale
        )
        seen = jnp.concatenate([seen_ref[...]] * per_kv, axis=0) > 0.5
        scores = jnp.where(seen, scores, NEGATIVE)
        top = jnp.max(scores, axis=1, keepdims=True)
        weights = jnp.where(seen, jnp.exp(scores - top), 0.0)
        total = jnp.sum(weights, axis=1, keepdims=True)
        mixed = (
            jnp.dot(
                weights.astype(jnp.bfloat16), value_ref[:, cols], preferred_element_type=jnp.float32
            )
            / total
        )
        lse = top + jnp.log(total)
        for sub in range(per_kv):
            head = at * per_kv + sub
            part = slice(sub * tokens, (sub + 1) * tokens)
            tree_ref[:, head * 128 : (head + 1) * 128] = mixed[part]
            column = sub * local_kv + at
            tree_lse_ref[:, column : column + 1] = lse[part]

    pieces = 8
    slots = keys_ref.shape[0] // pieces

    def apart(source, which):
        stage[...] = source[which * slots * local_kv : (which + 1) * slots * local_kv, :].astype(jnp.float32)
        return [stage[pl.ds(at, slots, stride=local_kv), :] for at in range(local_kv)]

    def keys_apart(which):
        if which == 0:
            loads[4].wait()
        for at, part in enumerate(apart(raw_keys, which)):
            keys_ref[which * slots : (which + 1) * slots, at * 128 : (at + 1) * 128] = part.astype(jnp.bfloat16)

    def values_apart(which):
        if which == 0:
            loads[5].wait()
        for at, part in enumerate(apart(raw_values, which)):
            turned_ref[at * 128 : (at + 1) * 128, which * slots : (which + 1) * slots] = jnp.transpose(
                part
            ).astype(jnp.bfloat16)

    keys_work()
    values_work()
    work = [functools.partial(keys_apart, which) for which in range(pieces)]
    work += [functools.partial(values_apart, which) for which in range(pieces)]
    work += [functools.partial(tree_work, at) for at in range(local_kv)]
    order = sorted(range(2, count, 2), key=lambda d: (-lowest(d), d))
    for distance in order:
        for at in range(local_req):
            hand_on(distance, at)
            if work:
                work.pop(0)()
    for rest in work:
        rest()
    for distance in range(1, count, 2):
        for at in range(local_req):
            hand_on(distance, at)
    for copy in wide_sent + sent:
        copy.wait_send()


def layer_front(
    hidden,
    small,
    w_query,
    w_key,
    w_value,
    cache_keys,
    cache_values,
    count,
    kv_count,
    tree,
    score_scale,
):
    tokens = hidden.shape[0]
    width = w_query.shape[1]
    local_kv = w_key.shape[1] // 128
    slots = cache_keys.shape[0] // local_kv
    vmem = pl.BlockSpec(memory_space=pltpu.VMEM)
    hbm = pl.BlockSpec(memory_space=pltpu.HBM)
    return pl.pallas_call(
        functools.partial(layer_kernel, count, kv_count, tree, score_scale),
        out_shape=(
            jax.ShapeDtypeStruct((count * tokens // tree, tree, width), jnp.bfloat16),
            jax.ShapeDtypeStruct((tokens, w_key.shape[1]), jnp.bfloat16),
            jax.ShapeDtypeStruct((tokens, w_value.shape[1]), jnp.bfloat16),
            jax.ShapeDtypeStruct((tokens, width), jnp.float32),
            jax.ShapeDtypeStruct((tokens, 128), jnp.float32),
            jax.ShapeDtypeStruct((tokens, width // 128), jnp.float32),
            jax.ShapeDtypeStruct((tokens, tokens), jnp.bfloat16),
            jax.ShapeDtypeStruct((slots, local_kv * 128), jnp.bfloat16),
            jax.ShapeDtypeStruct((local_kv * 128, slots), jnp.bfloat16),
        ),
        in_specs=[hbm, vmem] + [hbm] * 5,
        out_specs=(vmem,) * 9,
        scratch_shapes=[
            pltpu.VMEM((kv_count,) + hidden.shape, hidden.dtype),
            pltpu.VMEM(w_query.shape, w_query.dtype),
            pltpu.VMEM(w_key.shape, w_key.dtype),
            pltpu.VMEM(w_value.shape, w_value.dtype),
            pltpu.VMEM(cache_keys.shape, jnp.bfloat16),
            pltpu.VMEM(cache_values.shape, jnp.bfloat16),
            pltpu.VMEM((cache_keys.shape[0] // 8, 128), jnp.float32),
            pltpu.VMEM((tokens, 128), jnp.float32),
            pltpu.VMEM((tokens, 128), jnp.float32),
            pltpu.VMEM((tokens, tokens), jnp.float32),
            pltpu.SemaphoreType.DMA((6,)),
            pltpu.SemaphoreType.DMA((kv_count, tokens // tree)),
            pltpu.SemaphoreType.DMA((kv_count, tokens // tree)),
            pltpu.SemaphoreType.DMA((count, tokens // tree)),
            pltpu.SemaphoreType.DMA((count, tokens // tree)),
        ],
        compiler_params=pltpu.CompilerParams(
            collective_id=0, has_side_effects=True, vmem_limit_bytes=FRONT_VMEM
        ),
        name="layer_front",
    )(
        hidden,
        small,
        w_query,
        w_key,
        w_value,
        cache_keys,
        cache_values,
    )


def merge_order(count):
    begin, free = {}, {}
    for distance in range(count - 2, 0, -2):
        bit = lowest(distance)
        ready = max([begin[distance | low] + 2 for low in one_bits(bit)[1:]], default=0)
        begin[distance] = max(ready, free.get(bit, 0))
        free[bit] = begin[distance] + 1
    return sorted(begin, key=lambda distance: (begin[distance], -distance))


def merge_kernel(
    count,
    kv_count,
    per_kv,
    part_ref,
    lse_ref,
    tree_ref,
    tree_lse_ref,
    gate_ref,
    w_out_ref,
    hidden_ref,
    out_ref,
    got,
    got_lse,
    held,
    held_lse,
    w_out,
    attended,
    outgoing,
    arrived,
    send_sem,
    recv_sem,
    load_sem,
    out_send,
    out_recv,
    pair_lse,
    pair_sem,
    base_lse,
    base_mix,
    totals,
):
    me = lax.axis_index("seq")
    kv = lax.axis_index("kv")
    requests, rows, _ = part_ref.shape
    local_req = requests // count
    heads = part_ref.shape[2] // 128
    load = pltpu.make_async_copy(w_out_ref, w_out, load_sem)
    load.start()
    greet(me, count, kv, kv_count)

    def messages(distance, at):
        owner = flip(me, distance) * local_req + at
        if distance % 2:
            sources = (part_ref.at[owner],)
        else:
            sources = (held.at[distance // 2, at], held_lse.at[distance // 2, at])
        return [
            pltpu.make_async_remote_copy(
                src_ref=source,
                dst_ref=target.at[distance, at],
                send_sem=send_sem.at[which, distance, at],
                recv_sem=recv_sem.at[which, distance, at],
                device_id={"seq": flip(me, lowest(distance))},
            )
            for which, (source, target) in enumerate(zip(sources, (got, got_lse)))
        ]

    sent = []

    def send(distance, at):
        for copy in messages(distance, at):
            copy.start()
            sent.append(copy)

    def blended(levels, sources):
        top = functools.reduce(jnp.maximum, levels)
        shares = [jnp.exp(level - top) for level in levels]
        total = functools.reduce(jnp.add, shares)
        inverse = 1.0 / total
        shares = [jnp.transpose(share * inverse)[:rows] for share in shares]
        mixed = []
        for head in range(heads):
            cols = slice(head * 128, (head + 1) * 128)
            place = head % per_kv * (heads // per_kv) + head // per_kv
            mixed.append(
                functools.reduce(
                    jnp.add,
                    [
                        source(cols).astype(jnp.float32) * share[:, place : place + 1]
                        for source, share in zip(sources, shares)
                    ],
                )
            )
        return top + jnp.log(total), mixed

    def received(distance, at):
        for copy in messages(distance, at):
            copy.wait_recv()
        owner = flip(me, distance - lowest(distance)) * local_req + at
        level = pair_lse[owner] if distance % 2 else got_lse[distance, at]
        return level, lambda cols: got[distance, at, :, cols]

    def gathered(distance, at, bits):
        owner = flip(me, distance) * local_req + at
        parts = [(lse_ref[owner], lambda cols: part_ref[owner, :, cols])]
        return parts + [received(distance | bit, at) for bit in bits]

    def combined(distance, at):
        level, mixed = blended(*zip(*gathered(distance, at, one_bits(lowest(distance)))))
        held_lse[distance // 2, at] = level
        for head in range(heads):
            held[distance // 2, at, :, head * 128 : (head + 1) * 128] = mixed[head].astype(held.dtype)

    def begun(at):
        own = slice(at * rows, (at + 1) * rows)
        turned = jnp.transpose(tree_lse_ref[own, :])[:8]
        level = jnp.concatenate([turned] * (128 // rows), axis=1)
        parts = gathered(0, at, one_bits(count)[:EARLY]) + [(level, lambda cols: tree_ref[own, cols])]
        level, mixed = blended(*zip(*parts))
        base_lse[at] = level
        for head in range(heads):
            base_mix[at, :, head * 128 : (head + 1) * 128] = mixed[head] * gate_ref[own, head : head + 1]

    def ended(at):
        own = slice(at * rows, (at + 1) * rows)
        parts = [(base_lse[at], lambda cols: base_mix[at, :, cols])]
        for bit in one_bits(count)[EARLY:]:
            level, source = received(bit, at)
            parts.append((level, source))
        top = functools.reduce(jnp.maximum, [level for level, _ in parts])
        shares = [jnp.exp(level - top) for level, _ in parts]
        inverse = 1.0 / functools.reduce(jnp.add, shares)
        shares = [jnp.transpose(share * inverse)[:rows] for share in shares]
        for head in range(heads):
            cols = slice(head * 128, (head + 1) * 128)
            place = head % per_kv * (heads // per_kv) + head // per_kv
            gate = gate_ref[own, head : head + 1]
            mixed = parts[0][1](cols) * shares[0][:, place : place + 1]
            for (_, source), share in zip(parts[1:], shares[1:]):
                mixed = mixed + source(cols).astype(jnp.float32) * (share[:, place : place + 1] * gate)
            attended[own, cols] = mixed.astype(jnp.bfloat16)

    all_lse = pltpu.make_async_remote_copy(
        src_ref=lse_ref,
        dst_ref=pair_lse,
        send_sem=pair_sem.at[0],
        recv_sem=pair_sem.at[1],
        device_id={"seq": flip(me, 1)},
    )
    all_lse.start()
    for distance in sorted(range(1, count, 2), reverse=True):
        for at in range(local_req):
            send(distance, at)
    all_lse.wait()
    for distance in merge_order(count):
        for at in range(local_req):
            combined(distance, at)
            send(distance, at)
    for at in range(local_req):
        begun(at)
    width = out_ref.shape[1]
    half = width // HALVES

    def projected(target, at, which):
        cols = pl.ds(pl.multiple_of(target * width + which * half, 128), half)
        return jnp.dot(
            attended[at * rows : (at + 1) * rows, :], w_out[:, cols], preferred_element_type=jnp.float32
        )

    def out_message(hop, at, which):
        cols = slice(which * half, (which + 1) * half)
        return pltpu.make_async_remote_copy(
            src_ref=outgoing.at[hop, at, :, cols],
            dst_ref=arrived.at[hop, at, :, cols],
            send_sem=out_send.at[hop, at, which],
            recv_sem=out_recv.at[hop, at, which],
            device_id={"kv": (kv + hop) % kv_count},
        )

    load.wait()
    for at in range(local_req):
        ended(at)
        for hop in range(1, kv_count):
            for which in range(HALVES):
                outgoing[hop, at, :, which * half : (which + 1) * half] = projected(
                    (kv + hop) % kv_count, at, which
                ).astype(jnp.bfloat16)
                copy = out_message(hop, at, which)
                copy.start()
                sent.append(copy)
        own = slice(at * rows, (at + 1) * rows)
        for which in range(HALVES):
            cols = slice(which * half, (which + 1) * half)
            totals[own, cols] = projected(kv, at, which) + hidden_ref[own, cols].astype(jnp.float32)
    for at in range(local_req):
        own = slice(at * rows, (at + 1) * rows)
        for which in range(HALVES):
            cols = slice(which * half, (which + 1) * half)
            total = totals[own, cols]
            for hop in range(1, kv_count):
                out_message(hop, at, which).wait_recv()
                total = total + arrived[hop, at, :, cols].astype(jnp.float32)
            out_ref[own, cols] = total.astype(jnp.bfloat16)
    for copy in sent:
        copy.wait_send()


def merge_parts(parts, lse, tree_mix, tree_lse, gate, w_out, hidden, count, kv_count, per_kv):
    requests, rows, width = parts.shape
    local_req = requests // count
    half = max(1, count // 2)
    vmem = pl.BlockSpec(memory_space=pltpu.VMEM)
    crossing = (kv_count, local_req, rows, hidden.shape[1])
    return pl.pallas_call(
        functools.partial(merge_kernel, count, kv_count, per_kv),
        out_shape=jax.ShapeDtypeStruct(hidden.shape, jnp.bfloat16),
        in_specs=[vmem] * 5 + [pl.BlockSpec(memory_space=pltpu.HBM), vmem],
        out_specs=vmem,
        scratch_shapes=[
            pltpu.VMEM((count, local_req, rows, width), parts.dtype),
            pltpu.VMEM((count, local_req) + lse.shape[1:], jnp.float32),
            pltpu.VMEM((half, local_req, rows, width), parts.dtype),
            pltpu.VMEM((half, local_req) + lse.shape[1:], jnp.float32),
            pltpu.VMEM(w_out.shape, w_out.dtype),
            pltpu.VMEM((local_req * rows, width), jnp.bfloat16),
            pltpu.VMEM(crossing, jnp.bfloat16),
            pltpu.VMEM(crossing, jnp.bfloat16),
            pltpu.SemaphoreType.DMA((2, count, local_req)),
            pltpu.SemaphoreType.DMA((2, count, local_req)),
            pltpu.SemaphoreType.DMA,
            pltpu.SemaphoreType.DMA((kv_count, local_req, HALVES)),
            pltpu.SemaphoreType.DMA((kv_count, local_req, HALVES)),
            pltpu.VMEM(lse.shape, jnp.float32),
            pltpu.SemaphoreType.DMA((2,)),
            pltpu.VMEM((local_req,) + lse.shape[1:], jnp.float32),
            pltpu.VMEM((local_req, rows, width), jnp.float32),
            pltpu.VMEM(hidden.shape, jnp.float32),
        ],
        compiler_params=pltpu.CompilerParams(
            collective_id=1, has_side_effects=True, vmem_limit_bytes=48 * 2**20
        ),
        name="merge_parts",
    )(parts, lse, tree_mix, tree_lse, gate, w_out, hidden)


def pool_kernel(
    per_kv,
    block,
    own_block,
    score_scale,
    prefix_ref,
    own_ref,
    group_ref,
    q_ref,
    k_ref,
    vt_ref,
    select_ref,
    key_new_ref,
    value_new_ref,
    o_ref,
    lse_ref,
    accepted_keys_ref,
    accepted_values_ref,
    member_ref,
    picked_keys,
    picked_values,
    shared_q,
    shared_top,
    shared_sum,
    shared_mix,
    own_q,
    own_top,
    own_sum,
    own_mix,
    score_ref,
    peak_ref,
    picked_sem,
):
    requests, tree, width = q_ref.shape
    groups = prefix_ref.shape[0]
    pool, kv_width = k_ref.shape
    local_kv = kv_width // 128
    heads = local_kv * per_kv
    per_group = requests // groups
    rows = per_kv * per_group * tree
    part = min(256, block)
    base_two = score_scale / math.log(2.0)
    base = lax.axis_index("seq") * pool
    picked = select_ref[...]
    picked_keys[...] = jnp.dot(picked, key_new_ref[...], preferred_element_type=jnp.float32).astype(jnp.bfloat16)
    picked_values[...] = jnp.dot(picked, value_new_ref[...], preferred_element_type=jnp.float32).astype(
        jnp.bfloat16
    )
    copies = [
        pltpu.make_async_copy(picked_keys, accepted_keys_ref, picked_sem.at[0]),
        pltpu.make_async_copy(picked_values, accepted_values_ref, picked_sem.at[1]),
    ]
    for copy in copies:
        copy.start()
    o_ref[...] = jnp.zeros_like(o_ref)
    lse_ref[...] = jnp.full(lse_ref.shape, NEGATIVE, jnp.float32)

    def put_lse(owner, levels):
        wide = jnp.concatenate([levels] * (128 // tree), axis=1)
        if heads < 8:
            wide = jnp.concatenate([wide] * (8 // heads), axis=0)
        lse_ref[owner] = wide

    def bounds(start, length):
        return jnp.clip(start - base, 0, pool), jnp.clip(start + length - base, 0, pool)

    def find_members(group):
        def find(request, found):
            member_ref[found] = request
            return found + (group_ref[request] == group).astype(jnp.int32)

        lax.fori_loop(0, requests, find, 0)
        return [member_ref[at] for at in range(per_group)]

    def shared_part(group, first, last):
        members = find_members(group)
        for kv in range(local_kv):
            for sub in range(per_kv):
                head = kv * per_kv + sub
                for at, owner in enumerate(members):
                    place = sub * per_group + at
                    shared_q[kv, place * tree : (place + 1) * tree, :] = q_ref[
                        owner, :, head * 128 : (head + 1) * 128
                    ]
        shared_top[...] = jnp.full(shared_top.shape, NEGATIVE, jnp.float32)
        shared_sum[...] = jnp.zeros_like(shared_sum)
        shared_mix[...] = jnp.zeros_like(shared_mix)
        first_step = first // block
        final_step = (last + block - 1) // block - 1

        def scored(start, kv, piece):
            low = pl.multiple_of(start + piece * part, part)
            slots = low + lax.broadcasted_iota(jnp.int32, (part, 128), 0)
            bias = jnp.where((slots >= first) & (slots < last), 0.0, NEGATIVE)
            bias = jnp.concatenate([bias] * (rows // 128), axis=1)
            raw = (
                lax.dot_general(
                    k_ref[pl.ds(low, part), kv * 128 : (kv + 1) * 128],
                    shared_q[kv],
                    (((1,), (1,)), ((), ())),
                    preferred_element_type=jnp.float32,
                )
                + bias
            )
            score_ref[kv % 2, piece * part : (piece + 1) * part, :rows] = raw
            return jnp.max(raw, axis=0, keepdims=True)

        peaks = [scored(first_step * block, 0, piece) for piece in range(block // part)]
        peak_ref[0:1, :rows] = functools.reduce(jnp.maximum, peaks)

        def visit(step, unused):
            start = step * block
            later = jnp.minimum(step + 1, final_step) * block
            for kv in range(local_kv):
                next_kv = (kv + 1) % local_kv
                next_start = later if next_kv == 0 else start
                slot = kv % 2
                old_top = shared_top[kv : kv + 1, :]
                top = jnp.maximum(old_top, peak_ref[slot : slot + 1, :rows])
                factor = jnp.exp2((old_top - top) * base_two)
                shared_top[kv : kv + 1, :] = top
                total = shared_sum[kv : kv + 1, :] * factor
                mixed = shared_mix[kv] * factor
                peaks = []
                for piece in range(block // part):
                    peaks.append(scored(next_start, next_kv, piece))
                    weights = jnp.exp2(
                        (score_ref[slot, piece * part : (piece + 1) * part, :rows] - top) * base_two
                    )
                    total = total + jnp.sum(weights, axis=0, keepdims=True)
                    low = pl.multiple_of(start + piece * part, part)
                    mixed = mixed + jnp.dot(
                        vt_ref[kv * 128 : (kv + 1) * 128, pl.ds(low, part)],
                        weights.astype(jnp.bfloat16),
                        preferred_element_type=jnp.float32,
                    )
                peak_ref[1 - slot : 2 - slot, :rows] = functools.reduce(jnp.maximum, peaks)
                shared_sum[kv : kv + 1, :] = total
                shared_mix[kv] = mixed
            return unused

        lax.fori_loop(first_step, final_step + 1, visit, 0)
        levels = shared_top[...] * score_scale + jnp.log(shared_sum[...])
        for kv in range(local_kv):
            mixed = jnp.transpose(shared_mix[kv] / shared_sum[kv : kv + 1, :]).astype(o_ref.dtype)
            for sub in range(per_kv):
                head = kv * per_kv + sub
                for at, owner in enumerate(members):
                    place = sub * per_group + at
                    o_ref[owner, :, head * 128 : (head + 1) * 128] = mixed[place * tree : (place + 1) * tree]
        for at, owner in enumerate(members):
            put_lse(
                owner,
                jnp.concatenate(
                    [
                        levels[:, (sub * per_group + at) * tree : (sub * per_group + at + 1) * tree]
                        for sub in range(per_kv)
                    ],
                    axis=0,
                ),
            )

    lanes = heads * tree
    blocks = pool // own_block

    def own_parts(start):
        own_q[...] = jnp.zeros_like(own_q)

        def seek(request, found):
            owner, begin = found
            passed = (owner == request) & (begin + own_ref[request] <= base)
            return (
                owner + passed.astype(jnp.int32),
                begin + jnp.where(passed, own_ref[request], 0),
            )

        owner, begin = lax.fori_loop(0, requests - 1, seek, (0, start))

        def stop_of(owner, begin):
            return begin + own_ref[owner] - base

        def scored(step, slot, owner, stop):
            other = jnp.minimum(owner + 1, requests - 1)
            for which, request in enumerate((owner, other)):
                for head in range(heads):
                    cols = slice(head // per_kv * 128, (head // per_kv + 1) * 128)
                    low = which * lanes + head * tree
                    own_q[slot, low : low + tree, cols] = q_ref[request, :, head * 128 : (head + 1) * 128]
            low = pl.multiple_of(step * own_block, own_block)
            slots = low + lax.broadcasted_iota(jnp.int32, (own_block, 128), 0)
            before = jnp.where(slots < stop, 0.0, NEGATIVE)
            after = jnp.where(slots < stop, NEGATIVE, 0.0)
            bias = jnp.concatenate([before] * (lanes // 128) + [after] * (lanes // 128), axis=1)
            raw = (
                lax.dot_general(
                    k_ref[pl.ds(low, own_block), :],
                    own_q[slot],
                    (((1,), (1,)), ((), ())),
                    preferred_element_type=jnp.float32,
                )
                + bias
            )
            score_ref[slot, :own_block, : 2 * lanes] = raw
            peak_ref[pl.ds(slot, 1), : 2 * lanes] = jnp.max(raw, axis=0, keepdims=True)

        def finish(owner):
            levels = own_top[...] * score_scale + jnp.log(own_sum[...])
            mixed = jnp.transpose(own_mix[...] / own_sum[...]).astype(o_ref.dtype)
            for head in range(heads):
                o_ref[owner, :, head * 128 : (head + 1) * 128] = mixed[head * tree : (head + 1) * tree]
            put_lse(
                owner,
                jnp.concatenate(
                    [
                        levels[:, (kv * per_kv + sub) * tree : (kv * per_kv + sub + 1) * tree]
                        for sub in range(per_kv)
                        for kv in range(local_kv)
                    ],
                    axis=0,
                ),
            )

        scored(0, 0, owner, stop_of(owner, begin))
        own_top[...] = jnp.full(own_top.shape, NEGATIVE, jnp.float32)
        own_sum[...] = jnp.zeros_like(own_sum)
        own_mix[...] = jnp.zeros_like(own_mix)

        def visit(step, at):
            owner, begin = at
            slot = step % 2
            ended = stop_of(owner, begin) <= (step + 1) * own_block
            next_owner = jnp.where(ended, jnp.minimum(owner + 1, requests - 1), owner)
            next_begin = jnp.where(ended, begin + own_ref[owner], begin)
            scored(jnp.minimum(step + 1, blocks - 1), 1 - slot, next_owner, stop_of(next_owner, next_begin))
            peak = peak_ref[pl.ds(slot, 1), : 2 * lanes]
            old_top = own_top[...]
            mine = jnp.maximum(old_top, peak[:, :lanes])
            top = jnp.concatenate([mine, peak[:, lanes:]], axis=1)
            factor = jnp.exp2((old_top - mine) * base_two)
            weights = jnp.exp2((score_ref[slot, :own_block, : 2 * lanes] - top) * base_two)
            total = jnp.sum(weights, axis=0, keepdims=True)
            low = pl.multiple_of(step * own_block, own_block)
            whole = jnp.dot(
                vt_ref[:, pl.ds(low, own_block)],
                weights.astype(jnp.bfloat16),
                preferred_element_type=jnp.float32,
            )
            which = lax.broadcasted_iota(jnp.int32, (128, 2 * lanes), 1) // (per_kv * tree) % local_kv
            mixed = whole[:128]
            for kv in range(1, local_kv):
                mixed = jnp.where(which == kv, whole[kv * 128 : (kv + 1) * 128], mixed)
            own_top[...] = mine
            own_sum[...] = own_sum[...] * factor + total[:, :lanes]
            own_mix[...] = own_mix[...] * factor + mixed[:, :lanes]

            @pl.when(ended)
            def _():
                finish(owner)
                own_top[...] = peak[:, lanes:]
                own_sum[...] = total[:, lanes:]
                own_mix[...] = mixed[:, lanes:]

            return next_owner, next_begin

        owner, begin = lax.fori_loop(0, blocks, visit, (owner, begin))

        @pl.when(begin < base + pool)
        def _():
            finish(owner)

    def group_step(group, start):
        first, last = bounds(start, prefix_ref[group])

        @pl.when(last > first)
        def _():
            shared_part(group, first, last)

        return start + prefix_ref[group]

    own_start = lax.fori_loop(0, groups, group_step, 0)

    @pl.when(base + pool > own_start)
    def _():
        own_parts(own_start)

    for copy in copies:
        copy.wait()


def pool_attention(
    prefix_len, own_len, request_group, query, keys, turned, select, key_new, value_new, per_kv, score_scale
):
    requests, tree, width = query.shape
    pool, kv_width = keys.shape
    local_kv = kv_width // 128
    heads = local_kv * per_kv
    rows = per_kv * (requests // prefix_len.shape[0]) * tree
    lanes = heads * tree
    vmem = pl.BlockSpec(memory_space=pltpu.VMEM)
    smem = pl.BlockSpec(memory_space=pltpu.SMEM)
    hbm = pl.BlockSpec(memory_space=pltpu.HBM)
    return pl.pallas_call(
        functools.partial(pool_kernel, per_kv, min(512, pool), min(256, pool), score_scale),
        out_shape=(
            jax.ShapeDtypeStruct(query.shape, jnp.bfloat16),
            jax.ShapeDtypeStruct((requests, 8, 128), jnp.float32),
            jax.ShapeDtypeStruct(key_new.shape, jnp.bfloat16),
            jax.ShapeDtypeStruct(value_new.shape, jnp.bfloat16),
        ),
        in_specs=[smem] * 3 + [vmem] * 6,
        out_specs=(vmem, vmem, hbm, hbm),
        scratch_shapes=[
            pltpu.SMEM((requests + 1,), jnp.int32),
            pltpu.VMEM(key_new.shape, jnp.bfloat16),
            pltpu.VMEM(value_new.shape, jnp.bfloat16),
            pltpu.VMEM((local_kv, rows, 128), jnp.bfloat16),
            pltpu.VMEM((local_kv, rows), jnp.float32),
            pltpu.VMEM((local_kv, rows), jnp.float32),
            pltpu.VMEM((local_kv, 128, rows), jnp.float32),
            pltpu.VMEM((2, 2 * lanes, kv_width), jnp.bfloat16),
            pltpu.VMEM((1, lanes), jnp.float32),
            pltpu.VMEM((1, lanes), jnp.float32),
            pltpu.VMEM((128, lanes), jnp.float32),
            pltpu.VMEM((2, 512, max(rows, 2 * lanes)), jnp.float32),
            pltpu.VMEM((2, max(rows, 2 * lanes)), jnp.float32),
            pltpu.SemaphoreType.DMA((2,)),
        ],
        compiler_params=pltpu.CompilerParams(vmem_limit_bytes=40 * 2**20),
        name="pool_attention",
    )(prefix_len, own_len, request_group, query, keys, turned, select, key_new, value_new)


def body(
    hidden,
    in_gain,
    w_query,
    key_projection_weight,
    value_projection_weight,
    w_gate,
    w_out,
    q_gain,
    k_gain,
    cache_keys,
    pooled_cache_values,
    prefix_len,
    own_len,
    request_group,
    parents,
    accepted_leaf,
):
    local_req, tree = parents.shape
    requests = own_len.shape[0]
    head_width = q_gain.shape[0]
    local_heads = w_gate.shape[1]
    local_kv = key_projection_weight.shape[1] // head_width
    per_kv = local_heads // local_kv
    local_tok = hidden.shape[0]
    pool_dev = cache_keys.shape[0]
    score_scale = 1.0 / math.sqrt(head_width)
    seq_count = requests // local_req
    kv_count = in_gain.shape[0] // hidden.shape[1]
    half = np.exp(np.arange(head_width // 2) * (-2.0 * math.log(ROPE_BASE) / head_width))
    freqs = np.concatenate([half, half]).astype(np.float32)

    lines = [in_gain[None], q_gain[None], k_gain[None], jnp.asarray(freqs)[None]]
    lines += [prefix_len[None], own_len[None], request_group[None], accepted_leaf[None], parents]
    gate_top = 16
    depth = gate_top + local_heads + -local_heads % 8
    sums = {}
    top = 0
    for values in lines + [w_gate.T]:
        rows, lanes = values.shape
        low = gate_top if values.dtype == jnp.bfloat16 else top
        edges = ((low, depth - low - rows, 0), (0, in_gain.shape[0] - lanes, 0))
        padded = lax.pad(values, jnp.zeros((), values.dtype), edges)
        sums[values.dtype] = sums[values.dtype] + padded if values.dtype in sums else padded
        top += rows
    small = functools.reduce(jnp.add, [total.astype(jnp.float32) for total in sums.values()])
    gathered, key_new, value_new, tree_mix, tree_lse, gate, select, keys, turned = layer_front(
        hidden,
        small,
        w_query,
        key_projection_weight,
        value_projection_weight,
        cache_keys.reshape(pool_dev * local_kv, head_width),
        pooled_cache_values.reshape(pool_dev * local_kv, head_width),
        seq_count,
        kv_count,
        tree,
        score_scale,
    )
    parts, part_lse, accepted_keys, accepted_values = pool_attention(
        prefix_len,
        own_len,
        request_group,
        gathered,
        keys,
        turned,
        select,
        key_new,
        value_new,
        per_kv,
        score_scale,
    )
    layer_out = merge_parts(
        parts, part_lse, tree_mix, tree_lse, gate, w_out, hidden, seq_count, kv_count, per_kv
    )
    return (
        layer_out,
        accepted_keys.reshape(local_req, tree, local_kv * head_width),
        accepted_values.reshape(local_req, tree, local_kv * head_width),
    )


def solution(mesh):
    in_specs = (
        P("seq", "kv"),
        P(),
        P(None, "kv"),
        P(None, "kv"),
        P(None, "kv"),
        P(None, "kv"),
        P("kv", None),
        P(),
        P(),
        P("seq", "kv", None),
        P("seq", "kv", None),
        P(),
        P(),
        P(),
        P("seq", None),
        P("seq"),
    )
    out_specs = (P("seq", "kv"), P("seq", None, "kv"), P("seq", None, "kv"))
    return jax.shard_map(body, mesh=mesh, in_specs=in_specs, out_specs=out_specs, check_vma=False)
```

```python
import functools
import math

import jax
import jax.numpy as jnp
import numpy as np
from jax import lax
from jax.experimental import pallas as pl
from jax.experimental.pallas import tpu as pltpu
from jax.sharding import PartitionSpec as P

EPSILON = 1e-06
ROPE_BASE = 1000000.0
NEGATIVE = -1e30
EARLY = 2
HALVES = 2
FRONT_VMEM = 47 * 2**20


def rms_scale(values, scales):
    mean_square = jnp.mean(values * values, axis=-1, keepdims=True)
    return values * lax.rsqrt(mean_square + EPSILON) * scales


def rope_angles(positions, freqs):
    angles = positions * freqs
    turns = jnp.floor(angles * (2.0 / math.pi) + 0.5)
    rest = angles - turns * 1.5703125
    rest = rest - turns * 4.837512969970703125e-4
    rest = rest - turns * 7.549789954891882e-8
    square = rest * rest
    sine = rest + rest * square * (
        -1.6666654611e-1 + square * (8.3321608736e-3 - square * 1.9515295891e-4)
    )
    cosine = (
        1.0
        - 0.5 * square
        + square * square * (4.166664568298827e-2 + square * (-1.388731625493765e-3 + square * 2.443315711809948e-5))
    )
    quarter = turns.astype(jnp.int32) & 3
    swapped = (quarter & 1) == 1
    cos_out = jnp.where(swapped, sine, cosine)
    sin_out = jnp.where(swapped, cosine, sine)
    cos_out = jnp.where((quarter == 1) | (quarter == 2), -cos_out, cos_out)
    sin_out = jnp.where(quarter >= 2, -sin_out, sin_out)
    return cos_out, sin_out


def tree_tables(parents, leaves, contexts, freqs):
    local_req, width = parents.shape
    tokens = local_req * width
    rows = lax.broadcasted_iota(jnp.int32, (tokens, tokens), 0)
    cols = lax.broadcasted_iota(jnp.int32, (tokens, tokens), 1)
    above = jnp.concatenate(
        [parents[at : at + 1, :] + at * width for at in range(local_req)], axis=1
    )
    reached = jnp.where((above == rows) | (rows == cols), 1.0, 0.0)
    for squaring in range(max(1, (width - 1).bit_length())):
        half = reached.astype(jnp.bfloat16)
        reached = jnp.minimum(jnp.dot(half, half, preferred_element_type=jnp.float32), 1.0)
    reach = jnp.transpose(reached)
    depth_across = jnp.sum(reached, axis=0, keepdims=True) - 1.0
    depth_down = jnp.sum(reach, axis=1, keepdims=True) - 1.0
    which = lax.broadcasted_iota(jnp.int32, (tokens, 1), 0) // width
    context = jnp.zeros((tokens, 1), jnp.float32)
    is_leaf = rows < 0
    for at in range(local_req):
        context = jnp.where(which == at, contexts[at], context)
        is_leaf = is_leaf | (rows == leaves[:, at : at + 1] + at * width)
    on_path = jnp.sum(jnp.where(is_leaf, reach, 0.0), axis=0, keepdims=True)
    level = (rows % width).astype(jnp.float32)
    picked = (depth_across == level) & (rows // width == cols // width)
    select = jnp.where(picked, jnp.broadcast_to(on_path, (tokens, tokens)), 0.0)
    cosine, sine = rope_angles(context + depth_down, freqs)
    lanes = lax.broadcasted_iota(jnp.int32, cosine.shape, 1)
    sine = jnp.where(lanes < cosine.shape[1] // 2, -sine, sine)
    return reach, select, cosine, sine


def lowest(distance):
    return distance & -distance


def flip(index, distance):
    out = index
    bit = 1
    while bit <= distance:
        if distance & bit:
            out = out + bit * (1 - 2 * ((index // bit) % 2))
        bit *= 2
    return out


def one_bits(count):
    bits = []
    bit = 1
    while bit < count:
        bits.append(bit)
        bit *= 2
    return bits


def greet(me, count, kv, kv_count):
    barrier = pltpu.get_barrier_semaphore()
    bits = one_bits(count)
    for bit in bits:
        pl.semaphore_signal(barrier, inc=1, device_id={"seq": flip(me, bit)})
    for hop in range(1, kv_count):
        pl.semaphore_signal(barrier, inc=1, device_id={"kv": (kv + hop) % kv_count})
    pl.semaphore_wait(barrier, len(bits) + kv_count - 1)


def layer_kernel(
    count,
    kv_count,
    tree,
    score_scale,
    hidden_ref,
    small_ref,
    w_query_ref,
    w_key_ref,
    w_value_ref,
    cache_key_ref,
    cache_value_ref,
    all_ref,
    picked_key_ref,
    picked_value_ref,
    tree_ref,
    tree_lse_ref,
    gate_ref,
    keys_ref,
    turned_ref,
    key_ref,
    value_ref,
    select_ref,
    wide,
    w_query,
    w_key,
    w_value,
    raw_keys,
    raw_values,
    stage,
    cos_ref,
    sin_ref,
    seen_ref,
    load_sem,
    wide_send,
    wide_recv,
    send_sem,
    recv_sem,
):
    me = lax.axis_index("seq")
    kv = lax.axis_index("kv")
    loads = [
        pltpu.make_async_copy(source, target, load_sem.at[which])
        for which, (source, target) in enumerate(
            [
                (hidden_ref, wide.at[kv]),
                (w_query_ref, w_query),
                (w_key_ref, w_key),
                (w_value_ref, w_value),
                (cache_key_ref, raw_keys),
                (cache_value_ref, raw_values),
            ]
        )
    ]
    for load in loads:
        load.start()
    greet(me, count, kv, kv_count)

    local_req = hidden_ref.shape[0] // tree

    def wide_message(hop, owner, at):
        own = slice(at * tree, (at + 1) * tree)
        return pltpu.make_async_remote_copy(
            src_ref=hidden_ref.at[own],
            dst_ref=wide.at[owner, own],
            send_sem=wide_send.at[hop, at],
            recv_sem=wide_recv.at[hop, at],
            device_id={"kv": (kv + hop) % kv_count},
        )

    wide_sent = [wide_message(hop, kv, at) for at in range(local_req) for hop in range(1, kv_count)]
    for copy in wide_sent:
        copy.start()
    lane = lax.broadcasted_iota(jnp.int32, (1, 128), 1)

    def row(at):
        return small_ref[1 + at : 2 + at, :128]

    def taken(values, index):
        return jnp.sum(jnp.where(lane == index, values, 0.0), axis=1, keepdims=True)

    contexts = [
        taken(row(3), taken(row(5), me * local_req + at).astype(jnp.int32))
        + taken(row(4), me * local_req + at)
        for at in range(local_req)
    ]
    parents = jnp.concatenate([row(7 + at)[:, :tree] for at in range(local_req)], axis=0).astype(jnp.int32)
    reach, select, cosine, sine = tree_tables(parents, row(6).astype(jnp.int32), contexts, row(2))
    seen_ref[...] = reach
    select_ref[...] = select.astype(jnp.bfloat16)
    cos_ref[...] = cosine
    sin_ref[...] = sine
    heads = w_query.shape[1] // 128

    def rotated(values, gain, part):
        values = rms_scale(values, gain)
        return (values * cos_ref[part, :] + pltpu.roll(values, 64, 1) * sin_ref[part, :]).astype(jnp.bfloat16)

    def message(distance, place, at):
        return pltpu.make_async_remote_copy(
            src_ref=all_ref.at[place],
            dst_ref=all_ref.at[place],
            send_sem=send_sem.at[distance, at],
            recv_sem=recv_sem.at[distance, at],
            device_id={"seq": flip(me, lowest(distance))},
        )

    sent = []

    def hand_on(distance, at):
        owner = flip(me, distance) * local_req + at
        if distance:
            message(distance, owner, at).wait_recv()
        bits = one_bits(lowest(distance) if distance else count)
        for bit in bits[1:] + bits[:1]:
            copy = message(distance | bit, owner, at)
            copy.start()
            sent.append(copy)

    loads[0].wait()
    normed_parts = []
    query_parts = []
    for at in range(local_req):
        own = slice(at * tree, (at + 1) * tree)
        for hop in range(1, kv_count):
            wide_message(hop, (kv + kv_count - hop) % kv_count, at).wait_recv()
        rows = jnp.concatenate([wide[owner, own] for owner in range(kv_count)], axis=1).astype(jnp.float32)
        mean_square = jnp.mean(rows * rows, axis=-1, keepdims=True)
        inverse = lax.rsqrt(mean_square + EPSILON)
        normed_parts.append((rows * inverse * small_ref[0:1, :]).astype(jnp.bfloat16))
        if not at:
            loads[1].wait()
        query = jnp.dot(normed_parts[at], w_query[...], preferred_element_type=jnp.float32)
        query_parts.append([rotated(query[:, h * 128 : (h + 1) * 128], row(0), own) for h in range(heads)])
        for head in range(heads):
            all_ref[me * local_req + at, :, head * 128 : (head + 1) * 128] = query_parts[at][head]
        hand_on(0, at)
    normed = jnp.concatenate(normed_parts, axis=0)
    queries = [jnp.concatenate([part[head] for part in query_parts], axis=0) for head in range(heads)]
    local_kv = key_ref.shape[1] // 128
    per_kv = heads // local_kv
    tokens = hidden_ref.shape[0]

    def keys_work():
        loads[2].wait()
        key = jnp.dot(normed, w_key[...], preferred_element_type=jnp.float32)
        for at in range(local_kv):
            cols = slice(at * 128, (at + 1) * 128)
            key_ref[:, cols] = rotated(key[:, cols], row(1), slice(0, tokens))

    def values_work():
        loads[3].wait()
        value_ref[...] = jnp.dot(
            normed, w_value[...], preferred_element_type=jnp.float32
        ).astype(jnp.bfloat16)
        gate_ref[...] = jax.nn.sigmoid(
            lax.dot_general(
                normed,
                small_ref[16 : 16 + heads, :].astype(jnp.bfloat16),
                (((1,), (1,)), ((), ())),
                preferred_element_type=jnp.float32,
            )
        )
        tree_lse_ref[...] = jnp.zeros(tree_lse_ref.shape, jnp.float32)

    def tree_work(at):
        cols = slice(at * 128, (at + 1) * 128)
        stacked = jnp.concatenate(queries[at * per_kv : (at + 1) * per_kv], axis=0)
        scores = (
            lax.dot_general(
                stacked,
                key_ref[:, cols],
                (((1,), (1,)), ((), ())),
                preferred_element_type=jnp.float32,
            )
            * score_scale
        )
        seen = jnp.concatenate([seen_ref[...]] * per_kv, axis=0) > 0.5
        scores = jnp.where(seen, scores, NEGATIVE)
        top = jnp.max(scores, axis=1, keepdims=True)
        weights = jnp.where(seen, jnp.exp(scores - top), 0.0)
        total = jnp.sum(weights, axis=1, keepdims=True)
        mixed = (
            jnp.dot(
                weights.astype(jnp.bfloat16), value_ref[:, cols], preferred_element_type=jnp.float32
            )
            / total
        )
        lse = top + jnp.log(total)
        for sub in range(per_kv):
            head = at * per_kv + sub
            part = slice(sub * tokens, (sub + 1) * tokens)
            tree_ref[:, head * 128 : (head + 1) * 128] = mixed[part]
            column = sub * local_kv + at
            tree_lse_ref[:, column : column + 1] = lse[part]

    pieces = 8
    slots = keys_ref.shape[0] // pieces

    def apart(source, which):
        stage[...] = source[which * slots * local_kv : (which + 1) * slots * local_kv, :].astype(jnp.float32)
        return [stage[pl.ds(at, slots, stride=local_kv), :] for at in range(local_kv)]

    def keys_apart(which):
        if which == 0:
            loads[4].wait()
        for at, part in enumerate(apart(raw_keys, which)):
            keys_ref[which * slots : (which + 1) * slots, at * 128 : (at + 1) * 128] = part.astype(jnp.bfloat16)

    def values_apart(which):
        if which == 0:
            loads[5].wait()
        for at, part in enumerate(apart(raw_values, which)):
            turned_ref[at * 128 : (at + 1) * 128, which * slots : (which + 1) * slots] = jnp.transpose(
                part
            ).astype(jnp.bfloat16)

    keys_work()
    values_work()
    def picks():
        picked = select_ref[...]
        for source, target in ((key_ref, picked_key_ref), (value_ref, picked_value_ref)):
            target[...] = jnp.dot(picked, source[...], preferred_element_type=jnp.float32).astype(jnp.bfloat16)

    work = [functools.partial(keys_apart, which) for which in range(pieces)]
    work += [functools.partial(values_apart, which) for which in range(pieces)]
    work += [functools.partial(tree_work, at) for at in range(local_kv)] + [picks]
    order = sorted(range(2, count, 2), key=lambda d: (-lowest(d), d))
    for distance in order:
        for at in range(local_req):
            hand_on(distance, at)
            if work:
                work.pop(0)()
    for rest in work:
        rest()
    for distance in range(1, count, 2):
        for at in range(local_req):
            hand_on(distance, at)
    for copy in wide_sent + sent:
        copy.wait_send()


def layer_front(
    hidden,
    small,
    w_query,
    w_key,
    w_value,
    cache_keys,
    cache_values,
    count,
    kv_count,
    tree,
    score_scale,
):
    tokens = hidden.shape[0]
    width = w_query.shape[1]
    local_kv = w_key.shape[1] // 128
    slots = cache_keys.shape[0] // local_kv
    vmem = pl.BlockSpec(memory_space=pltpu.VMEM)
    hbm = pl.BlockSpec(memory_space=pltpu.HBM)
    return pl.pallas_call(
        functools.partial(layer_kernel, count, kv_count, tree, score_scale),
        out_shape=(
            jax.ShapeDtypeStruct((count * tokens // tree, tree, width), jnp.bfloat16),
            jax.ShapeDtypeStruct((tokens, w_key.shape[1]), jnp.bfloat16),
            jax.ShapeDtypeStruct((tokens, w_value.shape[1]), jnp.bfloat16),
            jax.ShapeDtypeStruct((tokens, width), jnp.float32),
            jax.ShapeDtypeStruct((tokens, 128), jnp.float32),
            jax.ShapeDtypeStruct((tokens, width // 128), jnp.float32),
            jax.ShapeDtypeStruct((slots, local_kv * 128), jnp.bfloat16),
            jax.ShapeDtypeStruct((local_kv * 128, slots), jnp.bfloat16),
        ),
        in_specs=[vmem] * 2 + [hbm] * 5,
        out_specs=(vmem,) * 8,
        scratch_shapes=[
            pltpu.VMEM((tokens, w_key.shape[1]), jnp.bfloat16),
            pltpu.VMEM((tokens, w_value.shape[1]), jnp.bfloat16),
            pltpu.VMEM((tokens, tokens), jnp.bfloat16),
            pltpu.VMEM((kv_count,) + hidden.shape, hidden.dtype),
            pltpu.VMEM(w_query.shape, w_query.dtype),
            pltpu.VMEM(w_key.shape, w_key.dtype),
            pltpu.VMEM(w_value.shape, w_value.dtype),
            pltpu.VMEM(cache_keys.shape, jnp.bfloat16),
            pltpu.VMEM(cache_values.shape, jnp.bfloat16),
            pltpu.VMEM((cache_keys.shape[0] // 8, 128), jnp.float32),
            pltpu.VMEM((tokens, 128), jnp.float32),
            pltpu.VMEM((tokens, 128), jnp.float32),
            pltpu.VMEM((tokens, tokens), jnp.float32),
            pltpu.SemaphoreType.DMA((6,)),
            pltpu.SemaphoreType.DMA((kv_count, tokens // tree)),
            pltpu.SemaphoreType.DMA((kv_count, tokens // tree)),
            pltpu.SemaphoreType.DMA((count, tokens // tree)),
            pltpu.SemaphoreType.DMA((count, tokens // tree)),
        ],
        compiler_params=pltpu.CompilerParams(
            collective_id=0, has_side_effects=True, vmem_limit_bytes=FRONT_VMEM
        ),
        name="layer_front",
    )(
        hidden,
        small,
        w_query,
        w_key,
        w_value,
        cache_keys,
        cache_values,
    )


def merge_order(count):
    begin, free = {}, {}
    for distance in range(count - 2, 0, -2):
        bit = lowest(distance)
        ready = max([begin[distance | low] + 2 for low in one_bits(bit)[1:]], default=0)
        begin[distance] = max(ready, free.get(bit, 0))
        free[bit] = begin[distance] + 1
    return sorted(begin, key=lambda distance: (begin[distance], -distance))


def merge_kernel(
    count,
    kv_count,
    per_kv,
    part_ref,
    lse_ref,
    tree_ref,
    tree_lse_ref,
    gate_ref,
    w_out_ref,
    hidden_ref,
    out_ref,
    got,
    got_lse,
    held,
    held_lse,
    w_out,
    attended,
    outgoing,
    arrived,
    send_sem,
    recv_sem,
    load_sem,
    out_send,
    out_recv,
    pair_lse,
    pair_sem,
    base_lse,
    base_mix,
    totals,
):
    me = lax.axis_index("seq")
    kv = lax.axis_index("kv")
    requests, rows, _ = part_ref.shape
    local_req = requests // count
    heads = part_ref.shape[2] // 128
    load = pltpu.make_async_copy(w_out_ref, w_out, load_sem)
    load.start()
    greet(me, count, kv, kv_count)

    def messages(distance, at):
        owner = flip(me, distance) * local_req + at
        if distance % 2:
            sources = (part_ref.at[owner],)
        else:
            sources = (held.at[distance // 2, at], held_lse.at[distance // 2, at])
        return [
            pltpu.make_async_remote_copy(
                src_ref=source,
                dst_ref=target.at[distance, at],
                send_sem=send_sem.at[which, distance, at],
                recv_sem=recv_sem.at[which, distance, at],
                device_id={"seq": flip(me, lowest(distance))},
            )
            for which, (source, target) in enumerate(zip(sources, (got, got_lse)))
        ]

    sent = []

    def send(distance, at):
        for copy in messages(distance, at):
            copy.start()
            sent.append(copy)

    def blended(levels, sources):
        top = functools.reduce(jnp.maximum, levels)
        shares = [jnp.exp(level - top) for level in levels]
        total = functools.reduce(jnp.add, shares)
        inverse = 1.0 / total
        shares = [jnp.transpose(share * inverse)[:rows] for share in shares]
        mixed = []
        for head in range(heads):
            cols = slice(head * 128, (head + 1) * 128)
            place = head % per_kv * (heads // per_kv) + head // per_kv
            mixed.append(
                functools.reduce(
                    jnp.add,
                    [
                        source(cols).astype(jnp.float32) * share[:, place : place + 1]
                        for source, share in zip(sources, shares)
                    ],
                )
            )
        return top + jnp.log(total), mixed

    def received(distance, at):
        for copy in messages(distance, at):
            copy.wait_recv()
        owner = flip(me, distance - lowest(distance)) * local_req + at
        level = pair_lse[owner] if distance % 2 else got_lse[distance, at]
        return level, lambda cols: got[distance, at, :, cols]

    def gathered(distance, at, bits):
        owner = flip(me, distance) * local_req + at
        parts = [(lse_ref[owner], lambda cols: part_ref[owner, :, cols])]
        return parts + [received(distance | bit, at) for bit in bits]

    def combined(distance, at):
        level, mixed = blended(*zip(*gathered(distance, at, one_bits(lowest(distance)))))
        held_lse[distance // 2, at] = level
        for head in range(heads):
            held[distance // 2, at, :, head * 128 : (head + 1) * 128] = mixed[head].astype(held.dtype)

    def begun(at):
        own = slice(at * rows, (at + 1) * rows)
        turned = jnp.transpose(tree_lse_ref[own, :])[:8]
        level = jnp.concatenate([turned] * (128 // rows), axis=1)
        parts = gathered(0, at, one_bits(count)[:EARLY]) + [(level, lambda cols: tree_ref[own, cols])]
        level, mixed = blended(*zip(*parts))
        base_lse[at] = level
        for head in range(heads):
            base_mix[at, :, head * 128 : (head + 1) * 128] = mixed[head] * gate_ref[own, head : head + 1]

    def ended(at):
        own = slice(at * rows, (at + 1) * rows)
        parts = [(base_lse[at], lambda cols: base_mix[at, :, cols])]
        for bit in one_bits(count)[EARLY:]:
            level, source = received(bit, at)
            parts.append((level, source))
        top = functools.reduce(jnp.maximum, [level for level, _ in parts])
        shares = [jnp.exp(level - top) for level, _ in parts]
        inverse = 1.0 / functools.reduce(jnp.add, shares)
        shares = [jnp.transpose(share * inverse)[:rows] for share in shares]
        for head in range(heads):
            cols = slice(head * 128, (head + 1) * 128)
            place = head % per_kv * (heads // per_kv) + head // per_kv
            gate = gate_ref[own, head : head + 1]
            mixed = parts[0][1](cols) * shares[0][:, place : place + 1]
            for (_, source), share in zip(parts[1:], shares[1:]):
                mixed = mixed + source(cols).astype(jnp.float32) * (share[:, place : place + 1] * gate)
            attended[own, cols] = mixed.astype(jnp.bfloat16)

    all_lse = pltpu.make_async_remote_copy(
        src_ref=lse_ref,
        dst_ref=pair_lse,
        send_sem=pair_sem.at[0],
        recv_sem=pair_sem.at[1],
        device_id={"seq": flip(me, 1)},
    )
    all_lse.start()
    for distance in sorted(range(1, count, 2), reverse=True):
        for at in range(local_req):
            send(distance, at)
    all_lse.wait()
    for distance in merge_order(count):
        for at in range(local_req):
            combined(distance, at)
            send(distance, at)
    for at in range(local_req):
        begun(at)
    width = out_ref.shape[1]
    half = width // HALVES

    def projected(target, at, which):
        cols = pl.ds(pl.multiple_of(target * width + which * half, 128), half)
        return jnp.dot(
            attended[at * rows : (at + 1) * rows, :], w_out[:, cols], preferred_element_type=jnp.float32
        )

    def out_message(hop, at, which):
        cols = slice(which * half, (which + 1) * half)
        return pltpu.make_async_remote_copy(
            src_ref=outgoing.at[hop, at, :, cols],
            dst_ref=arrived.at[hop, at, :, cols],
            send_sem=out_send.at[hop, at, which],
            recv_sem=out_recv.at[hop, at, which],
            device_id={"kv": (kv + hop) % kv_count},
        )

    load.wait()
    for at in range(local_req):
        ended(at)
        for hop in range(1, kv_count):
            for which in range(HALVES):
                outgoing[hop, at, :, which * half : (which + 1) * half] = projected(
                    (kv + hop) % kv_count, at, which
                ).astype(jnp.bfloat16)
                copy = out_message(hop, at, which)
                copy.start()
                sent.append(copy)
        own = slice(at * rows, (at + 1) * rows)
        for which in range(HALVES):
            cols = slice(which * half, (which + 1) * half)
            totals[own, cols] = projected(kv, at, which) + hidden_ref[own, cols].astype(jnp.float32)
    for at in range(local_req):
        own = slice(at * rows, (at + 1) * rows)
        for which in range(HALVES):
            cols = slice(which * half, (which + 1) * half)
            total = totals[own, cols]
            for hop in range(1, kv_count):
                out_message(hop, at, which).wait_recv()
                total = total + arrived[hop, at, :, cols].astype(jnp.float32)
            out_ref[own, cols] = total.astype(jnp.bfloat16)
    for copy in sent:
        copy.wait_send()


def merge_parts(parts, lse, tree_mix, tree_lse, gate, w_out, hidden, count, kv_count, per_kv):
    requests, rows, width = parts.shape
    local_req = requests // count
    half = max(1, count // 2)
    vmem = pl.BlockSpec(memory_space=pltpu.VMEM)
    crossing = (kv_count, local_req, rows, hidden.shape[1])
    return pl.pallas_call(
        functools.partial(merge_kernel, count, kv_count, per_kv),
        out_shape=jax.ShapeDtypeStruct(hidden.shape, jnp.bfloat16),
        in_specs=[vmem] * 5 + [pl.BlockSpec(memory_space=pltpu.HBM), vmem],
        out_specs=vmem,
        scratch_shapes=[
            pltpu.VMEM((count, local_req, rows, width), parts.dtype),
            pltpu.VMEM((count, local_req) + lse.shape[1:], jnp.float32),
            pltpu.VMEM((half, local_req, rows, width), parts.dtype),
            pltpu.VMEM((half, local_req) + lse.shape[1:], jnp.float32),
            pltpu.VMEM(w_out.shape, w_out.dtype),
            pltpu.VMEM((local_req * rows, width), jnp.bfloat16),
            pltpu.VMEM(crossing, jnp.bfloat16),
            pltpu.VMEM(crossing, jnp.bfloat16),
            pltpu.SemaphoreType.DMA((2, count, local_req)),
            pltpu.SemaphoreType.DMA((2, count, local_req)),
            pltpu.SemaphoreType.DMA,
            pltpu.SemaphoreType.DMA((kv_count, local_req, HALVES)),
            pltpu.SemaphoreType.DMA((kv_count, local_req, HALVES)),
            pltpu.VMEM(lse.shape, jnp.float32),
            pltpu.SemaphoreType.DMA((2,)),
            pltpu.VMEM((local_req,) + lse.shape[1:], jnp.float32),
            pltpu.VMEM((local_req, rows, width), jnp.float32),
            pltpu.VMEM(hidden.shape, jnp.float32),
        ],
        compiler_params=pltpu.CompilerParams(
            collective_id=1, has_side_effects=True, vmem_limit_bytes=48 * 2**20
        ),
        name="merge_parts",
    )(parts, lse, tree_mix, tree_lse, gate, w_out, hidden)


def pool_kernel(
    per_kv,
    block,
    own_block,
    score_scale,
    prefix_ref,
    own_ref,
    group_ref,
    q_ref,
    k_ref,
    vt_ref,
    picked_keys,
    picked_values,
    o_ref,
    lse_ref,
    accepted_keys_ref,
    accepted_values_ref,
    member_ref,
    shared_q,
    shared_top,
    shared_sum,
    shared_mix,
    own_q,
    own_top,
    own_sum,
    own_mix,
    score_ref,
    peak_ref,
    picked_sem,
):
    requests, tree, width = q_ref.shape
    groups = prefix_ref.shape[0]
    pool, kv_width = k_ref.shape
    local_kv = kv_width // 128
    heads = local_kv * per_kv
    per_group = requests // groups
    rows = per_kv * per_group * tree
    part = min(256, block)
    base_two = score_scale / math.log(2.0)
    base = lax.axis_index("seq") * pool
    copies = [
        pltpu.make_async_copy(picked_keys, accepted_keys_ref, picked_sem.at[0]),
        pltpu.make_async_copy(picked_values, accepted_values_ref, picked_sem.at[1]),
    ]
    for copy in copies:
        copy.start()
    o_ref[...] = jnp.zeros_like(o_ref)
    lse_ref[...] = jnp.full(lse_ref.shape, NEGATIVE, jnp.float32)

    def put_lse(owner, levels):
        wide = jnp.concatenate([levels] * (128 // tree), axis=1)
        if heads < 8:
            wide = jnp.concatenate([wide] * (8 // heads), axis=0)
        lse_ref[owner] = wide

    def bounds(start, length):
        return jnp.clip(start - base, 0, pool), jnp.clip(start + length - base, 0, pool)

    def find_members(group):
        def find(request, found):
            member_ref[found] = request
            return found + (group_ref[request] == group).astype(jnp.int32)

        lax.fori_loop(0, requests, find, 0)
        return [member_ref[at] for at in range(per_group)]

    def shared_part(group, first, last):
        members = find_members(group)
        for kv in range(local_kv):
            for sub in range(per_kv):
                head = kv * per_kv + sub
                for at, owner in enumerate(members):
                    place = sub * per_group + at
                    shared_q[kv, place * tree : (place + 1) * tree, :] = q_ref[
                        owner, :, head * 128 : (head + 1) * 128
                    ]
        shared_top[...] = jnp.full(shared_top.shape, NEGATIVE, jnp.float32)
        shared_sum[...] = jnp.zeros_like(shared_sum)
        shared_mix[...] = jnp.zeros_like(shared_mix)
        first_step = first // block
        final_step = (last + block - 1) // block - 1

        def scored(start, kv, piece):
            low = pl.multiple_of(start + piece * part, part)
            slots = low + lax.broadcasted_iota(jnp.int32, (part, 128), 0)
            bias = jnp.where((slots >= first) & (slots < last), 0.0, NEGATIVE)
            bias = jnp.concatenate([bias] * (rows // 128), axis=1)
            raw = (
                lax.dot_general(
                    k_ref[pl.ds(low, part), kv * 128 : (kv + 1) * 128],
                    shared_q[kv],
                    (((1,), (1,)), ((), ())),
                    preferred_element_type=jnp.float32,
                )
                + bias
            )
            score_ref[kv % 2, piece * part : (piece + 1) * part, :rows] = raw
            return jnp.max(raw, axis=0, keepdims=True)

        peaks = [scored(first_step * block, 0, piece) for piece in range(block // part)]
        peak_ref[0:1, :rows] = functools.reduce(jnp.maximum, peaks)

        def visit(step, unused):
            start = step * block
            later = jnp.minimum(step + 1, final_step) * block
            for kv in range(local_kv):
                next_kv = (kv + 1) % local_kv
                next_start = later if next_kv == 0 else start
                slot = kv % 2
                old_top = shared_top[kv : kv + 1, :]
                top = jnp.maximum(old_top, peak_ref[slot : slot + 1, :rows])
                factor = jnp.exp2((old_top - top) * base_two)
                shared_top[kv : kv + 1, :] = top
                total = shared_sum[kv : kv + 1, :] * factor
                mixed = shared_mix[kv] * factor
                peaks = []
                for piece in range(block // part):
                    peaks.append(scored(next_start, next_kv, piece))
                    weights = jnp.exp2(
                        (score_ref[slot, piece * part : (piece + 1) * part, :rows] - top) * base_two
                    )
                    total = total + jnp.sum(weights, axis=0, keepdims=True)
                    low = pl.multiple_of(start + piece * part, part)
                    mixed = mixed + jnp.dot(
                        vt_ref[kv * 128 : (kv + 1) * 128, pl.ds(low, part)],
                        weights.astype(jnp.bfloat16),
                        preferred_element_type=jnp.float32,
                    )
                peak_ref[1 - slot : 2 - slot, :rows] = functools.reduce(jnp.maximum, peaks)
                shared_sum[kv : kv + 1, :] = total
                shared_mix[kv] = mixed
            return unused

        lax.fori_loop(first_step, final_step + 1, visit, 0)
        levels = shared_top[...] * score_scale + jnp.log(shared_sum[...])
        for kv in range(local_kv):
            mixed = jnp.transpose(shared_mix[kv] / shared_sum[kv : kv + 1, :]).astype(o_ref.dtype)
            for sub in range(per_kv):
                head = kv * per_kv + sub
                for at, owner in enumerate(members):
                    place = sub * per_group + at
                    o_ref[owner, :, head * 128 : (head + 1) * 128] = mixed[place * tree : (place + 1) * tree]
        for at, owner in enumerate(members):
            put_lse(
                owner,
                jnp.concatenate(
                    [
                        levels[:, (sub * per_group + at) * tree : (sub * per_group + at + 1) * tree]
                        for sub in range(per_kv)
                    ],
                    axis=0,
                ),
            )

    lanes = heads * tree
    blocks = pool // own_block

    def own_parts(start):
        own_q[...] = jnp.zeros_like(own_q)

        def seek(request, found):
            owner, begin = found
            passed = (owner == request) & (begin + own_ref[request] <= base)
            return (
                owner + passed.astype(jnp.int32),
                begin + jnp.where(passed, own_ref[request], 0),
            )

        owner, begin = lax.fori_loop(0, requests - 1, seek, (0, start))

        def stop_of(owner, begin):
            return begin + own_ref[owner] - base

        def scored(step, slot, owner, stop):
            other = jnp.minimum(owner + 1, requests - 1)
            for which, request in enumerate((owner, other)):
                for head in range(heads):
                    cols = slice(head // per_kv * 128, (head // per_kv + 1) * 128)
                    low = which * lanes + head * tree
                    own_q[slot, low : low + tree, cols] = q_ref[request, :, head * 128 : (head + 1) * 128]
            low = pl.multiple_of(step * own_block, own_block)
            slots = low + lax.broadcasted_iota(jnp.int32, (own_block, 128), 0)
            before = jnp.where(slots < stop, 0.0, NEGATIVE)
            after = jnp.where(slots < stop, NEGATIVE, 0.0)
            bias = jnp.concatenate([before] * (lanes // 128) + [after] * (lanes // 128), axis=1)
            raw = (
                lax.dot_general(
                    k_ref[pl.ds(low, own_block), :],
                    own_q[slot],
                    (((1,), (1,)), ((), ())),
                    preferred_element_type=jnp.float32,
                )
                + bias
            )
            score_ref[slot, :own_block, : 2 * lanes] = raw
            peak_ref[pl.ds(slot, 1), : 2 * lanes] = jnp.max(raw, axis=0, keepdims=True)

        def finish(owner):
            levels = own_top[...] * score_scale + jnp.log(own_sum[...])
            mixed = jnp.transpose(own_mix[...] / own_sum[...]).astype(o_ref.dtype)
            for head in range(heads):
                o_ref[owner, :, head * 128 : (head + 1) * 128] = mixed[head * tree : (head + 1) * tree]
            put_lse(
                owner,
                jnp.concatenate(
                    [
                        levels[:, (kv * per_kv + sub) * tree : (kv * per_kv + sub + 1) * tree]
                        for sub in range(per_kv)
                        for kv in range(local_kv)
                    ],
                    axis=0,
                ),
            )

        scored(0, 0, owner, stop_of(owner, begin))
        own_top[...] = jnp.full(own_top.shape, NEGATIVE, jnp.float32)
        own_sum[...] = jnp.zeros_like(own_sum)
        own_mix[...] = jnp.zeros_like(own_mix)

        def visit(step, at):
            owner, begin = at
            slot = step % 2
            ended = stop_of(owner, begin) <= (step + 1) * own_block
            next_owner = jnp.where(ended, jnp.minimum(owner + 1, requests - 1), owner)
            next_begin = jnp.where(ended, begin + own_ref[owner], begin)
            scored(jnp.minimum(step + 1, blocks - 1), 1 - slot, next_owner, stop_of(next_owner, next_begin))
            peak = peak_ref[pl.ds(slot, 1), : 2 * lanes]
            old_top = own_top[...]
            mine = jnp.maximum(old_top, peak[:, :lanes])
            top = jnp.concatenate([mine, peak[:, lanes:]], axis=1)
            factor = jnp.exp2((old_top - mine) * base_two)
            weights = jnp.exp2((score_ref[slot, :own_block, : 2 * lanes] - top) * base_two)
            total = jnp.sum(weights, axis=0, keepdims=True)
            low = pl.multiple_of(step * own_block, own_block)
            whole = jnp.dot(
                vt_ref[:, pl.ds(low, own_block)],
                weights.astype(jnp.bfloat16),
                preferred_element_type=jnp.float32,
            )
            which = lax.broadcasted_iota(jnp.int32, (128, 2 * lanes), 1) // (per_kv * tree) % local_kv
            mixed = whole[:128]
            for kv in range(1, local_kv):
                mixed = jnp.where(which == kv, whole[kv * 128 : (kv + 1) * 128], mixed)
            own_top[...] = mine
            own_sum[...] = own_sum[...] * factor + total[:, :lanes]
            own_mix[...] = own_mix[...] * factor + mixed[:, :lanes]

            @pl.when(ended)
            def _():
                finish(owner)
                own_top[...] = peak[:, lanes:]
                own_sum[...] = total[:, lanes:]
                own_mix[...] = mixed[:, lanes:]

            return next_owner, next_begin

        owner, begin = lax.fori_loop(0, blocks, visit, (owner, begin))

        @pl.when(begin < base + pool)
        def _():
            finish(owner)

    def group_step(group, start):
        first, last = bounds(start, prefix_ref[group])

        @pl.when(last > first)
        def _():
            shared_part(group, first, last)

        return start + prefix_ref[group]

    own_start = lax.fori_loop(0, groups, group_step, 0)

    @pl.when(base + pool > own_start)
    def _():
        own_parts(own_start)

    for copy in copies:
        copy.wait()


def pool_attention(
    prefix_len, own_len, request_group, query, keys, turned, picked_keys, picked_values, per_kv, score_scale
):
    requests, tree, width = query.shape
    pool, kv_width = keys.shape
    local_kv = kv_width // 128
    heads = local_kv * per_kv
    rows = per_kv * (requests // prefix_len.shape[0]) * tree
    lanes = heads * tree
    vmem = pl.BlockSpec(memory_space=pltpu.VMEM)
    smem = pl.BlockSpec(memory_space=pltpu.SMEM)
    hbm = pl.BlockSpec(memory_space=pltpu.HBM)
    return pl.pallas_call(
        functools.partial(pool_kernel, per_kv, min(512, pool), min(256, pool), score_scale),
        out_shape=(
            jax.ShapeDtypeStruct(query.shape, jnp.bfloat16),
            jax.ShapeDtypeStruct((requests, 8, 128), jnp.float32),
            jax.ShapeDtypeStruct(picked_keys.shape, jnp.bfloat16),
            jax.ShapeDtypeStruct(picked_values.shape, jnp.bfloat16),
        ),
        in_specs=[smem] * 3 + [vmem] * 5,
        out_specs=(vmem, vmem, hbm, hbm),
        scratch_shapes=[
            pltpu.SMEM((requests + 1,), jnp.int32),
            pltpu.VMEM((local_kv, rows, 128), jnp.bfloat16),
            pltpu.VMEM((local_kv, rows), jnp.float32),
            pltpu.VMEM((local_kv, rows), jnp.float32),
            pltpu.VMEM((local_kv, 128, rows), jnp.float32),
            pltpu.VMEM((2, 2 * lanes, kv_width), jnp.bfloat16),
            pltpu.VMEM((1, lanes), jnp.float32),
            pltpu.VMEM((1, lanes), jnp.float32),
            pltpu.VMEM((128, lanes), jnp.float32),
            pltpu.VMEM((2, 512, max(rows, 2 * lanes)), jnp.float32),
            pltpu.VMEM((2, max(rows, 2 * lanes)), jnp.float32),
            pltpu.SemaphoreType.DMA((2,)),
        ],
        compiler_params=pltpu.CompilerParams(vmem_limit_bytes=40 * 2**20),
        name="pool_attention",
    )(prefix_len, own_len, request_group, query, keys, turned, picked_keys, picked_values)


def body(
    hidden,
    in_gain,
    w_query,
    key_projection_weight,
    value_projection_weight,
    w_gate,
    w_out,
    q_gain,
    k_gain,
    cache_keys,
    pooled_cache_values,
    prefix_len,
    own_len,
    request_group,
    parents,
    accepted_leaf,
):
    local_req, tree = parents.shape
    requests = own_len.shape[0]
    head_width = q_gain.shape[0]
    local_heads = w_gate.shape[1]
    local_kv = key_projection_weight.shape[1] // head_width
    per_kv = local_heads // local_kv
    local_tok = hidden.shape[0]
    pool_dev = cache_keys.shape[0]
    score_scale = 1.0 / math.sqrt(head_width)
    seq_count = requests // local_req
    kv_count = in_gain.shape[0] // hidden.shape[1]
    half = np.exp(np.arange(head_width // 2) * (-2.0 * math.log(ROPE_BASE) / head_width))
    freqs = np.concatenate([half, half]).astype(np.float32)

    lines = [in_gain[None], q_gain[None], k_gain[None], jnp.asarray(freqs)[None]]
    lines += [prefix_len[None], own_len[None], request_group[None], accepted_leaf[None], parents]
    gate_top = 16
    depth = gate_top + local_heads + -local_heads % 8
    sums = {}
    top = 0
    for values in lines + [w_gate.T]:
        rows, lanes = values.shape
        low = gate_top if values.dtype == jnp.bfloat16 else top
        edges = ((low, depth - low - rows, 0), (0, in_gain.shape[0] - lanes, 0))
        padded = lax.pad(values, jnp.zeros((), values.dtype), edges)
        sums[values.dtype] = sums[values.dtype] + padded if values.dtype in sums else padded
        top += rows
    small = functools.reduce(jnp.add, [total.astype(jnp.float32) for total in sums.values()])
    gathered, picked_keys, picked_values, tree_mix, tree_lse, gate, keys, turned = layer_front(
        hidden,
        small,
        w_query,
        key_projection_weight,
        value_projection_weight,
        cache_keys.reshape(pool_dev * local_kv, head_width),
        pooled_cache_values.reshape(pool_dev * local_kv, head_width),
        seq_count,
        kv_count,
        tree,
        score_scale,
    )
    parts, part_lse, accepted_keys, accepted_values = pool_attention(
        prefix_len,
        own_len,
        request_group,
        gathered,
        keys,
        turned,
        picked_keys,
        picked_values,
        per_kv,
        score_scale,
    )
    layer_out = merge_parts(
        parts, part_lse, tree_mix, tree_lse, gate, w_out, hidden, seq_count, kv_count, per_kv
    )
    return (
        layer_out,
        accepted_keys.reshape(local_req, tree, local_kv * head_width),
        accepted_values.reshape(local_req, tree, local_kv * head_width),
    )


def solution(mesh):
    in_specs = (
        P("seq", "kv"),
        P(),
        P(None, "kv"),
        P(None, "kv"),
        P(None, "kv"),
        P(None, "kv"),
        P("kv", None),
        P(),
        P(),
        P("seq", "kv", None),
        P("seq", "kv", None),
        P(),
        P(),
        P(),
        P("seq", None),
        P("seq"),
    )
    out_specs = (P("seq", "kv"), P("seq", None, "kv"), P("seq", None, "kv"))
    return jax.shard_map(body, mesh=mesh, in_specs=in_specs, out_specs=out_specs, check_vma=False)
```

```python
import functools
import math

import jax
import jax.numpy as jnp
import numpy as np
from jax import lax
from jax.experimental import pallas as pl
from jax.experimental.pallas import tpu as pltpu
from jax.sharding import PartitionSpec as P

EPSILON = 1e-06
ROPE_BASE = 1000000.0
NEGATIVE = -1e30
EARLY = 2
HALVES = 2
FRONT_VMEM = 47 * 2**20


def rms_scale(values, scales):
    mean_square = jnp.mean(values * values, axis=-1, keepdims=True)
    return values * lax.rsqrt(mean_square + EPSILON) * scales


def rope_angles(positions, freqs):
    angles = positions * freqs
    turns = jnp.floor(angles * (2.0 / math.pi) + 0.5)
    rest = angles - turns * 1.5703125
    rest = rest - turns * 4.837512969970703125e-4
    rest = rest - turns * 7.549789954891882e-8
    square = rest * rest
    sine = rest + rest * square * (
        -1.6666654611e-1 + square * (8.3321608736e-3 - square * 1.9515295891e-4)
    )
    cosine = (
        1.0
        - 0.5 * square
        + square * square * (4.166664568298827e-2 + square * (-1.388731625493765e-3 + square * 2.443315711809948e-5))
    )
    quarter = turns.astype(jnp.int32) & 3
    swapped = (quarter & 1) == 1
    cos_out = jnp.where(swapped, sine, cosine)
    sin_out = jnp.where(swapped, cosine, sine)
    cos_out = jnp.where((quarter == 1) | (quarter == 2), -cos_out, cos_out)
    sin_out = jnp.where(quarter >= 2, -sin_out, sin_out)
    return cos_out, sin_out


def tree_tables(parents, leaves, contexts, freqs):
    local_req, width = parents.shape
    tokens = local_req * width
    rows = lax.broadcasted_iota(jnp.int32, (tokens, tokens), 0)
    cols = lax.broadcasted_iota(jnp.int32, (tokens, tokens), 1)
    above = jnp.concatenate(
        [parents[at : at + 1, :] + at * width for at in range(local_req)], axis=1
    )
    reached = jnp.where((above == rows) | (rows == cols), 1.0, 0.0)
    for squaring in range(max(1, (width - 1).bit_length())):
        half = reached.astype(jnp.bfloat16)
        reached = jnp.minimum(jnp.dot(half, half, preferred_element_type=jnp.float32), 1.0)
    reach = jnp.transpose(reached)
    depth_across = jnp.sum(reached, axis=0, keepdims=True) - 1.0
    depth_down = jnp.sum(reach, axis=1, keepdims=True) - 1.0
    which = lax.broadcasted_iota(jnp.int32, (tokens, 1), 0) // width
    context = jnp.zeros((tokens, 1), jnp.float32)
    is_leaf = rows < 0
    for at in range(local_req):
        context = jnp.where(which == at, contexts[at], context)
        is_leaf = is_leaf | (rows == leaves[:, at : at + 1] + at * width)
    on_path = jnp.sum(jnp.where(is_leaf, reach, 0.0), axis=0, keepdims=True)
    level = (rows % width).astype(jnp.float32)
    picked = (depth_across == level) & (rows // width == cols // width)
    select = jnp.where(picked, jnp.broadcast_to(on_path, (tokens, tokens)), 0.0)
    cosine, sine = rope_angles(context + depth_down, freqs)
    lanes = lax.broadcasted_iota(jnp.int32, cosine.shape, 1)
    sine = jnp.where(lanes < cosine.shape[1] // 2, -sine, sine)
    return reach, select, cosine, sine


def lowest(distance):
    return distance & -distance


def flip(index, distance):
    out = index
    bit = 1
    while bit <= distance:
        if distance & bit:
            out = out + bit * (1 - 2 * ((index // bit) % 2))
        bit *= 2
    return out


def one_bits(count):
    bits = []
    bit = 1
    while bit < count:
        bits.append(bit)
        bit *= 2
    return bits


def greet(me, count, kv, kv_count):
    barrier = pltpu.get_barrier_semaphore()
    bits = one_bits(count)
    for bit in bits:
        pl.semaphore_signal(barrier, inc=1, device_id={"seq": flip(me, bit)})
    for hop in range(1, kv_count):
        pl.semaphore_signal(barrier, inc=1, device_id={"kv": (kv + hop) % kv_count})
    pl.semaphore_wait(barrier, len(bits) + kv_count - 1)


def layer_kernel(
    count,
    kv_count,
    tree,
    score_scale,
    hidden_ref,
    small_ref,
    w_query_ref,
    w_key_ref,
    w_value_ref,
    cache_key_ref,
    cache_value_ref,
    all_ref,
    picked_key_ref,
    picked_value_ref,
    tree_ref,
    tree_lse_ref,
    gate_ref,
    keys_ref,
    turned_ref,
    key_ref,
    value_ref,
    select_ref,
    wide,
    w_query,
    w_key,
    w_value,
    raw_keys,
    raw_values,
    stage,
    cos_ref,
    sin_ref,
    seen_ref,
    load_sem,
    wide_send,
    wide_recv,
    send_sem,
    recv_sem,
):
    me = lax.axis_index("seq")
    kv = lax.axis_index("kv")
    loads = [
        pltpu.make_async_copy(source, target, load_sem.at[which])
        for which, (source, target) in enumerate(
            [
                (hidden_ref, wide.at[kv]),
                (w_query_ref, w_query),
                (w_key_ref, w_key),
                (w_value_ref, w_value),
                (cache_key_ref, raw_keys),
                (cache_value_ref, raw_values),
            ]
        )
    ]
    for load in loads:
        load.start()
    greet(me, count, kv, kv_count)

    local_req = hidden_ref.shape[0] // tree

    def wide_message(hop, owner, at):
        own = slice(at * tree, (at + 1) * tree)
        return pltpu.make_async_remote_copy(
            src_ref=hidden_ref.at[own],
            dst_ref=wide.at[owner, own],
            send_sem=wide_send.at[hop, at],
            recv_sem=wide_recv.at[hop, at],
            device_id={"kv": (kv + hop) % kv_count},
        )

    wide_sent = [wide_message(hop, kv, at) for at in range(local_req) for hop in range(1, kv_count)]
    for copy in wide_sent:
        copy.start()
    lane = lax.broadcasted_iota(jnp.int32, (1, 128), 1)

    def row(at):
        return small_ref[1 + at : 2 + at, :128]

    def taken(values, index):
        return jnp.sum(jnp.where(lane == index, values, 0.0), axis=1, keepdims=True)

    contexts = [
        taken(row(3), taken(row(5), me * local_req + at).astype(jnp.int32))
        + taken(row(4), me * local_req + at)
        for at in range(local_req)
    ]
    parents = jnp.concatenate([row(7 + at)[:, :tree] for at in range(local_req)], axis=0).astype(jnp.int32)
    reach, select, cosine, sine = tree_tables(parents, row(6).astype(jnp.int32), contexts, row(2))
    seen_ref[...] = reach
    select_ref[...] = select.astype(jnp.bfloat16)
    cos_ref[...] = cosine
    sin_ref[...] = sine
    heads = w_query.shape[1] // 128

    def rotated(values, gain, part):
        values = rms_scale(values, gain)
        return (values * cos_ref[part, :] + pltpu.roll(values, 64, 1) * sin_ref[part, :]).astype(jnp.bfloat16)

    def message(distance, place, at):
        return pltpu.make_async_remote_copy(
            src_ref=all_ref.at[place],
            dst_ref=all_ref.at[place],
            send_sem=send_sem.at[distance, at],
            recv_sem=recv_sem.at[distance, at],
            device_id={"seq": flip(me, lowest(distance))},
        )

    sent = []

    def hand_on(distance, at):
        owner = flip(me, distance) * local_req + at
        if distance:
            message(distance, owner, at).wait_recv()
        bits = one_bits(lowest(distance) if distance else count)
        for bit in bits[1:] + bits[:1]:
            copy = message(distance | bit, owner, at)
            copy.start()
            sent.append(copy)

    loads[0].wait()
    normed_parts = []
    query_parts = []
    for at in range(local_req):
        own = slice(at * tree, (at + 1) * tree)
        for hop in range(1, kv_count):
            wide_message(hop, (kv + kv_count - hop) % kv_count, at).wait_recv()
        rows = jnp.concatenate([wide[owner, own] for owner in range(kv_count)], axis=1).astype(jnp.float32)
        mean_square = jnp.mean(rows * rows, axis=-1, keepdims=True)
        inverse = lax.rsqrt(mean_square + EPSILON)
        normed_parts.append((rows * inverse * small_ref[0:1, :]).astype(jnp.bfloat16))
        if not at:
            loads[1].wait()
        query = jnp.dot(normed_parts[at], w_query[...], preferred_element_type=jnp.float32)
        query_parts.append([rotated(query[:, h * 128 : (h + 1) * 128], row(0), own) for h in range(heads)])
        for head in range(heads):
            all_ref[me * local_req + at, :, head * 128 : (head + 1) * 128] = query_parts[at][head]
        hand_on(0, at)
    normed = jnp.concatenate(normed_parts, axis=0)
    queries = [jnp.concatenate([part[head] for part in query_parts], axis=0) for head in range(heads)]
    local_kv = key_ref.shape[1] // 128
    per_kv = heads // local_kv
    tokens = hidden_ref.shape[0]

    def keys_work():
        loads[2].wait()
        key = jnp.dot(normed, w_key[...], preferred_element_type=jnp.float32)
        for at in range(local_kv):
            cols = slice(at * 128, (at + 1) * 128)
            key_ref[:, cols] = rotated(key[:, cols], row(1), slice(0, tokens))

    def values_work():
        loads[3].wait()
        value_ref[...] = jnp.dot(
            normed, w_value[...], preferred_element_type=jnp.float32
        ).astype(jnp.bfloat16)
        gate_ref[...] = jax.nn.sigmoid(
            lax.dot_general(
                normed,
                small_ref[16 : 16 + heads, :].astype(jnp.bfloat16),
                (((1,), (1,)), ((), ())),
                preferred_element_type=jnp.float32,
            )
        )
        tree_lse_ref[...] = jnp.zeros(tree_lse_ref.shape, jnp.float32)

    def tree_work(at):
        cols = slice(at * 128, (at + 1) * 128)
        stacked = jnp.concatenate(queries[at * per_kv : (at + 1) * per_kv], axis=0)
        scores = (
            lax.dot_general(
                stacked,
                key_ref[:, cols],
                (((1,), (1,)), ((), ())),
                preferred_element_type=jnp.float32,
            )
            * score_scale
        )
        seen = jnp.concatenate([seen_ref[...]] * per_kv, axis=0) > 0.5
        scores = jnp.where(seen, scores, NEGATIVE)
        top = jnp.max(scores, axis=1, keepdims=True)
        weights = jnp.where(seen, jnp.exp(scores - top), 0.0)
        total = jnp.sum(weights, axis=1, keepdims=True)
        mixed = (
            jnp.dot(
                weights.astype(jnp.bfloat16), value_ref[:, cols], preferred_element_type=jnp.float32
            )
            / total
        )
        lse = top + jnp.log(total)
        for sub in range(per_kv):
            head = at * per_kv + sub
            part = slice(sub * tokens, (sub + 1) * tokens)
            tree_ref[:, head * 128 : (head + 1) * 128] = mixed[part]
            column = sub * local_kv + at
            tree_lse_ref[:, column : column + 1] = lse[part]

    pieces = 8
    slots = keys_ref.shape[0] // pieces

    def apart(source, which):
        stage[...] = source[which * slots * local_kv : (which + 1) * slots * local_kv, :].astype(jnp.float32)
        return [stage[pl.ds(at, slots, stride=local_kv), :] for at in range(local_kv)]

    def keys_apart(which):
        if which == 0:
            loads[4].wait()
        for at, part in enumerate(apart(raw_keys, which)):
            keys_ref[which * slots : (which + 1) * slots, at * 128 : (at + 1) * 128] = part.astype(jnp.bfloat16)

    def values_apart(which):
        if which == 0:
            loads[5].wait()
        for at, part in enumerate(apart(raw_values, which)):
            turned_ref[at * 128 : (at + 1) * 128, which * slots : (which + 1) * slots] = jnp.transpose(
                part
            ).astype(jnp.bfloat16)

    keys_work()
    values_work()
    def picks():
        picked = select_ref[...]
        for source, target in ((key_ref, picked_key_ref), (value_ref, picked_value_ref)):
            target[...] = jnp.dot(picked, source[...], preferred_element_type=jnp.float32).astype(jnp.bfloat16)

    work = [functools.partial(keys_apart, which) for which in range(pieces)]
    work += [functools.partial(values_apart, which) for which in range(pieces)]
    work += [functools.partial(tree_work, at) for at in range(local_kv)] + [picks]
    order = sorted(range(2, count, 2), key=lambda d: (-lowest(d), d))
    for distance in order:
        for at in range(local_req):
            hand_on(distance, at)
            if work:
                work.pop(0)()
    for rest in work:
        rest()
    for distance in range(1, count, 2):
        for at in range(local_req):
            hand_on(distance, at)
    for copy in wide_sent + sent:
        copy.wait_send()


def layer_front(
    hidden,
    small,
    w_query,
    w_key,
    w_value,
    cache_keys,
    cache_values,
    count,
    kv_count,
    tree,
    score_scale,
):
    tokens = hidden.shape[0]
    width = w_query.shape[1]
    local_kv = w_key.shape[1] // 128
    slots = cache_keys.shape[0] // local_kv
    vmem = pl.BlockSpec(memory_space=pltpu.VMEM)
    hbm = pl.BlockSpec(memory_space=pltpu.HBM)
    return pl.pallas_call(
        functools.partial(layer_kernel, count, kv_count, tree, score_scale),
        out_shape=(
            jax.ShapeDtypeStruct((count * tokens // tree, tree, width), jnp.bfloat16),
            jax.ShapeDtypeStruct((tokens, w_key.shape[1]), jnp.bfloat16),
            jax.ShapeDtypeStruct((tokens, w_value.shape[1]), jnp.bfloat16),
            jax.ShapeDtypeStruct((tokens, width), jnp.float32),
            jax.ShapeDtypeStruct((tokens, 128), jnp.float32),
            jax.ShapeDtypeStruct((tokens, width // 128), jnp.float32),
            jax.ShapeDtypeStruct((slots, local_kv * 128), jnp.bfloat16),
            jax.ShapeDtypeStruct((local_kv * 128, slots), jnp.bfloat16),
        ),
        in_specs=[vmem] * 2 + [hbm] * 5,
        out_specs=(vmem,) * 8,
        scratch_shapes=[
            pltpu.VMEM((tokens, w_key.shape[1]), jnp.bfloat16),
            pltpu.VMEM((tokens, w_value.shape[1]), jnp.bfloat16),
            pltpu.VMEM((tokens, tokens), jnp.bfloat16),
            pltpu.VMEM((kv_count,) + hidden.shape, hidden.dtype),
            pltpu.VMEM(w_query.shape, w_query.dtype),
            pltpu.VMEM(w_key.shape, w_key.dtype),
            pltpu.VMEM(w_value.shape, w_value.dtype),
            pltpu.VMEM(cache_keys.shape, jnp.bfloat16),
            pltpu.VMEM(cache_values.shape, jnp.bfloat16),
            pltpu.VMEM((cache_keys.shape[0] // 8, 128), jnp.float32),
            pltpu.VMEM((tokens, 128), jnp.float32),
            pltpu.VMEM((tokens, 128), jnp.float32),
            pltpu.VMEM((tokens, tokens), jnp.float32),
            pltpu.SemaphoreType.DMA((6,)),
            pltpu.SemaphoreType.DMA((kv_count, tokens // tree)),
            pltpu.SemaphoreType.DMA((kv_count, tokens // tree)),
            pltpu.SemaphoreType.DMA((count, tokens // tree)),
            pltpu.SemaphoreType.DMA((count, tokens // tree)),
        ],
        compiler_params=pltpu.CompilerParams(
            collective_id=0, has_side_effects=True, vmem_limit_bytes=FRONT_VMEM
        ),
        name="layer_front",
    )(
        hidden,
        small,
        w_query,
        w_key,
        w_value,
        cache_keys,
        cache_values,
    )


def leave_kernel(source_ref, target_ref, copy_sem):
    copy = pltpu.make_async_copy(source_ref, target_ref, copy_sem)
    copy.start()
    copy.wait()


def leave(result):
    return pl.pallas_call(
        leave_kernel,
        out_shape=jax.ShapeDtypeStruct(result.shape, result.dtype),
        in_specs=[pl.BlockSpec(memory_space=pltpu.VMEM)],
        out_specs=pl.BlockSpec(memory_space=pltpu.HBM),
        scratch_shapes=[pltpu.SemaphoreType.DMA],
        compiler_params=pltpu.CompilerParams(vmem_limit_bytes=4 * 2**20),
        name="leave",
    )(result)


def merge_order(count):
    begin, free = {}, {}
    for distance in range(count - 2, 0, -2):
        bit = lowest(distance)
        ready = max([begin[distance | low] + 2 for low in one_bits(bit)[1:]], default=0)
        begin[distance] = max(ready, free.get(bit, 0))
        free[bit] = begin[distance] + 1
    return sorted(begin, key=lambda distance: (begin[distance], -distance))


def merge_kernel(
    count,
    kv_count,
    per_kv,
    part_ref,
    lse_ref,
    tree_ref,
    tree_lse_ref,
    gate_ref,
    w_out_ref,
    hidden_ref,
    out_ref,
    got,
    got_lse,
    held,
    held_lse,
    w_out,
    attended,
    outgoing,
    arrived,
    send_sem,
    recv_sem,
    load_sem,
    out_send,
    out_recv,
    pair_lse,
    pair_sem,
    base_lse,
    base_mix,
    totals,
):
    me = lax.axis_index("seq")
    kv = lax.axis_index("kv")
    requests, rows, _ = part_ref.shape
    local_req = requests // count
    heads = part_ref.shape[2] // 128
    load = pltpu.make_async_copy(w_out_ref, w_out, load_sem)
    load.start()
    greet(me, count, kv, kv_count)

    def messages(distance, at):
        owner = flip(me, distance) * local_req + at
        if distance % 2:
            sources = (part_ref.at[owner],)
        else:
            sources = (held.at[distance // 2, at], held_lse.at[distance // 2, at])
        return [
            pltpu.make_async_remote_copy(
                src_ref=source,
                dst_ref=target.at[distance, at],
                send_sem=send_sem.at[which, distance, at],
                recv_sem=recv_sem.at[which, distance, at],
                device_id={"seq": flip(me, lowest(distance))},
            )
            for which, (source, target) in enumerate(zip(sources, (got, got_lse)))
        ]

    sent = []

    def send(distance, at):
        for copy in messages(distance, at):
            copy.start()
            sent.append(copy)

    def blended(levels, sources):
        top = functools.reduce(jnp.maximum, levels)
        shares = [jnp.exp(level - top) for level in levels]
        total = functools.reduce(jnp.add, shares)
        inverse = 1.0 / total
        shares = [jnp.transpose(share * inverse)[:rows] for share in shares]
        mixed = []
        for head in range(heads):
            cols = slice(head * 128, (head + 1) * 128)
            place = head % per_kv * (heads // per_kv) + head // per_kv
            mixed.append(
                functools.reduce(
                    jnp.add,
                    [
                        source(cols).astype(jnp.float32) * share[:, place : place + 1]
                        for source, share in zip(sources, shares)
                    ],
                )
            )
        return top + jnp.log(total), mixed

    def received(distance, at):
        for copy in messages(distance, at):
            copy.wait_recv()
        owner = flip(me, distance - lowest(distance)) * local_req + at
        level = pair_lse[owner] if distance % 2 else got_lse[distance, at]
        return level, lambda cols: got[distance, at, :, cols]

    def gathered(distance, at, bits):
        owner = flip(me, distance) * local_req + at
        parts = [(lse_ref[owner], lambda cols: part_ref[owner, :, cols])]
        return parts + [received(distance | bit, at) for bit in bits]

    def combined(distance, at):
        level, mixed = blended(*zip(*gathered(distance, at, one_bits(lowest(distance)))))
        held_lse[distance // 2, at] = level
        for head in range(heads):
            held[distance // 2, at, :, head * 128 : (head + 1) * 128] = mixed[head].astype(held.dtype)

    def begun(at):
        own = slice(at * rows, (at + 1) * rows)
        turned = jnp.transpose(tree_lse_ref[own, :])[:8]
        level = jnp.concatenate([turned] * (128 // rows), axis=1)
        parts = gathered(0, at, one_bits(count)[:EARLY]) + [(level, lambda cols: tree_ref[own, cols])]
        level, mixed = blended(*zip(*parts))
        base_lse[at] = level
        for head in range(heads):
            base_mix[at, :, head * 128 : (head + 1) * 128] = mixed[head] * gate_ref[own, head : head + 1]

    def ended(at):
        own = slice(at * rows, (at + 1) * rows)
        parts = [(base_lse[at], lambda cols: base_mix[at, :, cols])]
        for bit in one_bits(count)[EARLY:]:
            level, source = received(bit, at)
            parts.append((level, source))
        top = functools.reduce(jnp.maximum, [level for level, _ in parts])
        shares = [jnp.exp(level - top) for level, _ in parts]
        inverse = 1.0 / functools.reduce(jnp.add, shares)
        shares = [jnp.transpose(share * inverse)[:rows] for share in shares]
        for head in range(heads):
            cols = slice(head * 128, (head + 1) * 128)
            place = head % per_kv * (heads // per_kv) + head // per_kv
            gate = gate_ref[own, head : head + 1]
            mixed = parts[0][1](cols) * shares[0][:, place : place + 1]
            for (_, source), share in zip(parts[1:], shares[1:]):
                mixed = mixed + source(cols).astype(jnp.float32) * (share[:, place : place + 1] * gate)
            attended[own, cols] = mixed.astype(jnp.bfloat16)

    all_lse = pltpu.make_async_remote_copy(
        src_ref=lse_ref,
        dst_ref=pair_lse,
        send_sem=pair_sem.at[0],
        recv_sem=pair_sem.at[1],
        device_id={"seq": flip(me, 1)},
    )
    all_lse.start()
    for distance in sorted(range(1, count, 2), reverse=True):
        for at in range(local_req):
            send(distance, at)
    all_lse.wait()
    for distance in merge_order(count):
        for at in range(local_req):
            combined(distance, at)
            send(distance, at)
    for at in range(local_req):
        begun(at)
    width = out_ref.shape[1]
    half = width // HALVES

    def projected(target, at, which):
        cols = pl.ds(pl.multiple_of(target * width + which * half, 128), half)
        return jnp.dot(
            attended[at * rows : (at + 1) * rows, :], w_out[:, cols], preferred_element_type=jnp.float32
        )

    def out_message(hop, at, which):
        cols = slice(which * half, (which + 1) * half)
        return pltpu.make_async_remote_copy(
            src_ref=outgoing.at[hop, at, :, cols],
            dst_ref=arrived.at[hop, at, :, cols],
            send_sem=out_send.at[hop, at, which],
            recv_sem=out_recv.at[hop, at, which],
            device_id={"kv": (kv + hop) % kv_count},
        )

    load.wait()
    for at in range(local_req):
        ended(at)
        for hop in range(1, kv_count):
            for which in range(HALVES):
                outgoing[hop, at, :, which * half : (which + 1) * half] = projected(
                    (kv + hop) % kv_count, at, which
                ).astype(jnp.bfloat16)
                copy = out_message(hop, at, which)
                copy.start()
                sent.append(copy)
        own = slice(at * rows, (at + 1) * rows)
        for which in range(HALVES):
            cols = slice(which * half, (which + 1) * half)
            totals[own, cols] = projected(kv, at, which) + hidden_ref[own, cols].astype(jnp.float32)
    for at in range(local_req):
        own = slice(at * rows, (at + 1) * rows)
        for which in range(HALVES):
            cols = slice(which * half, (which + 1) * half)
            total = totals[own, cols]
            for hop in range(1, kv_count):
                out_message(hop, at, which).wait_recv()
                total = total + arrived[hop, at, :, cols].astype(jnp.float32)
            out_ref[own, cols] = total.astype(jnp.bfloat16)
    for copy in sent:
        copy.wait_send()


def merge_parts(parts, lse, tree_mix, tree_lse, gate, w_out, hidden, count, kv_count, per_kv):
    requests, rows, width = parts.shape
    local_req = requests // count
    half = max(1, count // 2)
    vmem = pl.BlockSpec(memory_space=pltpu.VMEM)
    crossing = (kv_count, local_req, rows, hidden.shape[1])
    return pl.pallas_call(
        functools.partial(merge_kernel, count, kv_count, per_kv),
        out_shape=jax.ShapeDtypeStruct(hidden.shape, jnp.bfloat16),
        in_specs=[vmem] * 5 + [pl.BlockSpec(memory_space=pltpu.HBM), vmem],
        out_specs=vmem,
        scratch_shapes=[
            pltpu.VMEM((count, local_req, rows, width), parts.dtype),
            pltpu.VMEM((count, local_req) + lse.shape[1:], jnp.float32),
            pltpu.VMEM((half, local_req, rows, width), parts.dtype),
            pltpu.VMEM((half, local_req) + lse.shape[1:], jnp.float32),
            pltpu.VMEM(w_out.shape, w_out.dtype),
            pltpu.VMEM((local_req * rows, width), jnp.bfloat16),
            pltpu.VMEM(crossing, jnp.bfloat16),
            pltpu.VMEM(crossing, jnp.bfloat16),
            pltpu.SemaphoreType.DMA((2, count, local_req)),
            pltpu.SemaphoreType.DMA((2, count, local_req)),
            pltpu.SemaphoreType.DMA,
            pltpu.SemaphoreType.DMA((kv_count, local_req, HALVES)),
            pltpu.SemaphoreType.DMA((kv_count, local_req, HALVES)),
            pltpu.VMEM(lse.shape, jnp.float32),
            pltpu.SemaphoreType.DMA((2,)),
            pltpu.VMEM((local_req,) + lse.shape[1:], jnp.float32),
            pltpu.VMEM((local_req, rows, width), jnp.float32),
            pltpu.VMEM(hidden.shape, jnp.float32),
        ],
        compiler_params=pltpu.CompilerParams(
            collective_id=1, has_side_effects=True, vmem_limit_bytes=48 * 2**20
        ),
        name="merge_parts",
    )(parts, lse, tree_mix, tree_lse, gate, w_out, hidden)


def pool_kernel(
    per_kv,
    block,
    own_block,
    score_scale,
    prefix_ref,
    own_ref,
    group_ref,
    q_ref,
    k_ref,
    vt_ref,
    picked_keys,
    picked_values,
    o_ref,
    lse_ref,
    accepted_keys_ref,
    accepted_values_ref,
    member_ref,
    shared_q,
    shared_top,
    shared_sum,
    shared_mix,
    own_q,
    own_top,
    own_sum,
    own_mix,
    score_ref,
    peak_ref,
    picked_sem,
):
    requests, tree, width = q_ref.shape
    groups = prefix_ref.shape[0]
    pool, kv_width = k_ref.shape
    local_kv = kv_width // 128
    heads = local_kv * per_kv
    per_group = requests // groups
    rows = per_kv * per_group * tree
    part = min(256, block)
    base_two = score_scale / math.log(2.0)
    base = lax.axis_index("seq") * pool
    copies = [
        pltpu.make_async_copy(picked_keys, accepted_keys_ref, picked_sem.at[0]),
        pltpu.make_async_copy(picked_values, accepted_values_ref, picked_sem.at[1]),
    ]
    for copy in copies:
        copy.start()
    o_ref[...] = jnp.zeros_like(o_ref)
    lse_ref[...] = jnp.full(lse_ref.shape, NEGATIVE, jnp.float32)

    def put_lse(owner, levels):
        wide = jnp.concatenate([levels] * (128 // tree), axis=1)
        if heads < 8:
            wide = jnp.concatenate([wide] * (8 // heads), axis=0)
        lse_ref[owner] = wide

    def bounds(start, length):
        return jnp.clip(start - base, 0, pool), jnp.clip(start + length - base, 0, pool)

    def find_members(group):
        def find(request, found):
            member_ref[found] = request
            return found + (group_ref[request] == group).astype(jnp.int32)

        lax.fori_loop(0, requests, find, 0)
        return [member_ref[at] for at in range(per_group)]

    def shared_part(group, first, last):
        members = find_members(group)
        for kv in range(local_kv):
            for sub in range(per_kv):
                head = kv * per_kv + sub
                for at, owner in enumerate(members):
                    place = sub * per_group + at
                    shared_q[kv, place * tree : (place + 1) * tree, :] = q_ref[
                        owner, :, head * 128 : (head + 1) * 128
                    ]
        shared_top[...] = jnp.full(shared_top.shape, NEGATIVE, jnp.float32)
        shared_sum[...] = jnp.zeros_like(shared_sum)
        shared_mix[...] = jnp.zeros_like(shared_mix)
        first_step = first // block
        final_step = (last + block - 1) // block - 1

        def scored(start, kv, piece):
            low = pl.multiple_of(start + piece * part, part)
            slots = low + lax.broadcasted_iota(jnp.int32, (part, 128), 0)
            bias = jnp.where((slots >= first) & (slots < last), 0.0, NEGATIVE)
            bias = jnp.concatenate([bias] * (rows // 128), axis=1)
            raw = (
                lax.dot_general(
                    k_ref[pl.ds(low, part), kv * 128 : (kv + 1) * 128],
                    shared_q[kv],
                    (((1,), (1,)), ((), ())),
                    preferred_element_type=jnp.float32,
                )
                + bias
            )
            score_ref[kv % 2, piece * part : (piece + 1) * part, :rows] = raw
            return jnp.max(raw, axis=0, keepdims=True)

        peaks = [scored(first_step * block, 0, piece) for piece in range(block // part)]
        peak_ref[0:1, :rows] = functools.reduce(jnp.maximum, peaks)

        def visit(step, unused):
            start = step * block
            later = jnp.minimum(step + 1, final_step) * block
            for kv in range(local_kv):
                next_kv = (kv + 1) % local_kv
                next_start = later if next_kv == 0 else start
                slot = kv % 2
                old_top = shared_top[kv : kv + 1, :]
                top = jnp.maximum(old_top, peak_ref[slot : slot + 1, :rows])
                factor = jnp.exp2((old_top - top) * base_two)
                shared_top[kv : kv + 1, :] = top
                total = shared_sum[kv : kv + 1, :] * factor
                mixed = shared_mix[kv] * factor
                peaks = []
                for piece in range(block // part):
                    peaks.append(scored(next_start, next_kv, piece))
                    weights = jnp.exp2(
                        (score_ref[slot, piece * part : (piece + 1) * part, :rows] - top) * base_two
                    )
                    total = total + jnp.sum(weights, axis=0, keepdims=True)
                    low = pl.multiple_of(start + piece * part, part)
                    mixed = mixed + jnp.dot(
                        vt_ref[kv * 128 : (kv + 1) * 128, pl.ds(low, part)],
                        weights.astype(jnp.bfloat16),
                        preferred_element_type=jnp.float32,
                    )
                peak_ref[1 - slot : 2 - slot, :rows] = functools.reduce(jnp.maximum, peaks)
                shared_sum[kv : kv + 1, :] = total
                shared_mix[kv] = mixed
            return unused

        lax.fori_loop(first_step, final_step + 1, visit, 0)
        levels = shared_top[...] * score_scale + jnp.log(shared_sum[...])
        for kv in range(local_kv):
            mixed = jnp.transpose(shared_mix[kv] / shared_sum[kv : kv + 1, :]).astype(o_ref.dtype)
            for sub in range(per_kv):
                head = kv * per_kv + sub
                for at, owner in enumerate(members):
                    place = sub * per_group + at
                    o_ref[owner, :, head * 128 : (head + 1) * 128] = mixed[place * tree : (place + 1) * tree]
        for at, owner in enumerate(members):
            put_lse(
                owner,
                jnp.concatenate(
                    [
                        levels[:, (sub * per_group + at) * tree : (sub * per_group + at + 1) * tree]
                        for sub in range(per_kv)
                    ],
                    axis=0,
                ),
            )

    lanes = heads * tree
    blocks = pool // own_block

    def own_parts(start):
        own_q[...] = jnp.zeros_like(own_q)

        def seek(request, found):
            owner, begin = found
            passed = (owner == request) & (begin + own_ref[request] <= base)
            return (
                owner + passed.astype(jnp.int32),
                begin + jnp.where(passed, own_ref[request], 0),
            )

        owner, begin = lax.fori_loop(0, requests - 1, seek, (0, start))

        def stop_of(owner, begin):
            return begin + own_ref[owner] - base

        def scored(step, slot, owner, stop):
            other = jnp.minimum(owner + 1, requests - 1)
            for which, request in enumerate((owner, other)):
                for head in range(heads):
                    cols = slice(head // per_kv * 128, (head // per_kv + 1) * 128)
                    low = which * lanes + head * tree
                    own_q[slot, low : low + tree, cols] = q_ref[request, :, head * 128 : (head + 1) * 128]
            low = pl.multiple_of(step * own_block, own_block)
            slots = low + lax.broadcasted_iota(jnp.int32, (own_block, 128), 0)
            before = jnp.where(slots < stop, 0.0, NEGATIVE)
            after = jnp.where(slots < stop, NEGATIVE, 0.0)
            bias = jnp.concatenate([before] * (lanes // 128) + [after] * (lanes // 128), axis=1)
            raw = (
                lax.dot_general(
                    k_ref[pl.ds(low, own_block), :],
                    own_q[slot],
                    (((1,), (1,)), ((), ())),
                    preferred_element_type=jnp.float32,
                )
                + bias
            )
            score_ref[slot, :own_block, : 2 * lanes] = raw
            peak_ref[pl.ds(slot, 1), : 2 * lanes] = jnp.max(raw, axis=0, keepdims=True)

        def finish(owner):
            levels = own_top[...] * score_scale + jnp.log(own_sum[...])
            mixed = jnp.transpose(own_mix[...] / own_sum[...]).astype(o_ref.dtype)
            for head in range(heads):
                o_ref[owner, :, head * 128 : (head + 1) * 128] = mixed[head * tree : (head + 1) * tree]
            put_lse(
                owner,
                jnp.concatenate(
                    [
                        levels[:, (kv * per_kv + sub) * tree : (kv * per_kv + sub + 1) * tree]
                        for sub in range(per_kv)
                        for kv in range(local_kv)
                    ],
                    axis=0,
                ),
            )

        scored(0, 0, owner, stop_of(owner, begin))
        own_top[...] = jnp.full(own_top.shape, NEGATIVE, jnp.float32)
        own_sum[...] = jnp.zeros_like(own_sum)
        own_mix[...] = jnp.zeros_like(own_mix)

        def visit(step, at):
            owner, begin = at
            slot = step % 2
            ended = stop_of(owner, begin) <= (step + 1) * own_block
            next_owner = jnp.where(ended, jnp.minimum(owner + 1, requests - 1), owner)
            next_begin = jnp.where(ended, begin + own_ref[owner], begin)
            scored(jnp.minimum(step + 1, blocks - 1), 1 - slot, next_owner, stop_of(next_owner, next_begin))
            peak = peak_ref[pl.ds(slot, 1), : 2 * lanes]
            old_top = own_top[...]
            mine = jnp.maximum(old_top, peak[:, :lanes])
            top = jnp.concatenate([mine, peak[:, lanes:]], axis=1)
            factor = jnp.exp2((old_top - mine) * base_two)
            weights = jnp.exp2((score_ref[slot, :own_block, : 2 * lanes] - top) * base_two)
            total = jnp.sum(weights, axis=0, keepdims=True)
            low = pl.multiple_of(step * own_block, own_block)
            whole = jnp.dot(
                vt_ref[:, pl.ds(low, own_block)],
                weights.astype(jnp.bfloat16),
                preferred_element_type=jnp.float32,
            )
            which = lax.broadcasted_iota(jnp.int32, (128, 2 * lanes), 1) // (per_kv * tree) % local_kv
            mixed = whole[:128]
            for kv in range(1, local_kv):
                mixed = jnp.where(which == kv, whole[kv * 128 : (kv + 1) * 128], mixed)
            own_top[...] = mine
            own_sum[...] = own_sum[...] * factor + total[:, :lanes]
            own_mix[...] = own_mix[...] * factor + mixed[:, :lanes]

            @pl.when(ended)
            def _():
                finish(owner)
                own_top[...] = peak[:, lanes:]
                own_sum[...] = total[:, lanes:]
                own_mix[...] = mixed[:, lanes:]

            return next_owner, next_begin

        owner, begin = lax.fori_loop(0, blocks, visit, (owner, begin))

        @pl.when(begin < base + pool)
        def _():
            finish(owner)

    def group_step(group, start):
        first, last = bounds(start, prefix_ref[group])

        @pl.when(last > first)
        def _():
            shared_part(group, first, last)

        return start + prefix_ref[group]

    own_start = lax.fori_loop(0, groups, group_step, 0)

    @pl.when(base + pool > own_start)
    def _():
        own_parts(own_start)

    for copy in copies:
        copy.wait()


def pool_attention(
    prefix_len, own_len, request_group, query, keys, turned, picked_keys, picked_values, per_kv, score_scale
):
    requests, tree, width = query.shape
    pool, kv_width = keys.shape
    local_kv = kv_width // 128
    heads = local_kv * per_kv
    rows = per_kv * (requests // prefix_len.shape[0]) * tree
    lanes = heads * tree
    vmem = pl.BlockSpec(memory_space=pltpu.VMEM)
    smem = pl.BlockSpec(memory_space=pltpu.SMEM)
    hbm = pl.BlockSpec(memory_space=pltpu.HBM)
    return pl.pallas_call(
        functools.partial(pool_kernel, per_kv, min(512, pool), min(256, pool), score_scale),
        out_shape=(
            jax.ShapeDtypeStruct(query.shape, jnp.bfloat16),
            jax.ShapeDtypeStruct((requests, 8, 128), jnp.float32),
            jax.ShapeDtypeStruct(picked_keys.shape, jnp.bfloat16),
            jax.ShapeDtypeStruct(picked_values.shape, jnp.bfloat16),
        ),
        in_specs=[smem] * 3 + [vmem] * 5,
        out_specs=(vmem, vmem, hbm, hbm),
        scratch_shapes=[
            pltpu.SMEM((requests + 1,), jnp.int32),
            pltpu.VMEM((local_kv, rows, 128), jnp.bfloat16),
            pltpu.VMEM((local_kv, rows), jnp.float32),
            pltpu.VMEM((local_kv, rows), jnp.float32),
            pltpu.VMEM((local_kv, 128, rows), jnp.float32),
            pltpu.VMEM((2, 2 * lanes, kv_width), jnp.bfloat16),
            pltpu.VMEM((1, lanes), jnp.float32),
            pltpu.VMEM((1, lanes), jnp.float32),
            pltpu.VMEM((128, lanes), jnp.float32),
            pltpu.VMEM((2, 512, max(rows, 2 * lanes)), jnp.float32),
            pltpu.VMEM((2, max(rows, 2 * lanes)), jnp.float32),
            pltpu.SemaphoreType.DMA((2,)),
        ],
        compiler_params=pltpu.CompilerParams(vmem_limit_bytes=40 * 2**20),
        name="pool_attention",
    )(prefix_len, own_len, request_group, query, keys, turned, picked_keys, picked_values)


def body(
    hidden,
    in_gain,
    w_query,
    key_projection_weight,
    value_projection_weight,
    w_gate,
    w_out,
    q_gain,
    k_gain,
    cache_keys,
    pooled_cache_values,
    prefix_len,
    own_len,
    request_group,
    parents,
    accepted_leaf,
):
    local_req, tree = parents.shape
    requests = own_len.shape[0]
    head_width = q_gain.shape[0]
    local_heads = w_gate.shape[1]
    local_kv = key_projection_weight.shape[1] // head_width
    per_kv = local_heads // local_kv
    local_tok = hidden.shape[0]
    pool_dev = cache_keys.shape[0]
    score_scale = 1.0 / math.sqrt(head_width)
    seq_count = requests // local_req
    kv_count = in_gain.shape[0] // hidden.shape[1]
    half = np.exp(np.arange(head_width // 2) * (-2.0 * math.log(ROPE_BASE) / head_width))
    freqs = np.concatenate([half, half]).astype(np.float32)

    lines = [in_gain[None], q_gain[None], k_gain[None], jnp.asarray(freqs)[None]]
    lines += [prefix_len[None], own_len[None], request_group[None], accepted_leaf[None], parents]
    gate_top = 16
    depth = gate_top + local_heads + -local_heads % 8
    sums = {}
    top = 0
    for values in lines + [w_gate.T]:
        rows, lanes = values.shape
        low = gate_top if values.dtype == jnp.bfloat16 else top
        edges = ((low, depth - low - rows, 0), (0, in_gain.shape[0] - lanes, 0))
        padded = lax.pad(values, jnp.zeros((), values.dtype), edges)
        sums[values.dtype] = sums[values.dtype] + padded if values.dtype in sums else padded
        top += rows
    small = functools.reduce(jnp.add, [total.astype(jnp.float32) for total in sums.values()])
    gathered, picked_keys, picked_values, tree_mix, tree_lse, gate, keys, turned = layer_front(
        hidden,
        small,
        w_query,
        key_projection_weight,
        value_projection_weight,
        cache_keys.reshape(pool_dev * local_kv, head_width),
        pooled_cache_values.reshape(pool_dev * local_kv, head_width),
        seq_count,
        kv_count,
        tree,
        score_scale,
    )
    parts, part_lse, accepted_keys, accepted_values = pool_attention(
        prefix_len,
        own_len,
        request_group,
        gathered,
        keys,
        turned,
        picked_keys,
        picked_values,
        per_kv,
        score_scale,
    )
    layer_out = merge_parts(
        parts, part_lse, tree_mix, tree_lse, gate, w_out, hidden, seq_count, kv_count, per_kv
    )
    return (
        leave(layer_out),
        accepted_keys.reshape(local_req, tree, local_kv * head_width),
        accepted_values.reshape(local_req, tree, local_kv * head_width),
    )


def solution(mesh):
    in_specs = (
        P("seq", "kv"),
        P(),
        P(None, "kv"),
        P(None, "kv"),
        P(None, "kv"),
        P(None, "kv"),
        P("kv", None),
        P(),
        P(),
        P("seq", "kv", None),
        P("seq", "kv", None),
        P(),
        P(),
        P(),
        P("seq", None),
        P("seq"),
    )
    out_specs = (P("seq", "kv"), P("seq", None, "kv"), P("seq", None, "kv"))
    return jax.shard_map(body, mesh=mesh, in_specs=in_specs, out_specs=out_specs, check_vma=False)
```

```python
import functools
import math

import jax
import jax.numpy as jnp
import numpy as np
from jax import lax
from jax.experimental import pallas as pl
from jax.experimental.pallas import tpu as pltpu
from jax.sharding import PartitionSpec as P

EPSILON = 1e-06
ROPE_BASE = 1000000.0
NEGATIVE = -1e30
EARLY = 2
HALVES = 2
FRONT_VMEM = 47 * 2**20


def rms_scale(values, scales):
    mean_square = jnp.mean(values * values, axis=-1, keepdims=True)
    return values * lax.rsqrt(mean_square + EPSILON) * scales


def rope_angles(positions, freqs):
    angles = positions * freqs
    turns = jnp.floor(angles * (2.0 / math.pi) + 0.5)
    rest = angles - turns * 1.5703125
    rest = rest - turns * 4.837512969970703125e-4
    rest = rest - turns * 7.549789954891882e-8
    square = rest * rest
    sine = rest + rest * square * (
        -1.6666654611e-1 + square * (8.3321608736e-3 - square * 1.9515295891e-4)
    )
    cosine = (
        1.0
        - 0.5 * square
        + square * square * (4.166664568298827e-2 + square * (-1.388731625493765e-3 + square * 2.443315711809948e-5))
    )
    quarter = turns.astype(jnp.int32) & 3
    swapped = (quarter & 1) == 1
    cos_out = jnp.where(swapped, sine, cosine)
    sin_out = jnp.where(swapped, cosine, sine)
    cos_out = jnp.where((quarter == 1) | (quarter == 2), -cos_out, cos_out)
    sin_out = jnp.where(quarter >= 2, -sin_out, sin_out)
    return cos_out, sin_out


def tree_tables(parents, leaves, contexts, freqs):
    local_req, width = parents.shape
    tokens = local_req * width
    rows = lax.broadcasted_iota(jnp.int32, (tokens, tokens), 0)
    cols = lax.broadcasted_iota(jnp.int32, (tokens, tokens), 1)
    above = jnp.concatenate(
        [parents[at : at + 1, :] + at * width for at in range(local_req)], axis=1
    )
    reached = jnp.where((above == rows) | (rows == cols), 1.0, 0.0)
    for squaring in range(max(1, (width - 1).bit_length())):
        half = reached.astype(jnp.bfloat16)
        reached = jnp.minimum(jnp.dot(half, half, preferred_element_type=jnp.float32), 1.0)
    reach = jnp.transpose(reached)
    depth_across = jnp.sum(reached, axis=0, keepdims=True) - 1.0
    depth_down = jnp.sum(reach, axis=1, keepdims=True) - 1.0
    which = lax.broadcasted_iota(jnp.int32, (tokens, 1), 0) // width
    context = jnp.zeros((tokens, 1), jnp.float32)
    is_leaf = rows < 0
    for at in range(local_req):
        context = jnp.where(which == at, contexts[at], context)
        is_leaf = is_leaf | (rows == leaves[:, at : at + 1] + at * width)
    on_path = jnp.sum(jnp.where(is_leaf, reach, 0.0), axis=0, keepdims=True)
    level = (rows % width).astype(jnp.float32)
    picked = (depth_across == level) & (rows // width == cols // width)
    select = jnp.where(picked, jnp.broadcast_to(on_path, (tokens, tokens)), 0.0)
    cosine, sine = rope_angles(context + depth_down, freqs)
    lanes = lax.broadcasted_iota(jnp.int32, cosine.shape, 1)
    sine = jnp.where(lanes < cosine.shape[1] // 2, -sine, sine)
    return reach, select, cosine, sine


def lowest(distance):
    return distance & -distance


def flip(index, distance):
    out = index
    bit = 1
    while bit <= distance:
        if distance & bit:
            out = out + bit * (1 - 2 * ((index // bit) % 2))
        bit *= 2
    return out


def one_bits(count):
    bits = []
    bit = 1
    while bit < count:
        bits.append(bit)
        bit *= 2
    return bits


def greet(me, count, kv, kv_count):
    barrier = pltpu.get_barrier_semaphore()
    bits = one_bits(count)
    for bit in bits:
        pl.semaphore_signal(barrier, inc=1, device_id={"seq": flip(me, bit)})
    for hop in range(1, kv_count):
        pl.semaphore_signal(barrier, inc=1, device_id={"kv": (kv + hop) % kv_count})
    pl.semaphore_wait(barrier, len(bits) + kv_count - 1)


def layer_kernel(
    count,
    kv_count,
    tree,
    score_scale,
    hidden_ref,
    small_ref,
    w_query_ref,
    w_key_ref,
    w_value_ref,
    cache_key_ref,
    cache_value_ref,
    all_ref,
    picked_key_ref,
    picked_value_ref,
    tree_ref,
    tree_lse_ref,
    gate_ref,
    keys_ref,
    turned_ref,
    key_ref,
    value_ref,
    select_ref,
    wide,
    w_query,
    w_key,
    w_value,
    raw_keys,
    raw_values,
    stage,
    cos_ref,
    sin_ref,
    seen_ref,
    load_sem,
    wide_send,
    wide_recv,
    send_sem,
    recv_sem,
):
    me = lax.axis_index("seq")
    kv = lax.axis_index("kv")
    loads = [
        pltpu.make_async_copy(source, target, load_sem.at[which])
        for which, (source, target) in enumerate(
            [
                (hidden_ref, wide.at[kv]),
                (w_query_ref, w_query),
                (w_key_ref, w_key),
                (w_value_ref, w_value),
                (cache_key_ref, raw_keys),
                (cache_value_ref, raw_values),
            ]
        )
    ]
    greet(me, count, kv, kv_count)

    local_req = hidden_ref.shape[0] // tree

    def wide_message(hop, owner, at):
        own = slice(at * tree, (at + 1) * tree)
        return pltpu.make_async_remote_copy(
            src_ref=hidden_ref.at[own],
            dst_ref=wide.at[owner, own],
            send_sem=wide_send.at[hop, at],
            recv_sem=wide_recv.at[hop, at],
            device_id={"kv": (kv + hop) % kv_count},
        )

    wide_sent = [wide_message(hop, kv, at) for at in range(local_req) for hop in range(1, kv_count)]
    for copy in wide_sent:
        copy.start()
    for load in loads:
        load.start()
    lane = lax.broadcasted_iota(jnp.int32, (1, 128), 1)

    def row(at):
        return small_ref[1 + at : 2 + at, :128]

    def taken(values, index):
        return jnp.sum(jnp.where(lane == index, values, 0.0), axis=1, keepdims=True)

    contexts = [
        taken(row(3), taken(row(5), me * local_req + at).astype(jnp.int32))
        + taken(row(4), me * local_req + at)
        for at in range(local_req)
    ]
    parents = jnp.concatenate([row(7 + at)[:, :tree] for at in range(local_req)], axis=0).astype(jnp.int32)
    reach, select, cosine, sine = tree_tables(parents, row(6).astype(jnp.int32), contexts, row(2))
    seen_ref[...] = reach
    select_ref[...] = select.astype(jnp.bfloat16)
    cos_ref[...] = cosine
    sin_ref[...] = sine
    heads = w_query.shape[1] // 128

    def rotated(values, gain, part):
        values = rms_scale(values, gain)
        return (values * cos_ref[part, :] + pltpu.roll(values, 64, 1) * sin_ref[part, :]).astype(jnp.bfloat16)

    def message(distance, place, at):
        return pltpu.make_async_remote_copy(
            src_ref=all_ref.at[place],
            dst_ref=all_ref.at[place],
            send_sem=send_sem.at[distance, at],
            recv_sem=recv_sem.at[distance, at],
            device_id={"seq": flip(me, lowest(distance))},
        )

    sent = []

    def hand_on(distance, at):
        owner = flip(me, distance) * local_req + at
        if distance:
            message(distance, owner, at).wait_recv()
        bits = one_bits(lowest(distance) if distance else count)
        for bit in bits[1:] + bits[:1]:
            copy = message(distance | bit, owner, at)
            copy.start()
            sent.append(copy)

    loads[0].wait()
    normed_parts = []
    query_parts = []
    for at in range(local_req):
        own = slice(at * tree, (at + 1) * tree)
        for hop in range(1, kv_count):
            wide_message(hop, (kv + kv_count - hop) % kv_count, at).wait_recv()
        rows = jnp.concatenate([wide[owner, own] for owner in range(kv_count)], axis=1).astype(jnp.float32)
        mean_square = jnp.mean(rows * rows, axis=-1, keepdims=True)
        inverse = lax.rsqrt(mean_square + EPSILON)
        normed_parts.append((rows * inverse * small_ref[0:1, :]).astype(jnp.bfloat16))
        if not at:
            loads[1].wait()
        query = jnp.dot(normed_parts[at], w_query[...], preferred_element_type=jnp.float32)
        query_parts.append([rotated(query[:, h * 128 : (h + 1) * 128], row(0), own) for h in range(heads)])
        for head in range(heads):
            all_ref[me * local_req + at, :, head * 128 : (head + 1) * 128] = query_parts[at][head]
        hand_on(0, at)
    normed = jnp.concatenate(normed_parts, axis=0)
    queries = [jnp.concatenate([part[head] for part in query_parts], axis=0) for head in range(heads)]
    local_kv = key_ref.shape[1] // 128
    per_kv = heads // local_kv
    tokens = hidden_ref.shape[0]

    def keys_work():
        loads[2].wait()
        key = jnp.dot(normed, w_key[...], preferred_element_type=jnp.float32)
        for at in range(local_kv):
            cols = slice(at * 128, (at + 1) * 128)
            key_ref[:, cols] = rotated(key[:, cols], row(1), slice(0, tokens))

    def values_work():
        loads[3].wait()
        value_ref[...] = jnp.dot(
            normed, w_value[...], preferred_element_type=jnp.float32
        ).astype(jnp.bfloat16)
        gate_ref[...] = jax.nn.sigmoid(
            lax.dot_general(
                normed,
                small_ref[16 : 16 + heads, :].astype(jnp.bfloat16),
                (((1,), (1,)), ((), ())),
                preferred_element_type=jnp.float32,
            )
        )
        tree_lse_ref[...] = jnp.zeros(tree_lse_ref.shape, jnp.float32)

    def tree_work(at):
        cols = slice(at * 128, (at + 1) * 128)
        stacked = jnp.concatenate(queries[at * per_kv : (at + 1) * per_kv], axis=0)
        scores = (
            lax.dot_general(
                stacked,
                key_ref[:, cols],
                (((1,), (1,)), ((), ())),
                preferred_element_type=jnp.float32,
            )
            * score_scale
        )
        seen = jnp.concatenate([seen_ref[...]] * per_kv, axis=0) > 0.5
        scores = jnp.where(seen, scores, NEGATIVE)
        top = jnp.max(scores, axis=1, keepdims=True)
        weights = jnp.where(seen, jnp.exp(scores - top), 0.0)
        total = jnp.sum(weights, axis=1, keepdims=True)
        mixed = (
            jnp.dot(
                weights.astype(jnp.bfloat16), value_ref[:, cols], preferred_element_type=jnp.float32
            )
            / total
        )
        lse = top + jnp.log(total)
        for sub in range(per_kv):
            head = at * per_kv + sub
            part = slice(sub * tokens, (sub + 1) * tokens)
            tree_ref[:, head * 128 : (head + 1) * 128] = mixed[part]
            column = sub * local_kv + at
            tree_lse_ref[:, column : column + 1] = lse[part]

    pieces = 8
    slots = keys_ref.shape[0] // pieces

    def apart(source, which):
        stage[...] = source[which * slots * local_kv : (which + 1) * slots * local_kv, :].astype(jnp.float32)
        return [stage[pl.ds(at, slots, stride=local_kv), :] for at in range(local_kv)]

    def keys_apart(which):
        if which == 0:
            loads[4].wait()
        for at, part in enumerate(apart(raw_keys, which)):
            keys_ref[which * slots : (which + 1) * slots, at * 128 : (at + 1) * 128] = part.astype(jnp.bfloat16)

    def values_apart(which):
        if which == 0:
            loads[5].wait()
        for at, part in enumerate(apart(raw_values, which)):
            turned_ref[at * 128 : (at + 1) * 128, which * slots : (which + 1) * slots] = jnp.transpose(
                part
            ).astype(jnp.bfloat16)

    keys_work()
    values_work()
    def picks():
        picked = select_ref[...]
        for source, target in ((key_ref, picked_key_ref), (value_ref, picked_value_ref)):
            target[...] = jnp.dot(picked, source[...], preferred_element_type=jnp.float32).astype(jnp.bfloat16)

    work = [functools.partial(keys_apart, which) for which in range(pieces)]
    work += [functools.partial(values_apart, which) for which in range(pieces)]
    work += [functools.partial(tree_work, at) for at in range(local_kv)] + [picks]
    order = sorted(range(2, count, 2), key=lambda d: (-lowest(d), d))
    for distance in order:
        for at in range(local_req):
            hand_on(distance, at)
            if work:
                work.pop(0)()
    for rest in work:
        rest()
    for distance in range(1, count, 2):
        for at in range(local_req):
            hand_on(distance, at)
    for copy in wide_sent + sent:
        copy.wait_send()


def layer_front(
    hidden,
    small,
    w_query,
    w_key,
    w_value,
    cache_keys,
    cache_values,
    count,
    kv_count,
    tree,
    score_scale,
):
    tokens = hidden.shape[0]
    width = w_query.shape[1]
    local_kv = w_key.shape[1] // 128
    slots = cache_keys.shape[0] // local_kv
    vmem = pl.BlockSpec(memory_space=pltpu.VMEM)
    hbm = pl.BlockSpec(memory_space=pltpu.HBM)
    return pl.pallas_call(
        functools.partial(layer_kernel, count, kv_count, tree, score_scale),
        out_shape=(
            jax.ShapeDtypeStruct((count * tokens // tree, tree, width), jnp.bfloat16),
            jax.ShapeDtypeStruct((tokens, w_key.shape[1]), jnp.bfloat16),
            jax.ShapeDtypeStruct((tokens, w_value.shape[1]), jnp.bfloat16),
            jax.ShapeDtypeStruct((tokens, width), jnp.float32),
            jax.ShapeDtypeStruct((tokens, 128), jnp.float32),
            jax.ShapeDtypeStruct((tokens, width // 128), jnp.float32),
            jax.ShapeDtypeStruct((slots, local_kv * 128), jnp.bfloat16),
            jax.ShapeDtypeStruct((local_kv * 128, slots), jnp.bfloat16),
        ),
        in_specs=[vmem] * 2 + [hbm] * 5,
        out_specs=(vmem,) * 8,
        scratch_shapes=[
            pltpu.VMEM((tokens, w_key.shape[1]), jnp.bfloat16),
            pltpu.VMEM((tokens, w_value.shape[1]), jnp.bfloat16),
            pltpu.VMEM((tokens, tokens), jnp.bfloat16),
            pltpu.VMEM((kv_count,) + hidden.shape, hidden.dtype),
            pltpu.VMEM(w_query.shape, w_query.dtype),
            pltpu.VMEM(w_key.shape, w_key.dtype),
            pltpu.VMEM(w_value.shape, w_value.dtype),
            pltpu.VMEM(cache_keys.shape, jnp.bfloat16),
            pltpu.VMEM(cache_values.shape, jnp.bfloat16),
            pltpu.VMEM((cache_keys.shape[0] // 8, 128), jnp.float32),
            pltpu.VMEM((tokens, 128), jnp.float32),
            pltpu.VMEM((tokens, 128), jnp.float32),
            pltpu.VMEM((tokens, tokens), jnp.float32),
            pltpu.SemaphoreType.DMA((6,)),
            pltpu.SemaphoreType.DMA((kv_count, tokens // tree)),
            pltpu.SemaphoreType.DMA((kv_count, tokens // tree)),
            pltpu.SemaphoreType.DMA((count, tokens // tree)),
            pltpu.SemaphoreType.DMA((count, tokens // tree)),
        ],
        compiler_params=pltpu.CompilerParams(
            collective_id=0, has_side_effects=True, vmem_limit_bytes=FRONT_VMEM
        ),
        name="layer_front",
    )(
        hidden,
        small,
        w_query,
        w_key,
        w_value,
        cache_keys,
        cache_values,
    )


def leave_kernel(source_ref, target_ref, copy_sem):
    copy = pltpu.make_async_copy(source_ref, target_ref, copy_sem)
    copy.start()
    copy.wait()


def leave(result):
    return pl.pallas_call(
        leave_kernel,
        out_shape=jax.ShapeDtypeStruct(result.shape, result.dtype),
        in_specs=[pl.BlockSpec(memory_space=pltpu.VMEM)],
        out_specs=pl.BlockSpec(memory_space=pltpu.HBM),
        scratch_shapes=[pltpu.SemaphoreType.DMA],
        compiler_params=pltpu.CompilerParams(vmem_limit_bytes=4 * 2**20),
        name="leave",
    )(result)


def merge_order(count):
    begin, free = {}, {}
    for distance in range(count - 2, 0, -2):
        bit = lowest(distance)
        ready = max([begin[distance | low] + 2 for low in one_bits(bit)[1:]], default=0)
        begin[distance] = max(ready, free.get(bit, 0))
        free[bit] = begin[distance] + 1
    return sorted(begin, key=lambda distance: (begin[distance], -distance))


def merge_kernel(
    count,
    kv_count,
    per_kv,
    part_ref,
    lse_ref,
    tree_ref,
    tree_lse_ref,
    gate_ref,
    w_out_ref,
    hidden_ref,
    out_ref,
    got,
    got_lse,
    held,
    held_lse,
    w_out,
    attended,
    outgoing,
    arrived,
    send_sem,
    recv_sem,
    load_sem,
    out_send,
    out_recv,
    pair_lse,
    pair_sem,
    base_lse,
    base_mix,
    totals,
):
    me = lax.axis_index("seq")
    kv = lax.axis_index("kv")
    requests, rows, _ = part_ref.shape
    local_req = requests // count
    heads = part_ref.shape[2] // 128
    load = pltpu.make_async_copy(w_out_ref, w_out, load_sem)
    load.start()
    greet(me, count, kv, kv_count)

    def messages(distance, at):
        owner = flip(me, distance) * local_req + at
        if distance % 2:
            sources = (part_ref.at[owner],)
        else:
            sources = (held.at[distance // 2, at], held_lse.at[distance // 2, at])
        return [
            pltpu.make_async_remote_copy(
                src_ref=source,
                dst_ref=target.at[distance, at],
                send_sem=send_sem.at[which, distance, at],
                recv_sem=recv_sem.at[which, distance, at],
                device_id={"seq": flip(me, lowest(distance))},
            )
            for which, (source, target) in enumerate(zip(sources, (got, got_lse)))
        ]

    sent = []

    def send(distance, at):
        for copy in messages(distance, at):
            copy.start()
            sent.append(copy)

    def blended(levels, sources):
        top = functools.reduce(jnp.maximum, levels)
        shares = [jnp.exp(level - top) for level in levels]
        total = functools.reduce(jnp.add, shares)
        inverse = 1.0 / total
        shares = [jnp.transpose(share * inverse)[:rows] for share in shares]
        mixed = []
        for head in range(heads):
            cols = slice(head * 128, (head + 1) * 128)
            place = head % per_kv * (heads // per_kv) + head // per_kv
            mixed.append(
                functools.reduce(
                    jnp.add,
                    [
                        source(cols).astype(jnp.float32) * share[:, place : place + 1]
                        for source, share in zip(sources, shares)
                    ],
                )
            )
        return top + jnp.log(total), mixed

    def received(distance, at):
        for copy in messages(distance, at):
            copy.wait_recv()
        owner = flip(me, distance - lowest(distance)) * local_req + at
        level = pair_lse[owner] if distance % 2 else got_lse[distance, at]
        return level, lambda cols: got[distance, at, :, cols]

    def gathered(distance, at, bits):
        owner = flip(me, distance) * local_req + at
        parts = [(lse_ref[owner], lambda cols: part_ref[owner, :, cols])]
        return parts + [received(distance | bit, at) for bit in bits]

    def combined(distance, at):
        level, mixed = blended(*zip(*gathered(distance, at, one_bits(lowest(distance)))))
        held_lse[distance // 2, at] = level
        for head in range(heads):
            held[distance // 2, at, :, head * 128 : (head + 1) * 128] = mixed[head].astype(held.dtype)

    def begun(at):
        own = slice(at * rows, (at + 1) * rows)
        turned = jnp.transpose(tree_lse_ref[own, :])[:8]
        level = jnp.concatenate([turned] * (128 // rows), axis=1)
        parts = gathered(0, at, one_bits(count)[:EARLY]) + [(level, lambda cols: tree_ref[own, cols])]
        level, mixed = blended(*zip(*parts))
        base_lse[at] = level
        for head in range(heads):
            base_mix[at, :, head * 128 : (head + 1) * 128] = mixed[head] * gate_ref[own, head : head + 1]

    def ended(at):
        own = slice(at * rows, (at + 1) * rows)
        parts = [(base_lse[at], lambda cols: base_mix[at, :, cols])]
        for bit in one_bits(count)[EARLY:]:
            level, source = received(bit, at)
            parts.append((level, source))
        top = functools.reduce(jnp.maximum, [level for level, _ in parts])
        shares = [jnp.exp(level - top) for level, _ in parts]
        inverse = 1.0 / functools.reduce(jnp.add, shares)
        shares = [jnp.transpose(share * inverse)[:rows] for share in shares]
        for head in range(heads):
            cols = slice(head * 128, (head + 1) * 128)
            place = head % per_kv * (heads // per_kv) + head // per_kv
            gate = gate_ref[own, head : head + 1]
            mixed = parts[0][1](cols) * shares[0][:, place : place + 1]
            for (_, source), share in zip(parts[1:], shares[1:]):
                mixed = mixed + source(cols).astype(jnp.float32) * (share[:, place : place + 1] * gate)
            attended[own, cols] = mixed.astype(jnp.bfloat16)

    all_lse = pltpu.make_async_remote_copy(
        src_ref=lse_ref,
        dst_ref=pair_lse,
        send_sem=pair_sem.at[0],
        recv_sem=pair_sem.at[1],
        device_id={"seq": flip(me, 1)},
    )
    all_lse.start()
    for distance in sorted(range(1, count, 2), reverse=True):
        for at in range(local_req):
            send(distance, at)
    all_lse.wait()
    for distance in merge_order(count):
        for at in range(local_req):
            combined(distance, at)
            send(distance, at)
    for at in range(local_req):
        begun(at)
    width = out_ref.shape[1]
    half = width // HALVES

    def projected(target, at, which):
        cols = pl.ds(pl.multiple_of(target * width + which * half, 128), half)
        return jnp.dot(
            attended[at * rows : (at + 1) * rows, :], w_out[:, cols], preferred_element_type=jnp.float32
        )

    def out_message(hop, at, which):
        cols = slice(which * half, (which + 1) * half)
        return pltpu.make_async_remote_copy(
            src_ref=outgoing.at[hop, at, :, cols],
            dst_ref=arrived.at[hop, at, :, cols],
            send_sem=out_send.at[hop, at, which],
            recv_sem=out_recv.at[hop, at, which],
            device_id={"kv": (kv + hop) % kv_count},
        )

    load.wait()
    for at in range(local_req):
        ended(at)
        for hop in range(1, kv_count):
            for which in range(HALVES):
                outgoing[hop, at, :, which * half : (which + 1) * half] = projected(
                    (kv + hop) % kv_count, at, which
                ).astype(jnp.bfloat16)
                copy = out_message(hop, at, which)
                copy.start()
                sent.append(copy)
        own = slice(at * rows, (at + 1) * rows)
        for which in range(HALVES):
            cols = slice(which * half, (which + 1) * half)
            totals[own, cols] = projected(kv, at, which) + hidden_ref[own, cols].astype(jnp.float32)
    for at in range(local_req):
        own = slice(at * rows, (at + 1) * rows)
        for which in range(HALVES):
            cols = slice(which * half, (which + 1) * half)
            total = totals[own, cols]
            for hop in range(1, kv_count):
                out_message(hop, at, which).wait_recv()
                total = total + arrived[hop, at, :, cols].astype(jnp.float32)
            out_ref[own, cols] = total.astype(jnp.bfloat16)
    for copy in sent:
        copy.wait_send()


def merge_parts(parts, lse, tree_mix, tree_lse, gate, w_out, hidden, count, kv_count, per_kv):
    requests, rows, width = parts.shape
    local_req = requests // count
    half = max(1, count // 2)
    vmem = pl.BlockSpec(memory_space=pltpu.VMEM)
    crossing = (kv_count, local_req, rows, hidden.shape[1])
    return pl.pallas_call(
        functools.partial(merge_kernel, count, kv_count, per_kv),
        out_shape=jax.ShapeDtypeStruct(hidden.shape, jnp.bfloat16),
        in_specs=[vmem] * 5 + [pl.BlockSpec(memory_space=pltpu.HBM), vmem],
        out_specs=vmem,
        scratch_shapes=[
            pltpu.VMEM((count, local_req, rows, width), parts.dtype),
            pltpu.VMEM((count, local_req) + lse.shape[1:], jnp.float32),
            pltpu.VMEM((half, local_req, rows, width), parts.dtype),
            pltpu.VMEM((half, local_req) + lse.shape[1:], jnp.float32),
            pltpu.VMEM(w_out.shape, w_out.dtype),
            pltpu.VMEM((local_req * rows, width), jnp.bfloat16),
            pltpu.VMEM(crossing, jnp.bfloat16),
            pltpu.VMEM(crossing, jnp.bfloat16),
            pltpu.SemaphoreType.DMA((2, count, local_req)),
            pltpu.SemaphoreType.DMA((2, count, local_req)),
            pltpu.SemaphoreType.DMA,
            pltpu.SemaphoreType.DMA((kv_count, local_req, HALVES)),
            pltpu.SemaphoreType.DMA((kv_count, local_req, HALVES)),
            pltpu.VMEM(lse.shape, jnp.float32),
            pltpu.SemaphoreType.DMA((2,)),
            pltpu.VMEM((local_req,) + lse.shape[1:], jnp.float32),
            pltpu.VMEM((local_req, rows, width), jnp.float32),
            pltpu.VMEM(hidden.shape, jnp.float32),
        ],
        compiler_params=pltpu.CompilerParams(
            collective_id=1, has_side_effects=True, vmem_limit_bytes=48 * 2**20
        ),
        name="merge_parts",
    )(parts, lse, tree_mix, tree_lse, gate, w_out, hidden)


def pool_kernel(
    per_kv,
    block,
    own_block,
    score_scale,
    prefix_ref,
    own_ref,
    group_ref,
    q_ref,
    k_ref,
    vt_ref,
    picked_keys,
    picked_values,
    o_ref,
    lse_ref,
    accepted_keys_ref,
    accepted_values_ref,
    member_ref,
    shared_q,
    shared_top,
    shared_sum,
    shared_mix,
    own_q,
    own_top,
    own_sum,
    own_mix,
    score_ref,
    peak_ref,
    picked_sem,
):
    requests, tree, width = q_ref.shape
    groups = prefix_ref.shape[0]
    pool, kv_width = k_ref.shape
    local_kv = kv_width // 128
    heads = local_kv * per_kv
    per_group = requests // groups
    rows = per_kv * per_group * tree
    part = min(256, block)
    base_two = score_scale / math.log(2.0)
    base = lax.axis_index("seq") * pool
    copies = [
        pltpu.make_async_copy(picked_keys, accepted_keys_ref, picked_sem.at[0]),
        pltpu.make_async_copy(picked_values, accepted_values_ref, picked_sem.at[1]),
    ]
    for copy in copies:
        copy.start()
    o_ref[...] = jnp.zeros_like(o_ref)
    lse_ref[...] = jnp.full(lse_ref.shape, NEGATIVE, jnp.float32)

    def put_lse(owner, levels):
        wide = jnp.concatenate([levels] * (128 // tree), axis=1)
        if heads < 8:
            wide = jnp.concatenate([wide] * (8 // heads), axis=0)
        lse_ref[owner] = wide

    def bounds(start, length):
        return jnp.clip(start - base, 0, pool), jnp.clip(start + length - base, 0, pool)

    def find_members(group):
        def find(request, found):
            member_ref[found] = request
            return found + (group_ref[request] == group).astype(jnp.int32)

        lax.fori_loop(0, requests, find, 0)
        return [member_ref[at] for at in range(per_group)]

    def shared_part(group, first, last):
        members = find_members(group)
        for kv in range(local_kv):
            for sub in range(per_kv):
                head = kv * per_kv + sub
                for at, owner in enumerate(members):
                    place = sub * per_group + at
                    shared_q[kv, place * tree : (place + 1) * tree, :] = q_ref[
                        owner, :, head * 128 : (head + 1) * 128
                    ]
        shared_top[...] = jnp.full(shared_top.shape, NEGATIVE, jnp.float32)
        shared_sum[...] = jnp.zeros_like(shared_sum)
        shared_mix[...] = jnp.zeros_like(shared_mix)
        first_step = first // block
        final_step = (last + block - 1) // block - 1

        def scored(start, kv, piece):
            low = pl.multiple_of(start + piece * part, part)
            slots = low + lax.broadcasted_iota(jnp.int32, (part, 128), 0)
            bias = jnp.where((slots >= first) & (slots < last), 0.0, NEGATIVE)
            bias = jnp.concatenate([bias] * (rows // 128), axis=1)
            raw = (
                lax.dot_general(
                    k_ref[pl.ds(low, part), kv * 128 : (kv + 1) * 128],
                    shared_q[kv],
                    (((1,), (1,)), ((), ())),
                    preferred_element_type=jnp.float32,
                )
                + bias
            )
            score_ref[kv % 2, piece * part : (piece + 1) * part, :rows] = raw
            return jnp.max(raw, axis=0, keepdims=True)

        peaks = [scored(first_step * block, 0, piece) for piece in range(block // part)]
        peak_ref[0:1, :rows] = functools.reduce(jnp.maximum, peaks)

        def visit(step, unused):
            start = step * block
            later = jnp.minimum(step + 1, final_step) * block
            for kv in range(local_kv):
                next_kv = (kv + 1) % local_kv
                next_start = later if next_kv == 0 else start
                slot = kv % 2
                old_top = shared_top[kv : kv + 1, :]
                top = jnp.maximum(old_top, peak_ref[slot : slot + 1, :rows])
                factor = jnp.exp2((old_top - top) * base_two)
                shared_top[kv : kv + 1, :] = top
                total = shared_sum[kv : kv + 1, :] * factor
                mixed = shared_mix[kv] * factor
                peaks = []
                for piece in range(block // part):
                    peaks.append(scored(next_start, next_kv, piece))
                    weights = jnp.exp2(
                        (score_ref[slot, piece * part : (piece + 1) * part, :rows] - top) * base_two
                    )
                    total = total + jnp.sum(weights, axis=0, keepdims=True)
                    low = pl.multiple_of(start + piece * part, part)
                    mixed = mixed + jnp.dot(
                        vt_ref[kv * 128 : (kv + 1) * 128, pl.ds(low, part)],
                        weights.astype(jnp.bfloat16),
                        preferred_element_type=jnp.float32,
                    )
                peak_ref[1 - slot : 2 - slot, :rows] = functools.reduce(jnp.maximum, peaks)
                shared_sum[kv : kv + 1, :] = total
                shared_mix[kv] = mixed
            return unused

        lax.fori_loop(first_step, final_step + 1, visit, 0)
        levels = shared_top[...] * score_scale + jnp.log(shared_sum[...])
        for kv in range(local_kv):
            mixed = jnp.transpose(shared_mix[kv] / shared_sum[kv : kv + 1, :]).astype(o_ref.dtype)
            for sub in range(per_kv):
                head = kv * per_kv + sub
                for at, owner in enumerate(members):
                    place = sub * per_group + at
                    o_ref[owner, :, head * 128 : (head + 1) * 128] = mixed[place * tree : (place + 1) * tree]
        for at, owner in enumerate(members):
            put_lse(
                owner,
                jnp.concatenate(
                    [
                        levels[:, (sub * per_group + at) * tree : (sub * per_group + at + 1) * tree]
                        for sub in range(per_kv)
                    ],
                    axis=0,
                ),
            )

    lanes = heads * tree
    blocks = pool // own_block

    def own_parts(start):
        own_q[...] = jnp.zeros_like(own_q)

        def seek(request, found):
            owner, begin = found
            passed = (owner == request) & (begin + own_ref[request] <= base)
            return (
                owner + passed.astype(jnp.int32),
                begin + jnp.where(passed, own_ref[request], 0),
            )

        owner, begin = lax.fori_loop(0, requests - 1, seek, (0, start))

        def stop_of(owner, begin):
            return begin + own_ref[owner] - base

        def scored(step, slot, owner, stop):
            other = jnp.minimum(owner + 1, requests - 1)
            for which, request in enumerate((owner, other)):
                for head in range(heads):
                    cols = slice(head // per_kv * 128, (head // per_kv + 1) * 128)
                    low = which * lanes + head * tree
                    own_q[slot, low : low + tree, cols] = q_ref[request, :, head * 128 : (head + 1) * 128]
            low = pl.multiple_of(step * own_block, own_block)
            slots = low + lax.broadcasted_iota(jnp.int32, (own_block, 128), 0)
            before = jnp.where(slots < stop, 0.0, NEGATIVE)
            after = jnp.where(slots < stop, NEGATIVE, 0.0)
            bias = jnp.concatenate([before] * (lanes // 128) + [after] * (lanes // 128), axis=1)
            raw = (
                lax.dot_general(
                    k_ref[pl.ds(low, own_block), :],
                    own_q[slot],
                    (((1,), (1,)), ((), ())),
                    preferred_element_type=jnp.float32,
                )
                + bias
            )
            score_ref[slot, :own_block, : 2 * lanes] = raw
            peak_ref[pl.ds(slot, 1), : 2 * lanes] = jnp.max(raw, axis=0, keepdims=True)

        def finish(owner):
            levels = own_top[...] * score_scale + jnp.log(own_sum[...])
            mixed = jnp.transpose(own_mix[...] / own_sum[...]).astype(o_ref.dtype)
            for head in range(heads):
                o_ref[owner, :, head * 128 : (head + 1) * 128] = mixed[head * tree : (head + 1) * tree]
            put_lse(
                owner,
                jnp.concatenate(
                    [
                        levels[:, (kv * per_kv + sub) * tree : (kv * per_kv + sub + 1) * tree]
                        for sub in range(per_kv)
                        for kv in range(local_kv)
                    ],
                    axis=0,
                ),
            )

        scored(0, 0, owner, stop_of(owner, begin))
        own_top[...] = jnp.full(own_top.shape, NEGATIVE, jnp.float32)
        own_sum[...] = jnp.zeros_like(own_sum)
        own_mix[...] = jnp.zeros_like(own_mix)

        def visit(step, at):
            owner, begin = at
            slot = step % 2
            ended = stop_of(owner, begin) <= (step + 1) * own_block
            next_owner = jnp.where(ended, jnp.minimum(owner + 1, requests - 1), owner)
            next_begin = jnp.where(ended, begin + own_ref[owner], begin)
            scored(jnp.minimum(step + 1, blocks - 1), 1 - slot, next_owner, stop_of(next_owner, next_begin))
            peak = peak_ref[pl.ds(slot, 1), : 2 * lanes]
            old_top = own_top[...]
            mine = jnp.maximum(old_top, peak[:, :lanes])
            top = jnp.concatenate([mine, peak[:, lanes:]], axis=1)
            factor = jnp.exp2((old_top - mine) * base_two)
            weights = jnp.exp2((score_ref[slot, :own_block, : 2 * lanes] - top) * base_two)
            total = jnp.sum(weights, axis=0, keepdims=True)
            low = pl.multiple_of(step * own_block, own_block)
            whole = jnp.dot(
                vt_ref[:, pl.ds(low, own_block)],
                weights.astype(jnp.bfloat16),
                preferred_element_type=jnp.float32,
            )
            which = lax.broadcasted_iota(jnp.int32, (128, 2 * lanes), 1) // (per_kv * tree) % local_kv
            mixed = whole[:128]
            for kv in range(1, local_kv):
                mixed = jnp.where(which == kv, whole[kv * 128 : (kv + 1) * 128], mixed)
            own_top[...] = mine
            own_sum[...] = own_sum[...] * factor + total[:, :lanes]
            own_mix[...] = own_mix[...] * factor + mixed[:, :lanes]

            @pl.when(ended)
            def _():
                finish(owner)
                own_top[...] = peak[:, lanes:]
                own_sum[...] = total[:, lanes:]
                own_mix[...] = mixed[:, lanes:]

            return next_owner, next_begin

        owner, begin = lax.fori_loop(0, blocks, visit, (owner, begin))

        @pl.when(begin < base + pool)
        def _():
            finish(owner)

    def group_step(group, start):
        first, last = bounds(start, prefix_ref[group])

        @pl.when(last > first)
        def _():
            shared_part(group, first, last)

        return start + prefix_ref[group]

    own_start = lax.fori_loop(0, groups, group_step, 0)

    @pl.when(base + pool > own_start)
    def _():
        own_parts(own_start)

    for copy in copies:
        copy.wait()


def pool_attention(
    prefix_len, own_len, request_group, query, keys, turned, picked_keys, picked_values, per_kv, score_scale
):
    requests, tree, width = query.shape
    pool, kv_width = keys.shape
    local_kv = kv_width // 128
    heads = local_kv * per_kv
    rows = per_kv * (requests // prefix_len.shape[0]) * tree
    lanes = heads * tree
    vmem = pl.BlockSpec(memory_space=pltpu.VMEM)
    smem = pl.BlockSpec(memory_space=pltpu.SMEM)
    hbm = pl.BlockSpec(memory_space=pltpu.HBM)
    return pl.pallas_call(
        functools.partial(pool_kernel, per_kv, min(512, pool), min(256, pool), score_scale),
        out_shape=(
            jax.ShapeDtypeStruct(query.shape, jnp.bfloat16),
            jax.ShapeDtypeStruct((requests, 8, 128), jnp.float32),
            jax.ShapeDtypeStruct(picked_keys.shape, jnp.bfloat16),
            jax.ShapeDtypeStruct(picked_values.shape, jnp.bfloat16),
        ),
        in_specs=[smem] * 3 + [vmem] * 5,
        out_specs=(vmem, vmem, hbm, hbm),
        scratch_shapes=[
            pltpu.SMEM((requests + 1,), jnp.int32),
            pltpu.VMEM((local_kv, rows, 128), jnp.bfloat16),
            pltpu.VMEM((local_kv, rows), jnp.float32),
            pltpu.VMEM((local_kv, rows), jnp.float32),
            pltpu.VMEM((local_kv, 128, rows), jnp.float32),
            pltpu.VMEM((2, 2 * lanes, kv_width), jnp.bfloat16),
            pltpu.VMEM((1, lanes), jnp.float32),
            pltpu.VMEM((1, lanes), jnp.float32),
            pltpu.VMEM((128, lanes), jnp.float32),
            pltpu.VMEM((2, 512, max(rows, 2 * lanes)), jnp.float32),
            pltpu.VMEM((2, max(rows, 2 * lanes)), jnp.float32),
            pltpu.SemaphoreType.DMA((2,)),
        ],
        compiler_params=pltpu.CompilerParams(vmem_limit_bytes=40 * 2**20),
        name="pool_attention",
    )(prefix_len, own_len, request_group, query, keys, turned, picked_keys, picked_values)


def body(
    hidden,
    in_gain,
    w_query,
    key_projection_weight,
    value_projection_weight,
    w_gate,
    w_out,
    q_gain,
    k_gain,
    cache_keys,
    pooled_cache_values,
    prefix_len,
    own_len,
    request_group,
    parents,
    accepted_leaf,
):
    local_req, tree = parents.shape
    requests = own_len.shape[0]
    head_width = q_gain.shape[0]
    local_heads = w_gate.shape[1]
    local_kv = key_projection_weight.shape[1] // head_width
    per_kv = local_heads // local_kv
    local_tok = hidden.shape[0]
    pool_dev = cache_keys.shape[0]
    score_scale = 1.0 / math.sqrt(head_width)
    seq_count = requests // local_req
    kv_count = in_gain.shape[0] // hidden.shape[1]
    half = np.exp(np.arange(head_width // 2) * (-2.0 * math.log(ROPE_BASE) / head_width))
    freqs = np.concatenate([half, half]).astype(np.float32)

    lines = [in_gain[None], q_gain[None], k_gain[None], jnp.asarray(freqs)[None]]
    lines += [prefix_len[None], own_len[None], request_group[None], accepted_leaf[None], parents]
    gate_top = 16
    depth = gate_top + local_heads + -local_heads % 8
    sums = {}
    top = 0
    for values in lines + [w_gate.T]:
        rows, lanes = values.shape
        low = gate_top if values.dtype == jnp.bfloat16 else top
        edges = ((low, depth - low - rows, 0), (0, in_gain.shape[0] - lanes, 0))
        padded = lax.pad(values, jnp.zeros((), values.dtype), edges)
        sums[values.dtype] = sums[values.dtype] + padded if values.dtype in sums else padded
        top += rows
    small = functools.reduce(jnp.add, [total.astype(jnp.float32) for total in sums.values()])
    gathered, picked_keys, picked_values, tree_mix, tree_lse, gate, keys, turned = layer_front(
        hidden,
        small,
        w_query,
        key_projection_weight,
        value_projection_weight,
        cache_keys.reshape(pool_dev * local_kv, head_width),
        pooled_cache_values.reshape(pool_dev * local_kv, head_width),
        seq_count,
        kv_count,
        tree,
        score_scale,
    )
    parts, part_lse, accepted_keys, accepted_values = pool_attention(
        prefix_len,
        own_len,
        request_group,
        gathered,
        keys,
        turned,
        picked_keys,
        picked_values,
        per_kv,
        score_scale,
    )
    layer_out = merge_parts(
        parts, part_lse, tree_mix, tree_lse, gate, w_out, hidden, seq_count, kv_count, per_kv
    )
    return (
        leave(layer_out),
        accepted_keys.reshape(local_req, tree, local_kv * head_width),
        accepted_values.reshape(local_req, tree, local_kv * head_width),
    )


def solution(mesh):
    in_specs = (
        P("seq", "kv"),
        P(),
        P(None, "kv"),
        P(None, "kv"),
        P(None, "kv"),
        P(None, "kv"),
        P("kv", None),
        P(),
        P(),
        P("seq", "kv", None),
        P("seq", "kv", None),
        P(),
        P(),
        P(),
        P("seq", None),
        P("seq"),
    )
    out_specs = (P("seq", "kv"), P("seq", None, "kv"), P("seq", None, "kv"))
    return jax.shard_map(body, mesh=mesh, in_specs=in_specs, out_specs=out_specs, check_vma=False)
```

```python
import functools
import math

import jax
import jax.numpy as jnp
import numpy as np
from jax import lax
from jax.experimental import pallas as pl
from jax.experimental.pallas import tpu as pltpu
from jax.sharding import PartitionSpec as P

EPSILON = 1e-06
ROPE_BASE = 1000000.0
NEGATIVE = -1e30
EARLY = 2
HALVES = 2
FRONT_VMEM = 47 * 2**20


def rms_scale(values, scales):
    mean_square = jnp.mean(values * values, axis=-1, keepdims=True)
    return values * lax.rsqrt(mean_square + EPSILON) * scales


def rope_angles(positions, freqs):
    angles = positions * freqs
    turns = jnp.floor(angles * (2.0 / math.pi) + 0.5)
    rest = angles - turns * 1.5703125
    rest = rest - turns * 4.837512969970703125e-4
    rest = rest - turns * 7.549789954891882e-8
    square = rest * rest
    sine = rest + rest * square * (
        -1.6666654611e-1 + square * (8.3321608736e-3 - square * 1.9515295891e-4)
    )
    cosine = (
        1.0
        - 0.5 * square
        + square * square * (4.166664568298827e-2 + square * (-1.388731625493765e-3 + square * 2.443315711809948e-5))
    )
    quarter = turns.astype(jnp.int32) & 3
    swapped = (quarter & 1) == 1
    cos_out = jnp.where(swapped, sine, cosine)
    sin_out = jnp.where(swapped, cosine, sine)
    cos_out = jnp.where((quarter == 1) | (quarter == 2), -cos_out, cos_out)
    sin_out = jnp.where(quarter >= 2, -sin_out, sin_out)
    return cos_out, sin_out


def tree_tables(parents, leaves, contexts, freqs):
    local_req, width = parents.shape
    tokens = local_req * width
    rows = lax.broadcasted_iota(jnp.int32, (tokens, tokens), 0)
    cols = lax.broadcasted_iota(jnp.int32, (tokens, tokens), 1)
    above = jnp.concatenate(
        [parents[at : at + 1, :] + at * width for at in range(local_req)], axis=1
    )
    reached = jnp.where((above == rows) | (rows == cols), 1.0, 0.0)
    for squaring in range(max(1, (width - 1).bit_length())):
        half = reached.astype(jnp.bfloat16)
        reached = jnp.minimum(jnp.dot(half, half, preferred_element_type=jnp.float32), 1.0)
    reach = jnp.transpose(reached)
    depth_across = jnp.sum(reached, axis=0, keepdims=True) - 1.0
    depth_down = jnp.sum(reach, axis=1, keepdims=True) - 1.0
    which = lax.broadcasted_iota(jnp.int32, (tokens, 1), 0) // width
    context = jnp.zeros((tokens, 1), jnp.float32)
    is_leaf = rows < 0
    for at in range(local_req):
        context = jnp.where(which == at, contexts[at], context)
        is_leaf = is_leaf | (rows == leaves[:, at : at + 1] + at * width)
    on_path = jnp.sum(jnp.where(is_leaf, reach, 0.0), axis=0, keepdims=True)
    level = (rows % width).astype(jnp.float32)
    picked = (depth_across == level) & (rows // width == cols // width)
    select = jnp.where(picked, jnp.broadcast_to(on_path, (tokens, tokens)), 0.0)
    cosine, sine = rope_angles(context + depth_down, freqs)
    lanes = lax.broadcasted_iota(jnp.int32, cosine.shape, 1)
    sine = jnp.where(lanes < cosine.shape[1] // 2, -sine, sine)
    return reach, select, cosine, sine


def lowest(distance):
    return distance & -distance


def flip(index, distance):
    out = index
    bit = 1
    while bit <= distance:
        if distance & bit:
            out = out + bit * (1 - 2 * ((index // bit) % 2))
        bit *= 2
    return out


def one_bits(count):
    bits = []
    bit = 1
    while bit < count:
        bits.append(bit)
        bit *= 2
    return bits


def greet(me, count, kv, kv_count):
    barrier = pltpu.get_barrier_semaphore()
    bits = one_bits(count)
    for bit in bits:
        pl.semaphore_signal(barrier, inc=1, device_id={"seq": flip(me, bit)})
    for hop in range(1, kv_count):
        pl.semaphore_signal(barrier, inc=1, device_id={"kv": (kv + hop) % kv_count})
    pl.semaphore_wait(barrier, len(bits) + kv_count - 1)


def layer_kernel(
    count,
    kv_count,
    tree,
    score_scale,
    hidden_ref,
    small_ref,
    w_query_ref,
    w_key_ref,
    w_value_ref,
    cache_key_ref,
    cache_value_ref,
    all_ref,
    picked_key_ref,
    picked_value_ref,
    tree_ref,
    tree_lse_ref,
    gate_ref,
    keys_ref,
    turned_ref,
    key_ref,
    value_ref,
    select_ref,
    wide,
    w_query,
    w_key,
    w_value,
    raw_keys,
    raw_values,
    stage,
    cos_ref,
    sin_ref,
    seen_ref,
    load_sem,
    wide_send,
    wide_recv,
    send_sem,
    recv_sem,
):
    me = lax.axis_index("seq")
    kv = lax.axis_index("kv")
    loads = [
        pltpu.make_async_copy(source, target, load_sem.at[which])
        for which, (source, target) in enumerate(
            [
                (hidden_ref, wide.at[kv]),
                (w_query_ref, w_query),
                (w_key_ref, w_key),
                (w_value_ref, w_value),
                (cache_key_ref, raw_keys),
                (cache_value_ref, raw_values),
            ]
        )
    ]
    for load in loads:
        load.start()
    greet(me, count, kv, kv_count)

    local_req = hidden_ref.shape[0] // tree

    def wide_message(hop, owner, at):
        own = slice(at * tree, (at + 1) * tree)
        return pltpu.make_async_remote_copy(
            src_ref=hidden_ref.at[own],
            dst_ref=wide.at[owner, own],
            send_sem=wide_send.at[hop, at],
            recv_sem=wide_recv.at[hop, at],
            device_id={"kv": (kv + hop) % kv_count},
        )

    wide_sent = [wide_message(hop, kv, at) for at in range(local_req) for hop in range(1, kv_count)]
    for copy in wide_sent:
        copy.start()
    lane = lax.broadcasted_iota(jnp.int32, (1, 128), 1)

    def row(at):
        return small_ref[1 + at : 2 + at, :128]

    def taken(values, index):
        return jnp.sum(jnp.where(lane == index, values, 0.0), axis=1, keepdims=True)

    contexts = [
        taken(row(3), taken(row(5), me * local_req + at).astype(jnp.int32))
        + taken(row(4), me * local_req + at)
        for at in range(local_req)
    ]
    parents = jnp.concatenate([row(7 + at)[:, :tree] for at in range(local_req)], axis=0).astype(jnp.int32)
    reach, select, cosine, sine = tree_tables(parents, row(6).astype(jnp.int32), contexts, row(2))
    seen_ref[...] = reach
    select_ref[...] = select.astype(jnp.bfloat16)
    cos_ref[...] = cosine
    sin_ref[...] = sine
    heads = w_query.shape[1] // 128

    def rotated(values, gain, part):
        values = rms_scale(values, gain)
        return (values * cos_ref[part, :] + pltpu.roll(values, 64, 1) * sin_ref[part, :]).astype(jnp.bfloat16)

    def message(distance, place, at):
        return pltpu.make_async_remote_copy(
            src_ref=all_ref.at[place],
            dst_ref=all_ref.at[place],
            send_sem=send_sem.at[distance, at],
            recv_sem=recv_sem.at[distance, at],
            device_id={"seq": flip(me, lowest(distance))},
        )

    sent = []

    def hand_on(distance, at):
        owner = flip(me, distance) * local_req + at
        if distance:
            message(distance, owner, at).wait_recv()
        bits = one_bits(lowest(distance) if distance else count)
        for bit in bits[1:] + bits[:1]:
            copy = message(distance | bit, owner, at)
            copy.start()
            sent.append(copy)

    loads[0].wait()
    normed_parts = []
    query_parts = []
    for at in range(local_req):
        own = slice(at * tree, (at + 1) * tree)
        for hop in range(1, kv_count):
            wide_message(hop, (kv + kv_count - hop) % kv_count, at).wait_recv()
        rows = jnp.concatenate([wide[owner, own] for owner in range(kv_count)], axis=1).astype(jnp.float32)
        mean_square = jnp.mean(rows * rows, axis=-1, keepdims=True)
        inverse = lax.rsqrt(mean_square + EPSILON)
        normed_parts.append((rows * inverse * small_ref[0:1, :]).astype(jnp.bfloat16))
        if not at:
            loads[1].wait()
        query = jnp.dot(normed_parts[at], w_query[...], preferred_element_type=jnp.float32)
        query_parts.append([rotated(query[:, h * 128 : (h + 1) * 128], row(0), own) for h in range(heads)])
        for head in range(heads):
            all_ref[me * local_req + at, :, head * 128 : (head + 1) * 128] = query_parts[at][head]
        hand_on(0, at)
    normed = jnp.concatenate(normed_parts, axis=0)
    queries = [jnp.concatenate([part[head] for part in query_parts], axis=0) for head in range(heads)]
    local_kv = key_ref.shape[1] // 128
    per_kv = heads // local_kv
    tokens = hidden_ref.shape[0]

    def keys_work():
        loads[2].wait()
        key = jnp.dot(normed, w_key[...], preferred_element_type=jnp.float32)
        for at in range(local_kv):
            cols = slice(at * 128, (at + 1) * 128)
            key_ref[:, cols] = rotated(key[:, cols], row(1), slice(0, tokens))

    def values_work():
        loads[3].wait()
        value_ref[...] = jnp.dot(
            normed, w_value[...], preferred_element_type=jnp.float32
        ).astype(jnp.bfloat16)
        gate_ref[...] = jax.nn.sigmoid(
            lax.dot_general(
                normed,
                small_ref[16 : 16 + heads, :].astype(jnp.bfloat16),
                (((1,), (1,)), ((), ())),
                preferred_element_type=jnp.float32,
            )
        )
        tree_lse_ref[...] = jnp.zeros(tree_lse_ref.shape, jnp.float32)

    def tree_work(at):
        cols = slice(at * 128, (at + 1) * 128)
        stacked = jnp.concatenate(queries[at * per_kv : (at + 1) * per_kv], axis=0)
        scores = (
            lax.dot_general(
                stacked,
                key_ref[:, cols],
                (((1,), (1,)), ((), ())),
                preferred_element_type=jnp.float32,
            )
            * score_scale
        )
        seen = jnp.concatenate([seen_ref[...]] * per_kv, axis=0) > 0.5
        scores = jnp.where(seen, scores, NEGATIVE)
        top = jnp.max(scores, axis=1, keepdims=True)
        weights = jnp.where(seen, jnp.exp(scores - top), 0.0)
        total = jnp.sum(weights, axis=1, keepdims=True)
        mixed = (
            jnp.dot(
                weights.astype(jnp.bfloat16), value_ref[:, cols], preferred_element_type=jnp.float32
            )
            / total
        )
        lse = top + jnp.log(total)
        for sub in range(per_kv):
            head = at * per_kv + sub
            part = slice(sub * tokens, (sub + 1) * tokens)
            tree_ref[:, head * 128 : (head + 1) * 128] = mixed[part]
            column = sub * local_kv + at
            tree_lse_ref[:, column : column + 1] = lse[part]

    pieces = 8
    slots = keys_ref.shape[0] // pieces

    def apart(source, which):
        stage[...] = source[which * slots * local_kv : (which + 1) * slots * local_kv, :].astype(jnp.float32)
        return [stage[pl.ds(at, slots, stride=local_kv), :] for at in range(local_kv)]

    def keys_apart(which):
        if which == 0:
            loads[4].wait()
        for at, part in enumerate(apart(raw_keys, which)):
            keys_ref[which * slots : (which + 1) * slots, at * 128 : (at + 1) * 128] = part.astype(jnp.bfloat16)

    def values_apart(which):
        if which == 0:
            loads[5].wait()
        for at, part in enumerate(apart(raw_values, which)):
            turned_ref[at * 128 : (at + 1) * 128, which * slots : (which + 1) * slots] = jnp.transpose(
                part
            ).astype(jnp.bfloat16)

    keys_work()
    values_work()
    def picks():
        picked = select_ref[...]
        for source, target in ((key_ref, picked_key_ref), (value_ref, picked_value_ref)):
            target[...] = jnp.dot(picked, source[...], preferred_element_type=jnp.float32).astype(jnp.bfloat16)

    work = [functools.partial(keys_apart, which) for which in range(pieces)]
    work += [functools.partial(values_apart, which) for which in range(pieces)]
    work += [functools.partial(tree_work, at) for at in range(local_kv)] + [picks]
    order = sorted(range(2, count, 2), key=lambda d: (-lowest(d), d))
    for distance in order:
        for at in range(local_req):
            hand_on(distance, at)
            if work:
                work.pop(0)()
    for rest in work:
        rest()
    for distance in range(1, count, 2):
        for at in range(local_req):
            hand_on(distance, at)
    for copy in wide_sent + sent:
        copy.wait_send()


def layer_front(
    hidden,
    small,
    w_query,
    w_key,
    w_value,
    cache_keys,
    cache_values,
    count,
    kv_count,
    tree,
    score_scale,
):
    tokens = hidden.shape[0]
    width = w_query.shape[1]
    local_kv = w_key.shape[1] // 128
    slots = cache_keys.shape[0] // local_kv
    vmem = pl.BlockSpec(memory_space=pltpu.VMEM)
    hbm = pl.BlockSpec(memory_space=pltpu.HBM)
    return pl.pallas_call(
        functools.partial(layer_kernel, count, kv_count, tree, score_scale),
        out_shape=(
            jax.ShapeDtypeStruct((count * tokens // tree, tree, width), jnp.bfloat16),
            jax.ShapeDtypeStruct((tokens, w_key.shape[1]), jnp.bfloat16),
            jax.ShapeDtypeStruct((tokens, w_value.shape[1]), jnp.bfloat16),
            jax.ShapeDtypeStruct((tokens, width), jnp.float32),
            jax.ShapeDtypeStruct((tokens, 128), jnp.float32),
            jax.ShapeDtypeStruct((tokens, width // 128), jnp.float32),
            jax.ShapeDtypeStruct((slots, local_kv * 128), jnp.bfloat16),
            jax.ShapeDtypeStruct((local_kv * 128, slots), jnp.bfloat16),
        ),
        in_specs=[vmem] * 2 + [hbm] * 5,
        out_specs=(vmem,) * 8,
        scratch_shapes=[
            pltpu.VMEM((tokens, w_key.shape[1]), jnp.bfloat16),
            pltpu.VMEM((tokens, w_value.shape[1]), jnp.bfloat16),
            pltpu.VMEM((tokens, tokens), jnp.bfloat16),
            pltpu.VMEM((kv_count,) + hidden.shape, hidden.dtype),
            pltpu.VMEM(w_query.shape, w_query.dtype),
            pltpu.VMEM(w_key.shape, w_key.dtype),
            pltpu.VMEM(w_value.shape, w_value.dtype),
            pltpu.VMEM(cache_keys.shape, jnp.bfloat16),
            pltpu.VMEM(cache_values.shape, jnp.bfloat16),
            pltpu.VMEM((cache_keys.shape[0] // 8, 128), jnp.float32),
            pltpu.VMEM((tokens, 128), jnp.float32),
            pltpu.VMEM((tokens, 128), jnp.float32),
            pltpu.VMEM((tokens, tokens), jnp.float32),
            pltpu.SemaphoreType.DMA((6,)),
            pltpu.SemaphoreType.DMA((kv_count, tokens // tree)),
            pltpu.SemaphoreType.DMA((kv_count, tokens // tree)),
            pltpu.SemaphoreType.DMA((count, tokens // tree)),
            pltpu.SemaphoreType.DMA((count, tokens // tree)),
        ],
        compiler_params=pltpu.CompilerParams(
            collective_id=0, has_side_effects=True, vmem_limit_bytes=FRONT_VMEM
        ),
        name="layer_front",
    )(
        hidden,
        small,
        w_query,
        w_key,
        w_value,
        cache_keys,
        cache_values,
    )


def leave_kernel(source_ref, target_ref, copy_sem):
    copy = pltpu.make_async_copy(source_ref, target_ref, copy_sem)
    copy.start()
    copy.wait()


def leave(result):
    return pl.pallas_call(
        leave_kernel,
        out_shape=jax.ShapeDtypeStruct(result.shape, result.dtype),
        in_specs=[pl.BlockSpec(memory_space=pltpu.VMEM)],
        out_specs=pl.BlockSpec(memory_space=pltpu.HBM),
        scratch_shapes=[pltpu.SemaphoreType.DMA],
        compiler_params=pltpu.CompilerParams(vmem_limit_bytes=4 * 2**20),
        name="leave",
    )(result)


def merge_order(count):
    begin, free = {}, {}
    for distance in range(count - 2, 0, -2):
        bit = lowest(distance)
        ready = max([begin[distance | low] + 2 for low in one_bits(bit)[1:]], default=0)
        begin[distance] = max(ready, free.get(bit, 0))
        free[bit] = begin[distance] + 1
    return sorted(begin, key=lambda distance: (begin[distance], -distance))


def merge_kernel(
    count,
    kv_count,
    per_kv,
    part_ref,
    lse_ref,
    tree_ref,
    tree_lse_ref,
    gate_ref,
    w_out_ref,
    hidden_ref,
    out_ref,
    got,
    got_lse,
    held,
    held_lse,
    w_out,
    attended,
    outgoing,
    arrived,
    send_sem,
    recv_sem,
    load_sem,
    out_send,
    out_recv,
    pair_lse,
    pair_sem,
    base_lse,
    base_mix,
    totals,
):
    me = lax.axis_index("seq")
    kv = lax.axis_index("kv")
    requests, rows, _ = part_ref.shape
    local_req = requests // count
    heads = part_ref.shape[2] // 128
    load = pltpu.make_async_copy(w_out_ref, w_out, load_sem)
    load.start()
    greet(me, count, kv, kv_count)

    def messages(distance, at):
        owner = flip(me, distance) * local_req + at
        if distance % 2:
            sources = (part_ref.at[owner],)
        else:
            sources = (held.at[distance // 2, at], held_lse.at[distance // 2, at])
        return [
            pltpu.make_async_remote_copy(
                src_ref=source,
                dst_ref=target.at[distance, at],
                send_sem=send_sem.at[which, distance, at],
                recv_sem=recv_sem.at[which, distance, at],
                device_id={"seq": flip(me, lowest(distance))},
            )
            for which, (source, target) in enumerate(zip(sources, (got, got_lse)))
        ]

    sent = []

    def send(distance, at):
        for copy in messages(distance, at):
            copy.start()
            sent.append(copy)

    def blended(levels, sources):
        top = functools.reduce(jnp.maximum, levels)
        shares = [jnp.exp(level - top) for level in levels]
        total = functools.reduce(jnp.add, shares)
        inverse = 1.0 / total
        shares = [jnp.transpose(share * inverse)[:rows] for share in shares]
        mixed = []
        for head in range(heads):
            cols = slice(head * 128, (head + 1) * 128)
            place = head % per_kv * (heads // per_kv) + head // per_kv
            mixed.append(
                functools.reduce(
                    jnp.add,
                    [
                        source(cols).astype(jnp.float32) * share[:, place : place + 1]
                        for source, share in zip(sources, shares)
                    ],
                )
            )
        return top + jnp.log(total), mixed

    def received(distance, at):
        for copy in messages(distance, at):
            copy.wait_recv()
        owner = flip(me, distance - lowest(distance)) * local_req + at
        level = pair_lse[owner] if distance % 2 else got_lse[distance, at]
        return level, lambda cols: got[distance, at, :, cols]

    def gathered(distance, at, bits):
        owner = flip(me, distance) * local_req + at
        parts = [(lse_ref[owner], lambda cols: part_ref[owner, :, cols])]
        return parts + [received(distance | bit, at) for bit in bits]

    def combined(distance, at):
        level, mixed = blended(*zip(*gathered(distance, at, one_bits(lowest(distance)))))
        held_lse[distance // 2, at] = level
        for head in range(heads):
            held[distance // 2, at, :, head * 128 : (head + 1) * 128] = mixed[head].astype(held.dtype)

    def begun(at):
        own = slice(at * rows, (at + 1) * rows)
        turned = jnp.transpose(tree_lse_ref[own, :])[:8]
        level = jnp.concatenate([turned] * (128 // rows), axis=1)
        parts = gathered(0, at, one_bits(count)[:EARLY]) + [(level, lambda cols: tree_ref[own, cols])]
        level, mixed = blended(*zip(*parts))
        base_lse[at] = level
        for head in range(heads):
            base_mix[at, :, head * 128 : (head + 1) * 128] = mixed[head] * gate_ref[own, head : head + 1]

    def ended(at):
        own = slice(at * rows, (at + 1) * rows)
        parts = [(base_lse[at], lambda cols: base_mix[at, :, cols])]
        for bit in one_bits(count)[EARLY:]:
            level, source = received(bit, at)
            parts.append((level, source))
        top = functools.reduce(jnp.maximum, [level for level, _ in parts])
        shares = [jnp.exp(level - top) for level, _ in parts]
        inverse = 1.0 / functools.reduce(jnp.add, shares)
        shares = [jnp.transpose(share * inverse)[:rows] for share in shares]
        for head in range(heads):
            cols = slice(head * 128, (head + 1) * 128)
            place = head % per_kv * (heads // per_kv) + head // per_kv
            gate = gate_ref[own, head : head + 1]
            mixed = parts[0][1](cols) * shares[0][:, place : place + 1]
            for (_, source), share in zip(parts[1:], shares[1:]):
                mixed = mixed + source(cols).astype(jnp.float32) * (share[:, place : place + 1] * gate)
            attended[own, cols] = mixed.astype(jnp.bfloat16)

    all_lse = pltpu.make_async_remote_copy(
        src_ref=lse_ref,
        dst_ref=pair_lse,
        send_sem=pair_sem.at[0],
        recv_sem=pair_sem.at[1],
        device_id={"seq": flip(me, 1)},
    )
    all_lse.start()
    for distance in merge_order(count) + [0]:
        for at in range(local_req):
            send(distance + 1, at)
    all_lse.wait()
    for distance in merge_order(count):
        for at in range(local_req):
            combined(distance, at)
            send(distance, at)
    for at in range(local_req):
        begun(at)
    width = out_ref.shape[1]
    half = width // HALVES

    def projected(target, at, which):
        cols = pl.ds(pl.multiple_of(target * width + which * half, 128), half)
        return jnp.dot(
            attended[at * rows : (at + 1) * rows, :], w_out[:, cols], preferred_element_type=jnp.float32
        )

    def out_message(hop, at, which):
        cols = slice(which * half, (which + 1) * half)
        return pltpu.make_async_remote_copy(
            src_ref=outgoing.at[hop, at, :, cols],
            dst_ref=arrived.at[hop, at, :, cols],
            send_sem=out_send.at[hop, at, which],
            recv_sem=out_recv.at[hop, at, which],
            device_id={"kv": (kv + hop) % kv_count},
        )

    load.wait()
    for at in range(local_req):
        ended(at)
        for hop in range(1, kv_count):
            for which in range(HALVES):
                outgoing[hop, at, :, which * half : (which + 1) * half] = projected(
                    (kv + hop) % kv_count, at, which
                ).astype(jnp.bfloat16)
                copy = out_message(hop, at, which)
                copy.start()
                sent.append(copy)
        own = slice(at * rows, (at + 1) * rows)
        for which in range(HALVES):
            cols = slice(which * half, (which + 1) * half)
            totals[own, cols] = projected(kv, at, which) + hidden_ref[own, cols].astype(jnp.float32)
    for at in range(local_req):
        own = slice(at * rows, (at + 1) * rows)
        for which in range(HALVES):
            cols = slice(which * half, (which + 1) * half)
            total = totals[own, cols]
            for hop in range(1, kv_count):
                out_message(hop, at, which).wait_recv()
                total = total + arrived[hop, at, :, cols].astype(jnp.float32)
            out_ref[own, cols] = total.astype(jnp.bfloat16)
    for copy in sent:
        copy.wait_send()


def merge_parts(parts, lse, tree_mix, tree_lse, gate, w_out, hidden, count, kv_count, per_kv):
    requests, rows, width = parts.shape
    local_req = requests // count
    half = max(1, count // 2)
    vmem = pl.BlockSpec(memory_space=pltpu.VMEM)
    crossing = (kv_count, local_req, rows, hidden.shape[1])
    return pl.pallas_call(
        functools.partial(merge_kernel, count, kv_count, per_kv),
        out_shape=jax.ShapeDtypeStruct(hidden.shape, jnp.bfloat16),
        in_specs=[vmem] * 5 + [pl.BlockSpec(memory_space=pltpu.HBM), vmem],
        out_specs=vmem,
        scratch_shapes=[
            pltpu.VMEM((count, local_req, rows, width), parts.dtype),
            pltpu.VMEM((count, local_req) + lse.shape[1:], jnp.float32),
            pltpu.VMEM((half, local_req, rows, width), parts.dtype),
            pltpu.VMEM((half, local_req) + lse.shape[1:], jnp.float32),
            pltpu.VMEM(w_out.shape, w_out.dtype),
            pltpu.VMEM((local_req * rows, width), jnp.bfloat16),
            pltpu.VMEM(crossing, jnp.bfloat16),
            pltpu.VMEM(crossing, jnp.bfloat16),
            pltpu.SemaphoreType.DMA((2, count, local_req)),
            pltpu.SemaphoreType.DMA((2, count, local_req)),
            pltpu.SemaphoreType.DMA,
            pltpu.SemaphoreType.DMA((kv_count, local_req, HALVES)),
            pltpu.SemaphoreType.DMA((kv_count, local_req, HALVES)),
            pltpu.VMEM(lse.shape, jnp.float32),
            pltpu.SemaphoreType.DMA((2,)),
            pltpu.VMEM((local_req,) + lse.shape[1:], jnp.float32),
            pltpu.VMEM((local_req, rows, width), jnp.float32),
            pltpu.VMEM(hidden.shape, jnp.float32),
        ],
        compiler_params=pltpu.CompilerParams(
            collective_id=1, has_side_effects=True, vmem_limit_bytes=48 * 2**20
        ),
        name="merge_parts",
    )(parts, lse, tree_mix, tree_lse, gate, w_out, hidden)


def pool_kernel(
    per_kv,
    block,
    own_block,
    score_scale,
    prefix_ref,
    own_ref,
    group_ref,
    q_ref,
    k_ref,
    vt_ref,
    picked_keys,
    picked_values,
    o_ref,
    lse_ref,
    accepted_keys_ref,
    accepted_values_ref,
    member_ref,
    shared_q,
    shared_top,
    shared_sum,
    shared_mix,
    own_q,
    own_top,
    own_sum,
    own_mix,
    score_ref,
    peak_ref,
    picked_sem,
):
    requests, tree, width = q_ref.shape
    groups = prefix_ref.shape[0]
    pool, kv_width = k_ref.shape
    local_kv = kv_width // 128
    heads = local_kv * per_kv
    per_group = requests // groups
    rows = per_kv * per_group * tree
    part = min(256, block)
    base_two = score_scale / math.log(2.0)
    base = lax.axis_index("seq") * pool
    copies = [
        pltpu.make_async_copy(picked_keys, accepted_keys_ref, picked_sem.at[0]),
        pltpu.make_async_copy(picked_values, accepted_values_ref, picked_sem.at[1]),
    ]
    for copy in copies:
        copy.start()
    o_ref[...] = jnp.zeros_like(o_ref)
    lse_ref[...] = jnp.full(lse_ref.shape, NEGATIVE, jnp.float32)

    def put_lse(owner, levels):
        wide = jnp.concatenate([levels] * (128 // tree), axis=1)
        if heads < 8:
            wide = jnp.concatenate([wide] * (8 // heads), axis=0)
        lse_ref[owner] = wide

    def bounds(start, length):
        return jnp.clip(start - base, 0, pool), jnp.clip(start + length - base, 0, pool)

    def find_members(group):
        def find(request, found):
            member_ref[found] = request
            return found + (group_ref[request] == group).astype(jnp.int32)

        lax.fori_loop(0, requests, find, 0, unroll=True)
        return [member_ref[at] for at in range(per_group)]

    def shared_part(group, first, last):
        members = find_members(group)
        for kv in range(local_kv):
            for sub in range(per_kv):
                head = kv * per_kv + sub
                for at, owner in enumerate(members):
                    place = sub * per_group + at
                    shared_q[kv, place * tree : (place + 1) * tree, :] = q_ref[
                        owner, :, head * 128 : (head + 1) * 128
                    ]
        shared_top[...] = jnp.full(shared_top.shape, NEGATIVE, jnp.float32)
        shared_sum[...] = jnp.zeros_like(shared_sum)
        shared_mix[...] = jnp.zeros_like(shared_mix)
        first_step = first // block
        final_step = (last + block - 1) // block - 1

        def scored(start, kv, piece):
            low = pl.multiple_of(start + piece * part, part)
            slots = low + lax.broadcasted_iota(jnp.int32, (part, 128), 0)
            bias = jnp.where((slots >= first) & (slots < last), 0.0, NEGATIVE)
            bias = jnp.concatenate([bias] * (rows // 128), axis=1)
            raw = (
                lax.dot_general(
                    k_ref[pl.ds(low, part), kv * 128 : (kv + 1) * 128],
                    shared_q[kv],
                    (((1,), (1,)), ((), ())),
                    preferred_element_type=jnp.float32,
                )
                + bias
            )
            score_ref[kv % 2, piece * part : (piece + 1) * part, :rows] = raw
            return jnp.max(raw, axis=0, keepdims=True)

        peaks = [scored(first_step * block, 0, piece) for piece in range(block // part)]
        peak_ref[0:1, :rows] = functools.reduce(jnp.maximum, peaks)

        def visit(step, unused):
            start = step * block
            later = jnp.minimum(step + 1, final_step) * block
            for kv in range(local_kv):
                next_kv = (kv + 1) % local_kv
                next_start = later if next_kv == 0 else start
                slot = kv % 2
                old_top = shared_top[kv : kv + 1, :]
                top = jnp.maximum(old_top, peak_ref[slot : slot + 1, :rows])
                factor = jnp.exp2((old_top - top) * base_two)
                shared_top[kv : kv + 1, :] = top
                total = shared_sum[kv : kv + 1, :] * factor
                mixed = shared_mix[kv] * factor
                peaks = []
                for piece in range(block // part):
                    peaks.append(scored(next_start, next_kv, piece))
                    weights = jnp.exp2(
                        (score_ref[slot, piece * part : (piece + 1) * part, :rows] - top) * base_two
                    )
                    total = total + jnp.sum(weights, axis=0, keepdims=True)
                    low = pl.multiple_of(start + piece * part, part)
                    mixed = mixed + jnp.dot(
                        vt_ref[kv * 128 : (kv + 1) * 128, pl.ds(low, part)],
                        weights.astype(jnp.bfloat16),
                        preferred_element_type=jnp.float32,
                    )
                peak_ref[1 - slot : 2 - slot, :rows] = functools.reduce(jnp.maximum, peaks)
                shared_sum[kv : kv + 1, :] = total
                shared_mix[kv] = mixed
            return unused

        lax.fori_loop(first_step, final_step + 1, visit, 0)
        levels = shared_top[...] * score_scale + jnp.log(shared_sum[...])
        for kv in range(local_kv):
            mixed = jnp.transpose(shared_mix[kv] / shared_sum[kv : kv + 1, :]).astype(o_ref.dtype)
            for sub in range(per_kv):
                head = kv * per_kv + sub
                for at, owner in enumerate(members):
                    place = sub * per_group + at
                    o_ref[owner, :, head * 128 : (head + 1) * 128] = mixed[place * tree : (place + 1) * tree]
        for at, owner in enumerate(members):
            put_lse(
                owner,
                jnp.concatenate(
                    [
                        levels[:, (sub * per_group + at) * tree : (sub * per_group + at + 1) * tree]
                        for sub in range(per_kv)
                    ],
                    axis=0,
                ),
            )

    lanes = heads * tree
    blocks = pool // own_block

    def own_parts(start):
        own_q[...] = jnp.zeros_like(own_q)

        def seek(request, found):
            owner, begin = found
            passed = (owner == request) & (begin + own_ref[request] <= base)
            return (
                owner + passed.astype(jnp.int32),
                begin + jnp.where(passed, own_ref[request], 0),
            )

        owner, begin = lax.fori_loop(0, requests - 1, seek, (0, start), unroll=True)

        def stop_of(owner, begin):
            return begin + own_ref[owner] - base

        def scored(step, slot, owner, stop):
            other = jnp.minimum(owner + 1, requests - 1)
            for which, request in enumerate((owner, other)):
                for head in range(heads):
                    cols = slice(head // per_kv * 128, (head // per_kv + 1) * 128)
                    low = which * lanes + head * tree
                    own_q[slot, low : low + tree, cols] = q_ref[request, :, head * 128 : (head + 1) * 128]
            low = pl.multiple_of(step * own_block, own_block)
            slots = low + lax.broadcasted_iota(jnp.int32, (own_block, 128), 0)
            before = jnp.where(slots < stop, 0.0, NEGATIVE)
            after = jnp.where(slots < stop, NEGATIVE, 0.0)
            bias = jnp.concatenate([before] * (lanes // 128) + [after] * (lanes // 128), axis=1)
            raw = (
                lax.dot_general(
                    k_ref[pl.ds(low, own_block), :],
                    own_q[slot],
                    (((1,), (1,)), ((), ())),
                    preferred_element_type=jnp.float32,
                )
                + bias
            )
            score_ref[slot, :own_block, : 2 * lanes] = raw
            peak_ref[pl.ds(slot, 1), : 2 * lanes] = jnp.max(raw, axis=0, keepdims=True)

        def finish(owner):
            levels = own_top[...] * score_scale + jnp.log(own_sum[...])
            mixed = jnp.transpose(own_mix[...] / own_sum[...]).astype(o_ref.dtype)
            for head in range(heads):
                o_ref[owner, :, head * 128 : (head + 1) * 128] = mixed[head * tree : (head + 1) * tree]
            put_lse(
                owner,
                jnp.concatenate(
                    [
                        levels[:, (kv * per_kv + sub) * tree : (kv * per_kv + sub + 1) * tree]
                        for sub in range(per_kv)
                        for kv in range(local_kv)
                    ],
                    axis=0,
                ),
            )

        scored(0, 0, owner, stop_of(owner, begin))
        own_top[...] = jnp.full(own_top.shape, NEGATIVE, jnp.float32)
        own_sum[...] = jnp.zeros_like(own_sum)
        own_mix[...] = jnp.zeros_like(own_mix)

        def visit(step, at):
            owner, begin = at
            slot = step % 2
            ended = stop_of(owner, begin) <= (step + 1) * own_block
            next_owner = jnp.where(ended, jnp.minimum(owner + 1, requests - 1), owner)
            next_begin = jnp.where(ended, begin + own_ref[owner], begin)
            scored(jnp.minimum(step + 1, blocks - 1), 1 - slot, next_owner, stop_of(next_owner, next_begin))
            peak = peak_ref[pl.ds(slot, 1), : 2 * lanes]
            old_top = own_top[...]
            mine = jnp.maximum(old_top, peak[:, :lanes])
            top = jnp.concatenate([mine, peak[:, lanes:]], axis=1)
            factor = jnp.exp2((old_top - mine) * base_two)
            weights = jnp.exp2((score_ref[slot, :own_block, : 2 * lanes] - top) * base_two)
            total = jnp.sum(weights, axis=0, keepdims=True)
            low = pl.multiple_of(step * own_block, own_block)
            whole = jnp.dot(
                vt_ref[:, pl.ds(low, own_block)],
                weights.astype(jnp.bfloat16),
                preferred_element_type=jnp.float32,
            )
            which = lax.broadcasted_iota(jnp.int32, (128, 2 * lanes), 1) // (per_kv * tree) % local_kv
            mixed = whole[:128]
            for kv in range(1, local_kv):
                mixed = jnp.where(which == kv, whole[kv * 128 : (kv + 1) * 128], mixed)
            own_top[...] = mine
            own_sum[...] = own_sum[...] * factor + total[:, :lanes]
            own_mix[...] = own_mix[...] * factor + mixed[:, :lanes]

            @pl.when(ended)
            def _():
                finish(owner)
                own_top[...] = peak[:, lanes:]
                own_sum[...] = total[:, lanes:]
                own_mix[...] = mixed[:, lanes:]

            return next_owner, next_begin

        owner, begin = lax.fori_loop(0, blocks, visit, (owner, begin))

        @pl.when(begin < base + pool)
        def _():
            finish(owner)

    def group_step(group, start):
        first, last = bounds(start, prefix_ref[group])

        @pl.when(last > first)
        def _():
            shared_part(group, first, last)

        return start + prefix_ref[group]

    own_start = lax.fori_loop(0, groups, group_step, 0)

    @pl.when(base + pool > own_start)
    def _():
        own_parts(own_start)

    for copy in copies:
        copy.wait()


def pool_attention(
    prefix_len, own_len, request_group, query, keys, turned, picked_keys, picked_values, per_kv, score_scale
):
    requests, tree, width = query.shape
    pool, kv_width = keys.shape
    local_kv = kv_width // 128
    heads = local_kv * per_kv
    rows = per_kv * (requests // prefix_len.shape[0]) * tree
    lanes = heads * tree
    vmem = pl.BlockSpec(memory_space=pltpu.VMEM)
    smem = pl.BlockSpec(memory_space=pltpu.SMEM)
    hbm = pl.BlockSpec(memory_space=pltpu.HBM)
    return pl.pallas_call(
        functools.partial(pool_kernel, per_kv, min(512, pool), min(256, pool), score_scale),
        out_shape=(
            jax.ShapeDtypeStruct(query.shape, jnp.bfloat16),
            jax.ShapeDtypeStruct((requests, 8, 128), jnp.float32),
            jax.ShapeDtypeStruct(picked_keys.shape, jnp.bfloat16),
            jax.ShapeDtypeStruct(picked_values.shape, jnp.bfloat16),
        ),
        in_specs=[smem] * 3 + [vmem] * 5,
        out_specs=(vmem, vmem, hbm, hbm),
        scratch_shapes=[
            pltpu.SMEM((requests + 1,), jnp.int32),
            pltpu.VMEM((local_kv, rows, 128), jnp.bfloat16),
            pltpu.VMEM((local_kv, rows), jnp.float32),
            pltpu.VMEM((local_kv, rows), jnp.float32),
            pltpu.VMEM((local_kv, 128, rows), jnp.float32),
            pltpu.VMEM((2, 2 * lanes, kv_width), jnp.bfloat16),
            pltpu.VMEM((1, lanes), jnp.float32),
            pltpu.VMEM((1, lanes), jnp.float32),
            pltpu.VMEM((128, lanes), jnp.float32),
            pltpu.VMEM((2, 512, max(rows, 2 * lanes)), jnp.float32),
            pltpu.VMEM((2, max(rows, 2 * lanes)), jnp.float32),
            pltpu.SemaphoreType.DMA((2,)),
        ],
        compiler_params=pltpu.CompilerParams(vmem_limit_bytes=40 * 2**20),
        name="pool_attention",
    )(prefix_len, own_len, request_group, query, keys, turned, picked_keys, picked_values)


def body(
    hidden,
    in_gain,
    w_query,
    key_projection_weight,
    value_projection_weight,
    w_gate,
    w_out,
    q_gain,
    k_gain,
    cache_keys,
    pooled_cache_values,
    prefix_len,
    own_len,
    request_group,
    parents,
    accepted_leaf,
):
    local_req, tree = parents.shape
    requests = own_len.shape[0]
    head_width = q_gain.shape[0]
    local_heads = w_gate.shape[1]
    local_kv = key_projection_weight.shape[1] // head_width
    per_kv = local_heads // local_kv
    local_tok = hidden.shape[0]
    pool_dev = cache_keys.shape[0]
    score_scale = 1.0 / math.sqrt(head_width)
    seq_count = requests // local_req
    kv_count = in_gain.shape[0] // hidden.shape[1]
    half = np.exp(np.arange(head_width // 2) * (-2.0 * math.log(ROPE_BASE) / head_width))
    freqs = np.concatenate([half, half]).astype(np.float32)

    lines = [in_gain[None], q_gain[None], k_gain[None], jnp.asarray(freqs)[None]]
    lines += [prefix_len[None], own_len[None], request_group[None], accepted_leaf[None], parents]
    gate_top = 16
    depth = gate_top + local_heads + -local_heads % 8
    sums = {}
    top = 0
    for values in lines + [w_gate.T]:
        rows, lanes = values.shape
        low = gate_top if values.dtype == jnp.bfloat16 else top
        edges = ((low, depth - low - rows, 0), (0, in_gain.shape[0] - lanes, 0))
        padded = lax.pad(values, jnp.zeros((), values.dtype), edges)
        sums[values.dtype] = sums[values.dtype] + padded if values.dtype in sums else padded
        top += rows
    small = functools.reduce(jnp.add, [total.astype(jnp.float32) for total in sums.values()])
    gathered, picked_keys, picked_values, tree_mix, tree_lse, gate, keys, turned = layer_front(
        hidden,
        small,
        w_query,
        key_projection_weight,
        value_projection_weight,
        cache_keys.reshape(pool_dev * local_kv, head_width),
        pooled_cache_values.reshape(pool_dev * local_kv, head_width),
        seq_count,
        kv_count,
        tree,
        score_scale,
    )
    parts, part_lse, accepted_keys, accepted_values = pool_attention(
        prefix_len,
        own_len,
        request_group,
        gathered,
        keys,
        turned,
        picked_keys,
        picked_values,
        per_kv,
        score_scale,
    )
    layer_out = merge_parts(
        parts, part_lse, tree_mix, tree_lse, gate, w_out, hidden, seq_count, kv_count, per_kv
    )
    return (
        leave(layer_out),
        accepted_keys.reshape(local_req, tree, local_kv * head_width),
        accepted_values.reshape(local_req, tree, local_kv * head_width),
    )


def solution(mesh):
    in_specs = (
        P("seq", "kv"),
        P(),
        P(None, "kv"),
        P(None, "kv"),
        P(None, "kv"),
        P(None, "kv"),
        P("kv", None),
        P(),
        P(),
        P("seq", "kv", None),
        P("seq", "kv", None),
        P(),
        P(),
        P(),
        P("seq", None),
        P("seq"),
    )
    out_specs = (P("seq", "kv"), P("seq", None, "kv"), P("seq", None, "kv"))
    return jax.shard_map(body, mesh=mesh, in_specs=in_specs, out_specs=out_specs, check_vma=False)
```
